32 devices in a mesh: dp: 8 (over y, x, core), grp: 4 (over z).
Axes of the slice: x: 2, y: 2, z: 4, core: 2. Of those that a mesh axis runs over, the one named last changes fastest.
Arguments:
- acts: bfloat16 [192, 32, 2048], P(('dp', 'grp')), may hold values from -6 to 6
- cotan: bfloat16 [192, 32, 1024], P(('dp', 'grp')), may hold values from -0.029907227 to 0.029907227
- lengths: int32 [192], P(('dp', 'grp')), may hold values from 0 to 32, as said below
- offsets: int32 [192], P(('dp', 'grp')), may hold values from 0 to 31, as said below
- kernel: float32 [32, 1024], replicated, may hold values from -1 to 1
- gamma: float32 [1024], replicated, may hold values from 0.1 to 1.9
- beta: float32 [1024], replicated, may hold values from -3 to 3
- w_out: bfloat16 [1024, 1024], replicated, may hold values from -0.1875 to 0.1875
Outputs:
- module_out: bfloat16 [192, 32, 1024], P(('dp', 'grp'))
- grad_w_out: float32 [1024, 1024], P('dp')
- grad_kernel: float32 [32, 1024], P(None, 'dp')
- grad_gamma: float32 [1024], replicated
- grad_beta: float32 [1024], replicated
The draws below stay inside these ranges and needn't reach their ends.
Inputs may be any that keep to these rules, and one draw needn't show every extreme that they name: `lengths`: each device holds 6 slots; its used slots come first and the others have length 0. A device holds 2 to 6 utterances; the devices with dp indices i and i + 8/2 and the same grp index hold 8 together, and in every draw some such pair holds 6 and 2. Some slot has 32 frames. The utterance of a slot fills frames offsets to offsets + lengths - 1 of that slot.
All inputs are finite; a program needn't handle non-finite values.
Results may differ from the reference program's by a relative error of at most 0.005.
Values may be sent and summed in bfloat16 or wider, within the bound.
No kernel may reach another device: no remote copies, remote signals or barrier semaphores. Data moves between devices by JAX's collectives and lax.ppermute only.
A program may use at most 64 MiB of HBM per device.

```python
import jax
import jax.numpy as jnp
from jax import lax

D = 1024
WIDE = 2048
KW = 32
SLOT = 32
UTT_MEAN = 4
SLOTS = 6
UTTS = 192
N_DP = 8
N_GRP = 4


def pair_layout(key):
    devices = N_DP * N_GRP
    half = N_DP // 2
    keys = jax.random.split(jax.random.fold_in(key, 7), 4)
    excess = jax.random.randint(keys[0], (half, N_GRP), 0, 3)
    excess = excess.at[0, 0].set(2)
    side = jax.random.randint(keys[1], (half, N_GRP), 0, 2) * 2 - 1
    lower = UTT_MEAN + side * excess
    upper = UTT_MEAN - side * excess
    counts = jnp.concatenate([lower, upper], axis=0).reshape(devices)
    slot_index = jnp.arange(SLOTS, dtype=jnp.int32)
    used = slot_index[None, :] < counts[:, None]
    device_index = jnp.arange(devices, dtype=jnp.int32)
    floor_len = SLOT // 2 + (SLOT - SLOT // 2) * device_index // max(devices - 1, 1)
    sizes_drawn = jax.random.randint(keys[2], (devices, SLOTS), floor_len[:, None], SLOT + 1)
    sizes_drawn = sizes_drawn.at[devices - 1, 0].set(SLOT)
    sizes_drawn = jnp.where(used, sizes_drawn, 0).astype(jnp.int32)
    starts = jax.random.randint(keys[3], (devices, SLOTS), 0, SLOT - sizes_drawn + 1).astype(jnp.int32)
    starts = jnp.minimum(starts, SLOT - 1)
    return (sizes_drawn.reshape(-1), starts.reshape(-1))


def draw_lengths(key, part):
    return pair_layout(key)[0]


def draw_offsets(key, part):
    return pair_layout(key)[1]


def shard_levels(key, shape, cuts, least, top_value):
    level, own = 1.0, jax.random.fold_in(key, 6)
    for axis_at, parts in cuts:
        draws = jnp.exp(jax.random.uniform(jax.random.fold_in(own, axis_at), (parts,), jnp.float32, least / len(cuts), top_value / len(cuts)))
        level = level * jnp.repeat(draws, shape[axis_at] // parts).reshape([-1 if axis == axis_at else 1 for axis in range(len(shape))])
    return level


def centred(stream_key, extent, spread, reach, shards=(), kind=jnp.bfloat16):
    factor_of = shard_levels(stream_key, extent, shards, -0.22, 0.18) if shards else 1.0
    result = jax.random.normal(stream_key, extent, jnp.float32) * spread * factor_of
    return jnp.minimum(jnp.maximum(result, -reach), reach).astype(kind)


def setup_inputs(seed: int = 0) -> dict:
    splits = jax.random.split(jax.random.key(seed), 9)
    acts = centred(splits[0], (UTTS, SLOT, WIDE), 1.0, 6.0, ((0, 32),))
    cotan = centred(splits[1], (UTTS, SLOT, D), 0.005, 0.029907227, ((0, 32),))
    lengths = draw_lengths(jax.random.fold_in(splits[8], 71), 0)
    offsets = draw_offsets(jax.random.fold_in(splits[8], 71), 0)
    kernel = centred(splits[4], (KW, D), KW ** -0.5, 1.0, (), jnp.float32)
    gamma = jnp.clip(1.0 + 0.18 * jax.random.normal(splits[5], (D,), jnp.float32), 0.1, 1.9)
    beta = centred(splits[6], (D,), 0.5, 3.0, (), jnp.float32)
    w_out = centred(splits[7], (D, D), D ** -0.5, 0.1875)
    return dict(acts=acts, cotan=cotan, lengths=lengths, offsets=offsets, kernel=kernel, gamma=gamma, beta=beta, w_out=w_out)


def convolve(block_acts, block_len, block_off, kernel):
    taps = kernel.shape[0]
    model_width = kernel.shape[1]
    frame_count = block_acts.shape[1]
    position = jnp.arange(frame_count, dtype=jnp.int32)
    valid = ((position[None, :] >= block_off[:, None]) & (position[None, :] < (block_off + block_len)[:, None])).astype(jnp.float32)
    wide_acts = block_acts.astype(jnp.float32)
    gated = wide_acts[..., :model_width] * jax.nn.sigmoid(wide_acts[..., model_width:]) * valid[..., None]
    padded = jnp.pad(gated, ((0, 0), (taps // 2 - 1, taps // 2), (0, 0)))
    conv_out = padded[:, 0:frame_count] * kernel[0]
    for tap in range(1, taps):
        conv_out = conv_out + padded[:, tap:tap + frame_count] * kernel[tap]
    return (valid, padded, conv_out)

def reference(acts, cotan, lengths, offsets, kernel, gamma, beta, w_out):
    blocks = N_DP * N_GRP
    block_acts = acts.reshape(blocks, SLOTS, SLOT, 2 * D)
    block_cotan = cotan.reshape(blocks, SLOTS, SLOT, D)
    block_len = lengths.reshape(blocks, SLOTS)
    block_off = offsets.reshape(blocks, SLOTS)

    def stats_step(carry, item):
        part_acts, part_len, part_off = item
        valid, padded, conv_out = convolve(part_acts, part_len, part_off, kernel)
        masked = conv_out * valid[..., None]
        return ((carry[0] + lax.optimization_barrier(jnp.sum(masked, axis=(0, 1))), carry[1] + lax.optimization_barrier(jnp.sum(masked * conv_out, axis=(0, 1))), carry[2] + jnp.sum(part_len).astype(jnp.float32)), None)
    zeros_row = jnp.zeros((D,), jnp.float32)
    (sum_first, sum_second, frame_total), unused = lax.scan(stats_step, (zeros_row, zeros_row, jnp.zeros((), jnp.float32)), (block_acts, block_len, block_off))
    mean_value = sum_first / frame_total
    inv_std = lax.rsqrt(sum_second / frame_total - mean_value * mean_value + 1e-05)

    def forward_back(part_acts, part_cotan, part_len, part_off):
        valid, padded, conv_out = convolve(part_acts, part_len, part_off, kernel)
        normed = (conv_out - mean_value) * inv_std
        shifted = gamma * normed + beta
        sig_value = jax.nn.sigmoid(shifted)
        hidden = (shifted * sig_value * valid[..., None]).astype(jnp.bfloat16)
        flat_hidden = hidden.reshape(-1, D)
        flat_cotan = part_cotan.reshape(-1, D)
        back_hidden = lax.dot_general(flat_cotan, w_out, (((1,), (1,)), ((), ())), preferred_element_type=jnp.float32).reshape(conv_out.shape)
        slope = back_hidden * sig_value * (1.0 + shifted * (1.0 - sig_value)) * valid[..., None]
        return (valid, padded, normed, flat_hidden, flat_cotan, slope)

    def main_step(carry, item):
        part_acts, part_cotan, part_len, part_off = item
        valid, padded, normed, flat_hidden, flat_cotan, slope = forward_back(part_acts, part_cotan, part_len, part_off)
        outputs = jnp.dot(flat_hidden, w_out, preferred_element_type=jnp.float32).astype(jnp.bfloat16)
        weight_term = lax.dot_general(flat_hidden, flat_cotan, (((0,), (0,)), ((), ())), preferred_element_type=jnp.float32)
        return ((carry[0] + weight_term, carry[1] + lax.optimization_barrier(jnp.sum(slope, axis=(0, 1))), carry[2] + lax.optimization_barrier(jnp.sum(slope * normed, axis=(0, 1)))), outputs.reshape(SLOTS, SLOT, D))
    (grad_w_out, beta_sum, gamma_sum), module_out = lax.scan(main_step, (jnp.zeros((D, D), jnp.float32), zeros_row, zeros_row), (block_acts, block_cotan, block_len, block_off))

    def kernel_step(carry, item):
        part_acts, part_cotan, part_len, part_off = item
        valid, padded, normed, flat_hidden, flat_cotan, slope = forward_back(part_acts, part_cotan, part_len, part_off)
        conv_grad = gamma * inv_std * (slope - beta_sum / frame_total - normed * gamma_sum / frame_total) * valid[..., None]
        term = jnp.stack([lax.optimization_barrier(jnp.sum(conv_grad * padded[:, tap:tap + SLOT], axis=(0, 1))) for tap in range(KW)], axis=0)
        return (carry + term, None)
    grad_kernel, unused = lax.scan(kernel_step, jnp.zeros((KW, D), jnp.float32), (block_acts, block_cotan, block_len, block_off))
    return (module_out.reshape(UTTS, SLOT, D), grad_w_out, grad_kernel, gamma_sum, beta_sum)
```

```python
import functools

import jax
import jax.numpy as jnp
from jax import lax
from jax.experimental import pallas as pl
from jax.experimental.pallas import tpu as pltpu
from jax.sharding import PartitionSpec as P


LANES = 128
F32 = jnp.float32
BF16 = jnp.bfloat16


def convolve(block_acts, block_len, block_off, kernel):
    taps = kernel.shape[0]
    model_width = kernel.shape[1]
    frame_count = block_acts.shape[1]
    position = jnp.arange(frame_count, dtype=jnp.int32)
    valid = (
        (position[None, :] >= block_off[:, None])
        & (position[None, :] < (block_off + block_len)[:, None])
    ).astype(jnp.float32)
    wide_acts = block_acts.astype(jnp.float32)
    gated = (
        wide_acts[..., :model_width]
        * jax.nn.sigmoid(wide_acts[..., model_width:])
        * valid[..., None]
    )
    padded = jnp.pad(gated, ((0, 0), (taps // 2 - 1, taps // 2), (0, 0)))
    conv_out = padded[:, 0:frame_count] * kernel[0]
    for tap in range(1, taps):
        conv_out = conv_out + padded[:, tap : tap + frame_count] * kernel[tap]
    return (valid, padded, conv_out)


def local_general(acts, cotan, lengths, offsets, kernel, gamma, beta, w_out):
    model_width = w_out.shape[0]
    taps = kernel.shape[0]
    valid, padded, conv_out = convolve(acts, lengths, offsets, kernel)
    masked = conv_out * valid[..., None]
    sum_first, sum_second, frame_total = lax.psum(
        (
            jnp.sum(masked, axis=(0, 1)),
            jnp.sum(masked * conv_out, axis=(0, 1)),
            jnp.sum(lengths).astype(jnp.float32),
        ),
        ("dp", "grp"),
    )
    mean_value = sum_first / frame_total
    inv_std = lax.rsqrt(sum_second / frame_total - mean_value * mean_value + 1e-05)
    normed = (conv_out - mean_value) * inv_std
    shifted = gamma * normed + beta
    sig_value = jax.nn.sigmoid(shifted)
    hidden = (shifted * sig_value * valid[..., None]).astype(jnp.bfloat16)
    flat_hidden = hidden.reshape(-1, model_width)
    flat_cotan = cotan.reshape(-1, model_width)
    outputs = (
        jnp.dot(flat_hidden, w_out, preferred_element_type=jnp.float32)
        .astype(jnp.bfloat16)
        .reshape(cotan.shape)
    )
    weight_rows = lax.psum_scatter(
        lax.dot_general(
            flat_hidden, flat_cotan, (((0,), (0,)), ((), ())), preferred_element_type=jnp.float32
        ),
        "dp",
        scatter_dimension=0,
        tiled=True,
    )
    back_hidden = lax.dot_general(
        flat_cotan, w_out, (((1,), (1,)), ((), ())), preferred_element_type=jnp.float32
    ).reshape(conv_out.shape)
    slope = back_hidden * sig_value * (1.0 + shifted * (1.0 - sig_value)) * valid[..., None]
    beta_sum, gamma_sum = lax.psum(
        (jnp.sum(slope, axis=(0, 1)), jnp.sum(slope * normed, axis=(0, 1))), ("dp", "grp")
    )
    conv_grad = (
        gamma
        * inv_std
        * (slope - beta_sum / frame_total - normed * gamma_sum / frame_total)
        * valid[..., None]
    )
    frame_count = conv_out.shape[1]
    kernel_term = jnp.stack(
        [
            jnp.sum(conv_grad * padded[:, tap : tap + frame_count], axis=(0, 1))
            for tap in range(taps)
        ],
        axis=0,
    )
    kernel_rows = lax.psum_scatter(kernel_term.T, "dp", scatter_dimension=0, tiled=True)
    weight_rows, kernel_rows = lax.psum((weight_rows, kernel_rows), "grp")
    return (outputs, weight_rows, kernel_rows.T, gamma_sum, beta_sum)


def mask_of(length, offset, frames):
    position = lax.broadcasted_iota(jnp.int32, (frames, LANES), 0)
    return ((position >= offset) & (position < offset + length)).astype(F32)


def fold(value):
    total = value[0:8]
    for at in range(8, value.shape[0], 8):
        total = total + value[at : at + 8]
    return total


def conv_body(len_ref, off_ref, a_ref, b_ref, k_ref, gp_ref, cv_ref, st_ref):
    slots, frames, _ = a_ref.shape
    taps = k_ref.shape[0]
    lead = taps // 2
    rows = gp_ref.shape[1]
    step = pl.program_id(0)

    def one(slot, carry):
        first, second = carry
        valid = mask_of(len_ref[slot], off_ref[slot], frames)
        gated = a_ref[slot].astype(F32) * jax.nn.sigmoid(b_ref[slot].astype(F32)) * valid
        gp_ref[slot, 0:lead, :] = jnp.zeros((lead, LANES), F32)
        gp_ref[slot, lead : lead + frames, :] = gated
        gp_ref[slot, lead + frames : rows, :] = jnp.zeros((rows - lead - frames, LANES), F32)
        total = gp_ref[slot, 1 : 1 + frames, :] * k_ref[0:1, :]
        for tap in range(1, taps):
            total = total + gp_ref[slot, 1 + tap : 1 + tap + frames, :] * k_ref[tap : tap + 1, :]
        cv_ref[slot] = total
        masked = total * valid
        return first + fold(masked), second + fold(masked * total)

    zero = jnp.zeros((8, LANES), F32)
    first, second = lax.fori_loop(0, slots, one, (zero, zero))
    at = pl.ds(pl.multiple_of(step * LANES, LANES), LANES)
    st_ref[0:1, at] = jnp.sum(first, axis=0, keepdims=True)
    st_ref[1:2, at] = jnp.sum(second, axis=0, keepdims=True)

    @pl.when(step == 0)
    def _():
        count = len_ref[0]
        for slot in range(1, slots):
            count = count + len_ref[slot]
        width = pl.num_programs(0) * LANES
        st_ref[:, st_ref.shape[1] - LANES :] = jnp.full((2, LANES), count.astype(F32), F32)


def lag_sums(gp_ref, weights, taps, frames, slots, group):
    found = []
    for low in range(0, taps, group):
        many = len(weights(0, probe=True))

        def one(slot, carry, low=low):
            items = weights(slot)
            out = list(carry)
            for j in range(group):
                shifted = gp_ref[slot, 1 + low + j : 1 + low + j + frames, :]
                for i, item in enumerate(items):
                    out[i * group + j] = out[i * group + j] + fold(item * shifted)
            return tuple(out)

        zero = jnp.zeros((8, LANES), F32)
        sums = lax.fori_loop(0, slots, one, (zero,) * (many * group))
        found.append(sums)
    rows = []
    for i in range(len(found[0]) // group):
        for sums in found:
            for j in range(group):
                rows.append(jnp.sum(sums[i * group + j], axis=0, keepdims=True))
    return rows


def aux_body(len_ref, off_ref, gp_ref, cv_ref, s2_ref, t3_ref):
    slots, frames, _ = cv_ref.shape
    taps = s2_ref.shape[0]

    def weights(slot, probe=False):
        if probe:
            return (0, 0)
        valid = mask_of(len_ref[slot], off_ref[slot], frames)
        return (valid, cv_ref[slot] * valid)

    rows = lag_sums(gp_ref, weights, taps, frames, slots, 8)
    for k in range(taps):
        s2_ref[k : k + 1, :] = rows[k]
        t3_ref[k : k + 1, :] = rows[taps + k]


def act_body(len_ref, off_ref, st_ref, cnt_ref, g_ref, b_ref, gp_ref, cv_ref, bk_ref, s2_ref, t3_ref,
             pay_ref, hid_ref, q_ref, sl_ref):
    slots, frames, _ = cv_ref.shape
    taps = s2_ref.shape[0]
    tokens = slots * frames
    count = cnt_ref[0:1, :]
    mean = st_ref[0:1, :] / count
    inv = lax.rsqrt(st_ref[1:2, :] / count - mean * mean + 1e-05)
    gain, shift = g_ref[...], b_ref[...]

    def one(slot, carry):
        first, second = carry
        valid = mask_of(len_ref[slot], off_ref[slot], frames)
        normed = (cv_ref[slot] - mean) * inv
        shifted = gain * normed + shift
        sig = jax.nn.sigmoid(shifted)
        hidden = (shifted * sig * valid).astype(BF16)
        at = pl.ds(pl.multiple_of(slot * frames, frames), frames)
        pay_ref[0, at, :] = hidden
        hid_ref[at, :] = hidden
        slope = bk_ref[at, :] * sig * (1.0 + shifted * (1.0 - sig)) * valid
        sl_ref[slot] = slope
        return first + fold(slope), second + fold(slope * normed)

    zero = jnp.zeros((8, LANES), F32)
    first, second = lax.fori_loop(0, slots, one, (zero, zero))

    def weights(slot, probe=False):
        return (0,) if probe else (sl_ref[slot],)

    rows = lag_sums(gp_ref, weights, taps, frames, slots, 16)
    for k in range(taps):
        q_ref[k : k + 1, :] = rows[k]
    s2 = s2_ref[...]
    q_ref[taps : 2 * taps, :] = s2
    q_ref[2 * taps : 3 * taps, :] = inv * (t3_ref[...] - mean * s2)
    extra = q_ref.shape[0]
    q_ref[3 * taps :, :] = jnp.zeros((extra - 3 * taps, LANES), F32)
    q_ref[3 * taps : 3 * taps + 1, :] = jnp.sum(first, axis=0, keepdims=True)
    q_ref[3 * taps + 1 : 3 * taps + 2, :] = jnp.sum(second, axis=0, keepdims=True)
    put_pair(pay_ref.at[0], tokens, q_ref[...])


def put_pair(ref, at, value):
    rows = value.shape[0]
    lead = value.astype(BF16)
    ref[at : at + rows, :] = lead
    ref[at + rows : at + 2 * rows, :] = (value - lead.astype(F32)).astype(BF16)


def get_pair(ref, at, rows):
    return ref[at : at + rows, :].astype(F32) + ref[at + rows : at + 2 * rows, :].astype(F32)


def rows_body(masks, tokens, n_q, at_ref, recv_ref, *refs):
    pieces, out_ref = refs[:-1], refs[-1]
    me, half = at_ref[0], at_ref[1]
    width = pieces[0].shape[1] // 2
    cols = pl.ds(pl.multiple_of(half * width, width), width)
    total = None
    for (mask, low), piece in zip(masks, pieces):
        source = jnp.bitwise_xor(me, mask)
        left = recv_ref[source, low : low + piece.shape[0], :]
        term = lax.dot_general(
            left, piece[:, cols], (((0,), (0,)), ((), ())), preferred_element_type=F32
        )
        total = term if total is None else total + term
    for block in range(width // LANES):
        out_ref[block * LANES : (block + 1) * LANES, :] = total[
            :, block * LANES : (block + 1) * LANES
        ].astype(BF16)
    if n_q:
        value = get_pair(recv_ref.at[0], tokens, n_q)
        for source in range(1, recv_ref.shape[0]):
            value = value + get_pair(recv_ref.at[source], tokens, n_q)
        put_pair(out_ref, width, value)


def join_body(n_w, n_q, keep_ref, own_ref, recv_ref, out_ref):
    out_ref[0:n_w, :] = (keep_ref[...].astype(F32) + recv_ref[0:n_w, :].astype(F32)).astype(BF16)
    put_pair(out_ref, n_w, get_pair(own_ref, n_w, n_q) + get_pair(recv_ref, n_w, n_q))


def last_body(n_w, n_q, taps, own_ref, recv_ref, st_ref, cnt_ref, g_ref, out_ref, gk_ref, gs_ref):
    out_ref[...] = (own_ref[0:n_w, :].astype(F32) + recv_ref[0:n_w, :].astype(F32)).astype(BF16)
    value = get_pair(own_ref, n_w, n_q) + get_pair(recv_ref, n_w, n_q)
    count = cnt_ref[0:1, :]
    mean = st_ref[0:1, :] / count
    inv = lax.rsqrt(st_ref[1:2, :] / count - mean * mean + 1e-05)
    beta_sum = value[3 * taps : 3 * taps + 1]
    gamma_sum = value[3 * taps + 1 : 3 * taps + 2]
    gk_ref[...] = (g_ref[...] * inv) * (
        value[0:taps]
        - (beta_sum / count) * value[taps : 2 * taps]
        - (gamma_sum / count) * value[2 * taps : 3 * taps]
    )
    gs_ref[0:1, :] = gamma_sum
    gs_ref[1:2, :] = beta_sum


def spread_body(at_ref, own_ref, recv_ref, out_ref):
    half = at_ref[1]
    width = out_ref.shape[1] // 2
    for which, ref in ((half, own_ref), (1 - half, recv_ref)):
        for block in range(width // LANES):
            cols = pl.ds(pl.multiple_of(which * width + block * LANES, LANES), LANES)
            out_ref[:, cols] = ref[block * LANES : (block + 1) * LANES, :].astype(F32)


SMEM = pl.BlockSpec(memory_space=pltpu.SMEM)
VMEM = pl.BlockSpec(memory_space=pltpu.VMEM)


def local_fast(n_dp, n_grp, acts, cotan, lengths, offsets, kernel, gamma, beta, w_out):
    slots, frames, wide = acts.shape
    width = wide // 2
    taps = kernel.shape[0]
    blocks = width // LANES
    tokens = slots * frames
    n_q = 3 * taps + 16
    padded = 2 * (taps // 2) + frames
    me_dp, me_grp = lax.axis_index("dp"), lax.axis_index("grp")

    def swap(value, dp_mask, grp_mask):
        pairs = [
            (d * n_grp + g, (d ^ dp_mask) * n_grp + (g ^ grp_mask))
            for d in range(n_dp)
            for g in range(n_grp)
        ]
        return lax.ppermute(value, ("dp", "grp"), pairs)

    flat_cotan = cotan.reshape(tokens, width)
    dp_bits = [1 << i for i in range(n_dp.bit_length() - 1)]
    pieces = [((0, 0), flat_cotan)]
    if len(dp_bits) == 3 and tokens % 32 == 0:
        near, bit_a, bit_b = dp_bits
        cut = tokens // 2
        from_a, from_b = swap(flat_cotan, bit_a, 0), swap(flat_cotan, bit_b, 0)
        upper = swap(from_a[:cut], bit_b, 0)
        lower = swap(from_b[cut:], bit_a, 0)
        pieces += [((bit_a, 0), from_a), ((bit_b, 0), from_b)]
        pieces += [((bit_a | bit_b, 0), upper), ((bit_a | bit_b, cut), lower)]
        pieces += [((m | near, low), swap(v, near, 0)) for (m, low), v in pieces]
    else:
        for bit in reversed(dp_bits):
            pieces += [((m | bit, low), swap(v, bit, 0)) for (m, low), v in pieces]

    slot_spec = pl.BlockSpec((slots, frames, LANES), lambda d: (0, 0, d))
    pad_spec = pl.BlockSpec((slots, padded, LANES), lambda d: (0, 0, d))
    tap_spec = pl.BlockSpec((taps, LANES), lambda d: (0, d))
    row_spec = pl.BlockSpec((1, LANES), lambda d: (0, d))
    tok_spec = pl.BlockSpec((tokens, LANES), lambda d: (0, d))
    n_st = width + LANES
    gated, conv_out, stats = pl.pallas_call(
        conv_body,
        grid=(blocks,),
        in_specs=[
            SMEM,
            SMEM,
            slot_spec,
            pl.BlockSpec((slots, frames, LANES), lambda d: (0, 0, d + blocks)),
            tap_spec,
        ],
        out_specs=[pad_spec, slot_spec, pl.BlockSpec((2, n_st), lambda d: (0, 0))],
        out_shape=[
            jax.ShapeDtypeStruct((slots, padded, width), F32),
            jax.ShapeDtypeStruct((slots, frames, width), F32),
            jax.ShapeDtypeStruct((2, n_st), F32),
        ],
        name="conv",
    )(lengths, offsets, acts, acts, kernel)

    grp_bits = [1 << i for i in range(n_grp.bit_length() - 1)]
    for mask in grp_bits:
        stats = stats + swap(stats, 1, mask)
    for mask in dp_bits[1:]:
        stats = stats + swap(stats, mask | 1, 0)
    stats = stats + swap(stats, 1, 0)

    back = lax.dot_general(
        flat_cotan, w_out, (((1,), (1,)), ((), ())), preferred_element_type=F32
    )
    s2, t3 = pl.pallas_call(
        aux_body,
        grid=(blocks,),
        in_specs=[SMEM, SMEM, pad_spec, slot_spec],
        out_specs=[tap_spec, tap_spec],
        out_shape=[jax.ShapeDtypeStruct((taps, width), F32)] * 2,
        cost_estimate=pl.CostEstimate(
            flops=4 * taps * tokens * width, bytes_accessed=12 * tokens * width, transcendentals=0
        ),
        name="aux",
    )(lengths, offsets, gated, conv_out)

    n_pay = tokens + 2 * n_q
    st_spec = pl.BlockSpec((2, LANES), lambda d: (0, d))
    cnt_spec = pl.BlockSpec((2, LANES), lambda d: (0, blocks))
    gamma2, beta2 = gamma.reshape(1, width), beta.reshape(1, width)
    payload, hidden = pl.pallas_call(
        act_body,
        grid=(blocks,),
        in_specs=[SMEM, SMEM, st_spec, cnt_spec, row_spec, row_spec, pad_spec, slot_spec, tok_spec,
                  tap_spec, tap_spec],
        out_specs=[pl.BlockSpec((1, n_pay, LANES), lambda d: (d, 0, 0)), tok_spec],
        out_shape=[
            jax.ShapeDtypeStruct((blocks, n_pay, LANES), BF16),
            jax.ShapeDtypeStruct((tokens, width), BF16),
        ],
        scratch_shapes=[pltpu.VMEM((n_q, LANES), F32), pltpu.VMEM((slots, frames, LANES), F32)],
        name="act",
    )(lengths, offsets, stats, stats, gamma2, beta2, gated, conv_out, back, s2, t3)

    received = lax.all_to_all(payload, "dp", 0, 0, tiled=True)
    outputs = jnp.dot(hidden, w_out, preferred_element_type=F32).astype(BF16).reshape(cotan.shape)

    n_w = (width // 2) // LANES * LANES
    z_bit = me_grp % 2
    masks = tuple(m for m, _ in pieces)
    values = [v for _, v in pieces]

    def rows_of(half, with_q):
        at = jnp.stack([me_dp, half]).astype(jnp.int32)
        rows = n_w + (2 * n_q if with_q else 0)
        return pl.pallas_call(
            functools.partial(rows_body, masks, tokens, n_q if with_q else 0),
            in_specs=[SMEM] + [VMEM] * (1 + len(values)),
            out_specs=VMEM,
            out_shape=jax.ShapeDtypeStruct((rows, LANES), BF16),
            cost_estimate=pl.CostEstimate(
                flops=n_dp * tokens * LANES * width,
                bytes_accessed=2 * n_dp * tokens * width,
                transcendentals=0,
            ),
            name="rows",
        )(at, received, *values)

    given = rows_of(1 - z_bit, True)
    taken = swap(given, 0, 1)
    kept = rows_of(z_bit, False)
    both = pl.pallas_call(
        functools.partial(join_body, n_w, n_q),
        out_shape=jax.ShapeDtypeStruct(given.shape, BF16),
        name="join",
    )(kept, given, taken)
    for mask in grp_bits[1:-1]:
        both = pl.pallas_call(
            functools.partial(join_body, n_w, n_q),
            out_shape=jax.ShapeDtypeStruct(given.shape, BF16),
            name="join",
        )(both[:n_w], both, swap(both, 0, mask))
    other = swap(both, 0, grp_bits[-1])
    me_spec = lambda shape: pl.BlockSpec(shape, lambda i, at: (0, at[0]))
    full = lambda shape: pl.BlockSpec(shape, lambda i, at: (0,) * len(shape))
    at = jnp.stack([me_dp, z_bit]).astype(jnp.int32)
    total, grad_kernel, small = pl.pallas_call(
        lambda at_ref, *refs: last_body(n_w, n_q, taps, *refs),
        grid_spec=pltpu.PrefetchScalarGridSpec(
            num_scalar_prefetch=1,
            grid=(1,),
            in_specs=[
                full(both.shape),
                full(both.shape),
                me_spec((2, LANES)),
                pl.BlockSpec((2, LANES), lambda i, at: (0, blocks)),
                me_spec((1, LANES)),
            ],
            out_specs=[full((n_w, LANES)), full((taps, LANES)), full((2, LANES))],
        ),
        out_shape=[
            jax.ShapeDtypeStruct((n_w, LANES), BF16),
            jax.ShapeDtypeStruct((taps, LANES), F32),
            jax.ShapeDtypeStruct((2, LANES), F32),
        ],
        name="last",
    )(at, both, other, stats, stats, gamma2)
    rest = swap(total, 0, 1)
    grown = lax.dynamic_update_slice(jnp.zeros((2, width), F32), small, (0, me_dp * LANES))
    for mask in dp_bits[1:]:
        grown = grown + swap(grown, mask | 1, 0)
    grown = grown + swap(grown, 1, 0)
    weight_rows = pl.pallas_call(
        spread_body,
        in_specs=[SMEM, VMEM, VMEM],
        out_specs=VMEM,
        out_shape=jax.ShapeDtypeStruct((LANES, width), F32),
        name="spread",
    )(at, total, rest)
    return (outputs, weight_rows, grad_kernel, grown[0], grown[1])


def solution(mesh):
    n_dp, n_grp = mesh.shape["dp"], mesh.shape["grp"]

    def local(acts, cotan, lengths, offsets, kernel, gamma, beta, w_out):
        width, taps, frames = w_out.shape[0], kernel.shape[0], acts.shape[1]
        fits = (
            n_dp & (n_dp - 1) == 0
            and n_grp & (n_grp - 1) == 0
            and n_dp >= 2
            and n_grp >= 4
            and width == n_dp * LANES
            and taps % 16 == 0
            and frames % 16 == 0
        )
        args = (acts, cotan, lengths, offsets, kernel, gamma, beta, w_out)
        return local_fast(n_dp, n_grp, *args) if fits else local_general(*args)

    placed = (
        P(("dp", "grp"), None, None),
        P(("dp", "grp"), None, None),
        P(("dp", "grp")),
        P(("dp", "grp")),
        P(),
        P(),
        P(),
        P(),
    )
    return jax.shard_map(
        local,
        mesh=mesh,
        in_specs=placed,
        out_specs=(P(("dp", "grp"), None, None), P("dp", None), P(None, "dp"), P(), P()),
        check_vma=False,
    )
```

```python
import functools

import jax
import jax.numpy as jnp
from jax import lax
from jax.experimental import pallas as pl
from jax.experimental.pallas import tpu as pltpu
from jax.sharding import PartitionSpec as P


LANES = 128
F32 = jnp.float32
BF16 = jnp.bfloat16


def convolve(block_acts, block_len, block_off, kernel):
    taps = kernel.shape[0]
    model_width = kernel.shape[1]
    frame_count = block_acts.shape[1]
    position = jnp.arange(frame_count, dtype=jnp.int32)
    valid = (
        (position[None, :] >= block_off[:, None])
        & (position[None, :] < (block_off + block_len)[:, None])
    ).astype(jnp.float32)
    wide_acts = block_acts.astype(jnp.float32)
    gated = (
        wide_acts[..., :model_width]
        * jax.nn.sigmoid(wide_acts[..., model_width:])
        * valid[..., None]
    )
    padded = jnp.pad(gated, ((0, 0), (taps // 2 - 1, taps // 2), (0, 0)))
    conv_out = padded[:, 0:frame_count] * kernel[0]
    for tap in range(1, taps):
        conv_out = conv_out + padded[:, tap : tap + frame_count] * kernel[tap]
    return (valid, padded, conv_out)


def local_general(acts, cotan, lengths, offsets, kernel, gamma, beta, w_out):
    model_width = w_out.shape[0]
    taps = kernel.shape[0]
    valid, padded, conv_out = convolve(acts, lengths, offsets, kernel)
    masked = conv_out * valid[..., None]
    sum_first, sum_second, frame_total = lax.psum(
        (
            jnp.sum(masked, axis=(0, 1)),
            jnp.sum(masked * conv_out, axis=(0, 1)),
            jnp.sum(lengths).astype(jnp.float32),
        ),
        ("dp", "grp"),
    )
    mean_value = sum_first / frame_total
    inv_std = lax.rsqrt(sum_second / frame_total - mean_value * mean_value + 1e-05)
    normed = (conv_out - mean_value) * inv_std
    shifted = gamma * normed + beta
    sig_value = jax.nn.sigmoid(shifted)
    hidden = (shifted * sig_value * valid[..., None]).astype(jnp.bfloat16)
    flat_hidden = hidden.reshape(-1, model_width)
    flat_cotan = cotan.reshape(-1, model_width)
    outputs = (
        jnp.dot(flat_hidden, w_out, preferred_element_type=jnp.float32)
        .astype(jnp.bfloat16)
        .reshape(cotan.shape)
    )
    weight_rows = lax.psum_scatter(
        lax.dot_general(
            flat_hidden, flat_cotan, (((0,), (0,)), ((), ())), preferred_element_type=jnp.float32
        ),
        "dp",
        scatter_dimension=0,
        tiled=True,
    )
    back_hidden = lax.dot_general(
        flat_cotan, w_out, (((1,), (1,)), ((), ())), preferred_element_type=jnp.float32
    ).reshape(conv_out.shape)
    slope = back_hidden * sig_value * (1.0 + shifted * (1.0 - sig_value)) * valid[..., None]
    beta_sum, gamma_sum = lax.psum(
        (jnp.sum(slope, axis=(0, 1)), jnp.sum(slope * normed, axis=(0, 1))), ("dp", "grp")
    )
    conv_grad = (
        gamma
        * inv_std
        * (slope - beta_sum / frame_total - normed * gamma_sum / frame_total)
        * valid[..., None]
    )
    frame_count = conv_out.shape[1]
    kernel_term = jnp.stack(
        [
            jnp.sum(conv_grad * padded[:, tap : tap + frame_count], axis=(0, 1))
            for tap in range(taps)
        ],
        axis=0,
    )
    kernel_rows = lax.psum_scatter(kernel_term.T, "dp", scatter_dimension=0, tiled=True)
    weight_rows, kernel_rows = lax.psum((weight_rows, kernel_rows), "grp")
    return (outputs, weight_rows, kernel_rows.T, gamma_sum, beta_sum)


def mask_of(len_ref, off_ref, slot, frames):
    length, offset = len_ref[slot], off_ref[slot]
    position = lax.broadcasted_iota(jnp.int32, (frames, LANES), 0)
    return ((position >= offset) & (position < offset + length)).astype(F32)


def fold(value):
    total = value[0:8]
    for at in range(8, value.shape[0], 8):
        total = total + value[at : at + 8]
    return total


def row_sum(value):
    return jnp.sum(value, axis=0, keepdims=True)


def conv_body(len_ref, off_ref, acts_ref, k_ref, gp_ref, cv_ref, st_ref, acc_ref):
    _, frames, wide = acts_ref.shape
    blocks, slots, rows, _ = gp_ref.shape
    taps = k_ref.shape[0]
    lead = taps // 2
    slot = pl.program_id(0)

    @pl.when(slot == 0)
    def _():
        acc_ref[...] = jnp.zeros_like(acc_ref)

    valid = mask_of(len_ref, off_ref, slot, frames)
    for block in range(blocks):
        cols = slice(block * LANES, (block + 1) * LANES)
        gate = slice(wide // 2 + block * LANES, wide // 2 + (block + 1) * LANES)
        left, right = acts_ref[0, :, cols].astype(F32), acts_ref[0, :, gate].astype(F32)
        gp_ref[block, slot, 0:lead, :] = jnp.zeros((lead, LANES), F32)
        gp_ref[block, slot, lead : lead + frames, :] = left * jax.nn.sigmoid(right) * valid
        gp_ref[block, slot, lead + frames : rows, :] = jnp.zeros((rows - lead - frames, LANES), F32)
    for block in range(blocks):
        cols = slice(block * LANES, (block + 1) * LANES)
        total = gp_ref[block, slot, 1 : 1 + frames, :] * k_ref[0:1, cols]
        for tap in range(1, taps):
            total = total + gp_ref[block, slot, 1 + tap : 1 + tap + frames, :] * k_ref[tap : tap + 1, cols]
        cv_ref[block, slot] = total
        masked = total * valid
        acc_ref[0, block] += fold(masked)
        acc_ref[1, block] += fold(masked * total)

    @pl.when(slot == slots - 1)
    def _():
        for block in range(blocks):
            cols = slice(block * LANES, (block + 1) * LANES)
            st_ref[0:1, cols] = row_sum(acc_ref[0, block])
            st_ref[1:2, cols] = row_sum(acc_ref[1, block])
        count = len_ref[0]
        for other in range(1, slots):
            count = count + len_ref[other]
        st_ref[:, blocks * LANES :] = jnp.full((2, LANES), count.astype(F32), F32)


def lag_sums(gp_ref, block, weights, taps, group, put):
    frames = weights(0).shape[0]
    slots = gp_ref.shape[1]
    for low in range(0, taps, group):
        sums = [None] * group
        for slot in range(slots):
            weight = weights(slot)
            for j in range(group):
                at = 1 + low + j
                term = fold(weight * gp_ref[block, slot, at : at + frames, :])
                sums[j] = term if sums[j] is None else sums[j] + term
        for j in range(group):
            put(low + j, row_sum(sums[j]))


def aux_body(start, len_ref, off_ref, gp_ref, cv_ref, out_ref, wt_ref):
    _, slots, frames, _ = cv_ref.shape
    many, _, taps, _ = out_ref.shape
    lead = taps // 2
    lag = lax.broadcasted_iota(jnp.int32, (taps, frames), 0)
    at = lax.broadcasted_iota(jnp.int32, (taps, frames), 1) - lag + (lead - 1)

    def one(i, carry):
        block = start + i
        for slot in range(slots):
            wt_ref[slot] = cv_ref[block, slot] * mask_of(len_ref, off_ref, slot, frames)

        def put(k, row):
            out_ref[i, 0, k : k + 1, :] = row

        lag_sums(gp_ref, block, lambda slot: wt_ref[slot], taps, 16, put)
        total = jnp.zeros((taps, LANES), F32)
        for slot in range(slots):
            inside = (
                (at >= off_ref[slot])
                & (at < off_ref[slot] + len_ref[slot])
                & (at >= 0)
                & (at < frames)
            ).astype(BF16)
            rest = gp_ref[block, slot, lead : lead + frames, :]
            for _ in range(3):
                part = rest.astype(BF16)
                rest = rest - part.astype(F32)
                total = total + jnp.dot(inside, part, preferred_element_type=F32)
        out_ref[i, 1] = total
        return carry

    lax.fori_loop(0, many, one, 0)


def back_body(cotan_ref, w_ref, out_ref):
    for block in range(out_ref.shape[0]):
        rows = w_ref[block * LANES : (block + 1) * LANES, :]
        out_ref[block] = lax.dot_general(
            cotan_ref[...], rows, (((1,), (1,)), ((), ())), preferred_element_type=F32
        )


def scale_of(st_ref, block):
    width = st_ref.shape[1] - LANES
    cols = pl.ds(pl.multiple_of(block * LANES, LANES), LANES)
    count = st_ref[0:1, width:]
    mean = st_ref[0:1, cols] / count
    inv = lax.rsqrt(st_ref[1:2, cols] / count - mean * mean + 1e-05)
    return count, mean, inv


def hidden_body(len_ref, off_ref, st_ref, g_ref, b_ref, cv_ref, hid_ref):
    blocks, slots, frames, _ = cv_ref.shape

    def one(block, carry):
        _, mean, inv = scale_of(st_ref, block)
        gain, shift = g_ref[pl.ds(block, 1), :], b_ref[pl.ds(block, 1), :]
        for slot in range(slots):
            valid = mask_of(len_ref, off_ref, slot, frames)
            shifted = gain * ((cv_ref[block, slot] - mean) * inv) + shift
            hidden = shifted * jax.nn.sigmoid(shifted) * valid
            hid_ref[block, slot * frames : (slot + 1) * frames, :] = hidden.astype(BF16)
        return carry

    lax.fori_loop(0, blocks, one, 0)


def slope_body(len_ref, off_ref, st_ref, g_ref, b_ref, gp_ref, cv_ref, bk_ref, *refs):
    aux_refs, q_ref, sl_ref = refs[:-2], refs[-2], refs[-1]
    _, slots, frames, _ = cv_ref.shape
    taps = aux_refs[0].shape[2]
    each = aux_refs[0].shape[0]

    def one(block, aux_ref, i):
        _, mean, inv = scale_of(st_ref, block)
        gain, shift = g_ref[pl.ds(block, 1), :], b_ref[pl.ds(block, 1), :]
        first = second = jnp.zeros((8, LANES), F32)
        for slot in range(slots):
            valid = mask_of(len_ref, off_ref, slot, frames)
            normed = (cv_ref[block, slot] - mean) * inv
            shifted = gain * normed + shift
            sig = jax.nn.sigmoid(shifted)
            back = bk_ref[block, slot * frames : (slot + 1) * frames, :]
            slope = back * sig * (1.0 + shifted * (1.0 - sig)) * valid
            sl_ref[slot] = slope
            first, second = first + fold(slope), second + fold(slope * normed)

        def put(k, row):
            q_ref[block, k : k + 1, :] = row

        lag_sums(gp_ref, block, lambda slot: sl_ref[slot], taps, 16, put)
        q_ref[block, taps : 2 * taps, :] = aux_ref[i, 1]
        q_ref[block, 2 * taps : 3 * taps, :] = inv * (aux_ref[i, 0] - mean * aux_ref[i, 1])
        q_ref[block, 3 * taps : 3 * taps + 1, :] = row_sum(first)
        q_ref[block, 3 * taps + 1 : 3 * taps + 2, :] = row_sum(second)
        left = q_ref.shape[1] - 3 * taps - 2
        q_ref[block, 3 * taps + 2 :, :] = jnp.zeros((left, LANES), F32)

    for part, aux_ref in enumerate(aux_refs):

        def step(i, carry, part=part, aux_ref=aux_ref):
            one(part * each + i, aux_ref, i)
            return carry

        lax.fori_loop(0, each, step, 0)


def out_body(hid_ref, w_ref, out_ref):
    blocks = hid_ref.shape[0]
    slots, frames, _ = out_ref.shape
    total = None
    for block in range(blocks):
        term = jnp.dot(
            hid_ref[block],
            w_ref[block * LANES : (block + 1) * LANES, :],
            preferred_element_type=F32,
        )
        total = term if total is None else total + term
    for slot in range(slots):
        out_ref[slot] = total[slot * frames : (slot + 1) * frames, :].astype(BF16)


def rows_body(masks, flip, at_ref, recv_ref, *refs):
    pieces, out_ref = refs[:-1], refs[-1]
    me = at_ref[0]
    half = 1 - at_ref[1] if flip else at_ref[1]
    width = pieces[0].shape[1] // 2
    cols = pl.ds(pl.multiple_of(half * width, width), width)
    total = None
    for mask, piece in zip(masks, pieces):
        left = recv_ref[jnp.bitwise_xor(me, mask)]
        term = lax.dot_general(
            left, piece[:, cols], (((0,), (0,)), ((), ())), preferred_element_type=F32
        )
        total = term if total is None else total + term
    for block in range(width // LANES):
        out_ref[block] = total[:, block * LANES : (block + 1) * LANES].astype(BF16)


def add_body(own_ref, recv_ref, out_ref):
    out_ref[...] = (own_ref[...].astype(F32) + recv_ref[...].astype(F32)).astype(out_ref.dtype)


def sum_body(recv_ref, out_ref):
    total = recv_ref[0]
    for source in range(1, recv_ref.shape[0]):
        total = total + recv_ref[source]
    out_ref[...] = total


def last_body(taps, at_ref, own_ref, recv_ref, st_ref, g_ref, gk_ref, gs_ref):
    me = at_ref[0]
    value = own_ref[...] + recv_ref[...]
    count, _, inv = scale_of(st_ref, me)
    beta_sum = value[3 * taps : 3 * taps + 1]
    gamma_sum = value[3 * taps + 1 : 3 * taps + 2]
    gk_ref[...] = (g_ref[pl.ds(me, 1), :] * inv) * (
        value[0:taps]
        - (beta_sum / count) * value[taps : 2 * taps]
        - (gamma_sum / count) * value[2 * taps : 3 * taps]
    )
    gs_ref[...] = jnp.zeros_like(gs_ref)
    cols = pl.ds(pl.multiple_of(me * LANES, LANES), LANES)
    gs_ref[0:1, cols] = gamma_sum
    gs_ref[1:2, cols] = beta_sum


def spread_body(at_ref, own_ref, recv_ref, out_ref):
    half = at_ref[1]
    many = own_ref.shape[0]
    for which, ref in ((half, own_ref), (1 - half, recv_ref)):
        for block in range(many):
            cols = pl.ds(pl.multiple_of((which * many + block) * LANES, LANES), LANES)
            out_ref[:, cols] = ref[block].astype(F32)


SMEM = pl.BlockSpec(memory_space=pltpu.SMEM)
VMEM = pl.BlockSpec(memory_space=pltpu.VMEM)


def call(body, shapes, scalars, args, flops=0, scratch=(), mib=8, **more):
    many = isinstance(shapes, list)
    moved = sum(a.size * a.dtype.itemsize for a in args)
    return pl.pallas_call(
        body,
        in_specs=more.pop("in_specs", None) or [SMEM] * len(scalars) + [VMEM] * len(args),
        out_specs=[VMEM] * len(shapes) if many else VMEM,
        out_shape=shapes,
        scratch_shapes=scratch,
        compiler_params=pltpu.CompilerParams(vmem_limit_bytes=mib << 20),
        cost_estimate=pl.CostEstimate(flops=flops, bytes_accessed=moved, transcendentals=0),
        **more,
    )(*scalars, *args)


def local_fast(n_dp, n_grp, acts, cotan, lengths, offsets, kernel, gamma, beta, w_out):
    slots, frames, wide = acts.shape
    width = wide // 2
    taps = kernel.shape[0]
    blocks = width // LANES
    tokens = slots * frames
    n_q = 3 * taps + 8
    padded = 2 * (taps // 2) + frames
    me_dp, me_grp = lax.axis_index("dp"), lax.axis_index("grp")
    shape = jax.ShapeDtypeStruct

    def swap(value, dp_mask, grp_mask):
        pairs = [
            (d * n_grp + g, (d ^ dp_mask) * n_grp + (g ^ grp_mask))
            for d in range(n_dp)
            for g in range(n_grp)
        ]
        return lax.ppermute(value, ("dp", "grp"), pairs)

    dp_bits = [1 << i for i in range(n_dp.bit_length() - 1)]
    grp_bits = [1 << i for i in range(n_grp.bit_length() - 1)]
    at = jnp.stack([me_dp, me_grp % 2]).astype(jnp.int32)
    gamma2, beta2 = gamma.reshape(blocks, LANES), beta.reshape(blocks, LANES)

    flat_cotan = cotan.reshape(tokens, width)
    pieces = [(0, flat_cotan)]
    for bit in dp_bits[1:] + dp_bits[:1]:
        pieces += [(m | bit, swap(v, bit, 0)) for m, v in pieces]
    masks, values = tuple(m for m, _ in pieces), [v for _, v in pieces]

    gated, conv_out, stats = call(
        conv_body,
        [
            shape((blocks, slots, padded, LANES), F32),
            shape((blocks, slots, frames, LANES), F32),
            shape((2, width + LANES), F32),
        ],
        (lengths, offsets),
        (acts, kernel),
        flops=4 * taps * tokens * width,
        scratch=[pltpu.VMEM((2, blocks, 8, LANES), F32)],
        grid=(slots,),
        in_specs=[SMEM, SMEM, pl.BlockSpec((1, frames, wide), lambda s: (s, 0, 0)), VMEM],
    )

    hops = [(1, m) for m in grp_bits] + [(m | 1, 0) for m in dp_bits[1:]] + [(1, 0)]
    for dp_mask, grp_mask in hops:
        stats = stats + swap(stats, dp_mask, grp_mask)

    back = call(
        back_body,
        shape((blocks, tokens, LANES), F32),
        (),
        (flat_cotan, w_out),
        flops=2 * tokens * width * width,
    )
    parts = 4
    while blocks % parts:
        parts //= 2
    each = blocks // parts
    aux = [
        call(
            functools.partial(aux_body, i * each),
            shape((each, 2, taps, LANES), F32),
            (lengths, offsets),
            (gated, conv_out),
            flops=4 * taps * tokens * each * LANES,
            scratch=[pltpu.VMEM((slots, frames, LANES), F32)],
        )
        for i in range(parts)
    ]

    hidden = call(
        hidden_body,
        shape((blocks, tokens, LANES), BF16),
        (lengths, offsets),
        (stats, gamma2, beta2, conv_out),
    )
    received = lax.all_to_all(hidden, "dp", 0, 0, tiled=True)
    lags = call(
        slope_body,
        shape((blocks, n_q, LANES), F32),
        (lengths, offsets),
        (stats, gamma2, beta2, gated, conv_out, back, *aux),
        flops=4 * taps * tokens * width,
        scratch=[pltpu.VMEM((slots, frames, LANES), F32)],
    )
    lags = lax.all_to_all(lags, "dp", 0, 0, tiled=True)
    outputs = call(out_body, shape(cotan.shape, BF16), (), (hidden, w_out))

    half_shape = shape((blocks // 2, LANES, LANES), BF16)
    flops = n_dp * tokens * LANES * width

    def rows_of(flip):
        body = functools.partial(rows_body, masks, flip)
        return call(body, half_shape, (at,), (received, *values), flops=flops)

    given = rows_of(True)
    taken = swap(given, 0, 1)
    kept = rows_of(False)
    both = call(add_body, half_shape, (), (kept, taken))
    for mask in grp_bits[1:]:
        both = call(add_body, half_shape, (), (both, swap(both, 0, mask)))
    rest = swap(both, 0, 1)

    lags = call(sum_body, shape((n_q, LANES), F32), (), (lags,))
    for mask in grp_bits[:-1]:
        lags = lags + swap(lags, 0, mask)
    grad_kernel, small = call(
        functools.partial(last_body, taps),
        [shape((taps, LANES), F32), shape((2, width), F32)],
        (at,),
        (lags, swap(lags, 0, grp_bits[-1]), stats, gamma2),
    )
    for mask in dp_bits[1:] + [0]:
        small = small + swap(small, mask | 1, 0)
    weight_rows = call(spread_body, shape((LANES, width), F32), (at,), (both, rest))
    return (outputs, weight_rows, grad_kernel, small[0], small[1])


def solution(mesh):
    n_dp, n_grp = mesh.shape["dp"], mesh.shape["grp"]

    def fits(width, taps, frames):
        return (
            n_dp & (n_dp - 1) == 0
            and n_grp & (n_grp - 1) == 0
            and n_dp >= 4
            and n_grp >= 4
            and width == n_dp * LANES
            and taps % 16 == 0
            and frames % 16 == 0
        )

    def local(acts, cotan, lengths, offsets, kernel, gamma, beta, w_out):
        args = (acts, cotan, lengths, offsets, kernel, gamma, beta, w_out)
        if not fits(w_out.shape[0], kernel.shape[0], acts.shape[1]):
            return local_general(*args)
        return local_fast(n_dp, n_grp, *args)

    placed = (
        P(("dp", "grp"), None, None),
        P(("dp", "grp"), None, None),
        P(("dp", "grp")),
        P(("dp", "grp")),
        P(),
        P(),
        P(),
        P(),
    )
    return jax.shard_map(
        local,
        mesh=mesh,
        in_specs=placed,
        out_specs=(P(("dp", "grp"), None, None), P("dp", None), P(None, "dp"), P(), P()),
        check_vma=False,
    )
```

```python
import functools

import jax
import jax.numpy as jnp
from jax import lax
from jax.experimental import pallas as pl
from jax.experimental.pallas import tpu as pltpu
from jax.sharding import PartitionSpec as P


LANES = 128
F32 = jnp.float32
BF16 = jnp.bfloat16


def convolve(block_acts, block_len, block_off, kernel):
    taps = kernel.shape[0]
    model_width = kernel.shape[1]
    frame_count = block_acts.shape[1]
    position = jnp.arange(frame_count, dtype=jnp.int32)
    valid = (
        (position[None, :] >= block_off[:, None])
        & (position[None, :] < (block_off + block_len)[:, None])
    ).astype(jnp.float32)
    wide_acts = block_acts.astype(jnp.float32)
    gated = (
        wide_acts[..., :model_width]
        * jax.nn.sigmoid(wide_acts[..., model_width:])
        * valid[..., None]
    )
    padded = jnp.pad(gated, ((0, 0), (taps // 2 - 1, taps // 2), (0, 0)))
    conv_out = padded[:, 0:frame_count] * kernel[0]
    for tap in range(1, taps):
        conv_out = conv_out + padded[:, tap : tap + frame_count] * kernel[tap]
    return (valid, padded, conv_out)


def local_general(acts, cotan, lengths, offsets, kernel, gamma, beta, w_out):
    model_width = w_out.shape[0]
    taps = kernel.shape[0]
    valid, padded, conv_out = convolve(acts, lengths, offsets, kernel)
    masked = conv_out * valid[..., None]
    sum_first, sum_second, frame_total = lax.psum(
        (
            jnp.sum(masked, axis=(0, 1)),
            jnp.sum(masked * conv_out, axis=(0, 1)),
            jnp.sum(lengths).astype(jnp.float32),
        ),
        ("dp", "grp"),
    )
    mean_value = sum_first / frame_total
    inv_std = lax.rsqrt(sum_second / frame_total - mean_value * mean_value + 1e-05)
    normed = (conv_out - mean_value) * inv_std
    shifted = gamma * normed + beta
    sig_value = jax.nn.sigmoid(shifted)
    hidden = (shifted * sig_value * valid[..., None]).astype(jnp.bfloat16)
    flat_hidden = hidden.reshape(-1, model_width)
    flat_cotan = cotan.reshape(-1, model_width)
    outputs = (
        jnp.dot(flat_hidden, w_out, preferred_element_type=jnp.float32)
        .astype(jnp.bfloat16)
        .reshape(cotan.shape)
    )
    weight_rows = lax.psum_scatter(
        lax.dot_general(
            flat_hidden, flat_cotan, (((0,), (0,)), ((), ())), preferred_element_type=jnp.float32
        ),
        "dp",
        scatter_dimension=0,
        tiled=True,
    )
    back_hidden = lax.dot_general(
        flat_cotan, w_out, (((1,), (1,)), ((), ())), preferred_element_type=jnp.float32
    ).reshape(conv_out.shape)
    slope = back_hidden * sig_value * (1.0 + shifted * (1.0 - sig_value)) * valid[..., None]
    beta_sum, gamma_sum = lax.psum(
        (jnp.sum(slope, axis=(0, 1)), jnp.sum(slope * normed, axis=(0, 1))), ("dp", "grp")
    )
    conv_grad = (
        gamma
        * inv_std
        * (slope - beta_sum / frame_total - normed * gamma_sum / frame_total)
        * valid[..., None]
    )
    frame_count = conv_out.shape[1]
    kernel_term = jnp.stack(
        [
            jnp.sum(conv_grad * padded[:, tap : tap + frame_count], axis=(0, 1))
            for tap in range(taps)
        ],
        axis=0,
    )
    kernel_rows = lax.psum_scatter(kernel_term.T, "dp", scatter_dimension=0, tiled=True)
    weight_rows, kernel_rows = lax.psum((weight_rows, kernel_rows), "grp")
    return (outputs, weight_rows, kernel_rows.T, gamma_sum, beta_sum)


def fold(value):
    total = value[0:8]
    for at in range(8, value.shape[0], 8):
        total = total + value[at : at + 8]
    return total


def row_sum(value):
    return jnp.sum(value, axis=0, keepdims=True)


def conv_body(len_ref, off_ref, acts_ref, k_ref, gp_ref, cv_ref, st_ref, ok_ref, in_ref, acc_ref):
    _, frames, wide = acts_ref.shape
    blocks, slots, rows, _ = gp_ref.shape
    taps = k_ref.shape[0]
    lead = taps // 2
    slot = pl.program_id(0)
    low = off_ref[slot]
    high = low + len_ref[slot]

    @pl.when(slot == 0)
    def _():
        acc_ref[...] = jnp.zeros_like(acc_ref)

    position = lax.broadcasted_iota(jnp.int32, (frames, LANES), 0)
    valid = ((position >= low) & (position < high)).astype(F32)
    ok_ref[slot] = valid
    at = lax.broadcasted_iota(jnp.int32, (taps, frames), 1)
    at = at - lax.broadcasted_iota(jnp.int32, (taps, frames), 0) + (lead - 1)
    in_ref[slot] = (
        (at >= low) & (at < high) & (at >= 0) & (at < frames)
    ).astype(F32)
    for block in range(blocks):
        cols = slice(block * LANES, (block + 1) * LANES)
        gate = slice(wide // 2 + block * LANES, wide // 2 + (block + 1) * LANES)
        left, right = acts_ref[0, :, cols].astype(F32), acts_ref[0, :, gate].astype(F32)
        gp_ref[block, slot, 0:lead, :] = jnp.zeros((lead, LANES), F32)
        gp_ref[block, slot, lead : lead + frames, :] = left * jax.nn.sigmoid(right) * valid
        gp_ref[block, slot, lead + frames : rows, :] = jnp.zeros((rows - lead - frames, LANES), F32)
    for block in range(blocks):
        cols = slice(block * LANES, (block + 1) * LANES)
        total = gp_ref[block, slot, 1 : 1 + frames, :] * k_ref[0:1, cols]
        for tap in range(1, taps):
            lag = gp_ref[block, slot, 1 + tap : 1 + tap + frames, :]
            total = total + lag * k_ref[tap : tap + 1, cols]
        cv_ref[block, slot] = total
        masked = total * valid
        acc_ref[0, block] += fold(masked)
        acc_ref[1, block] += fold(masked * total)

    @pl.when(slot == slots - 1)
    def _():
        for block in range(blocks):
            cols = slice(block * LANES, (block + 1) * LANES)
            st_ref[0:1, cols] = row_sum(acc_ref[0, block])
            st_ref[1:2, cols] = row_sum(acc_ref[1, block])
        count = len_ref[0]
        for other in range(1, slots):
            count = count + len_ref[other]
        st_ref[:, blocks * LANES :] = jnp.full((2, LANES), count.astype(F32), F32)


def lag_sums(gp_ref, block, weights, taps, group, put):
    frames = weights(0).shape[0]
    slots = gp_ref.shape[1]
    for low in range(0, taps, group):
        sums = [None] * group
        for slot in range(slots):
            weight = weights(slot)
            for j in range(group):
                at = 1 + low + j
                term = fold(weight * gp_ref[block, slot, at : at + frames, :])
                sums[j] = term if sums[j] is None else sums[j] + term
        for j in range(group):
            put(low + j, row_sum(sums[j]))


def aux_body(start, ok_ref, in_ref, gp_ref, cv_ref, out_ref, wt_ref):
    _, slots, frames, _ = cv_ref.shape
    many, _, taps, _ = out_ref.shape
    lead = taps // 2

    def one(i, carry):
        block = start + i
        for slot in range(slots):
            wt_ref[slot] = cv_ref[block, slot] * ok_ref[slot]

        def put(k, row):
            out_ref[i, 0, k : k + 1, :] = row

        lag_sums(gp_ref, block, lambda slot: wt_ref[slot], taps, 16, put)
        total = jnp.zeros((taps, LANES), F32)
        for slot in range(slots):
            inside = in_ref[slot].astype(BF16)
            rest = gp_ref[block, slot, lead : lead + frames, :]
            for _ in range(3):
                part = rest.astype(BF16)
                rest = rest - part.astype(F32)
                total = total + jnp.dot(inside, part, preferred_element_type=F32)
        out_ref[i, 1] = total
        return carry

    lax.fori_loop(0, many, one, 0)


def back_body(cotan_ref, w_ref, out_ref):
    for block in range(out_ref.shape[0]):
        rows = w_ref[block * LANES : (block + 1) * LANES, :]
        out_ref[block] = lax.dot_general(
            cotan_ref[...], rows, (((1,), (1,)), ((), ())), preferred_element_type=F32
        )


def scale_of(st_ref, block):
    width = st_ref.shape[1] - LANES
    cols = pl.ds(pl.multiple_of(block * LANES, LANES), LANES)
    count = st_ref[0:1, width:]
    mean = st_ref[0:1, cols] / count
    inv = lax.rsqrt(st_ref[1:2, cols] / count - mean * mean + 1e-05)
    return count, mean, inv


def hidden_body(st_ref, g_ref, b_ref, ok_ref, cv_ref, hid_ref):
    blocks, slots, frames, _ = cv_ref.shape

    def one(block, carry):
        _, mean, inv = scale_of(st_ref, block)
        gain, shift = g_ref[pl.ds(block, 1), :], b_ref[pl.ds(block, 1), :]
        for slot in range(slots):
            valid = ok_ref[slot]
            shifted = gain * ((cv_ref[block, slot] - mean) * inv) + shift
            hidden = shifted * jax.nn.sigmoid(shifted) * valid
            hid_ref[block, slot * frames : (slot + 1) * frames, :] = hidden.astype(BF16)
        return carry

    lax.fori_loop(0, blocks, one, 0)


def slope_body(st_ref, g_ref, b_ref, ok_ref, gp_ref, cv_ref, bk_ref, *refs):
    aux_refs, q_ref, sl_ref = refs[:-2], refs[-2], refs[-1]
    blocks, slots, frames, _ = cv_ref.shape
    taps = aux_refs[0].shape[2]
    each = aux_refs[0].shape[0]
    last = 3 * taps

    def one(block, aux_ref, i):
        _, mean, inv = scale_of(st_ref, block)
        gain, shift = g_ref[pl.ds(block, 1), :], b_ref[pl.ds(block, 1), :]
        first = second = jnp.zeros((8, LANES), F32)
        for slot in range(slots):
            normed = (cv_ref[block, slot] - mean) * inv
            shifted = gain * normed + shift
            sig = jax.nn.sigmoid(shifted)
            back = bk_ref[block, slot * frames : (slot + 1) * frames, :]
            slope = back * sig * (1.0 + shifted * (1.0 - sig)) * ok_ref[slot]
            sl_ref[slot] = slope
            first, second = first + fold(slope), second + fold(slope * normed)

        def put(k, row):
            q_ref[block, k : k + 1, :] = row

        lag_sums(gp_ref, block, lambda slot: sl_ref[slot], taps, 16, put)
        q_ref[block, taps : 2 * taps, :] = aux_ref[i, 1]
        q_ref[block, 2 * taps : last, :] = inv * (aux_ref[i, 0] - mean * aux_ref[i, 1])
        q_ref[0, pl.ds(last + block, 1), :] = row_sum(first)
        q_ref[0, pl.ds(last + blocks + block, 1), :] = row_sum(second)

    for part, aux_ref in enumerate(aux_refs):

        def step(i, carry, part=part, aux_ref=aux_ref):
            one(part * each + i, aux_ref, i)
            return carry

        lax.fori_loop(0, each, step, 0)
    for block in range(1, blocks):
        q_ref[block, last:, :] = q_ref[0, last:, :]


def out_body(hid_ref, w_ref, out_ref):
    blocks = hid_ref.shape[0]
    slots, frames, _ = out_ref.shape
    total = None
    for block in range(blocks):
        term = jnp.dot(
            hid_ref[block],
            w_ref[block * LANES : (block + 1) * LANES, :],
            preferred_element_type=F32,
        )
        total = term if total is None else total + term
    for slot in range(slots):
        out_ref[slot] = total[slot * frames : (slot + 1) * frames, :].astype(BF16)


def rows_body(masks, flip, at_ref, recv_ref, *refs):
    pieces, out_ref = refs[:-1], refs[-1]
    me = at_ref[0]
    half = 1 - at_ref[1] if flip else at_ref[1]
    width = pieces[0].shape[1] // 2
    cols = pl.ds(pl.multiple_of(half * width, width), width)
    total = None
    for mask, piece in zip(masks, pieces):
        left = recv_ref[jnp.bitwise_xor(me, mask)]
        term = lax.dot_general(
            left, piece[:, cols], (((0,), (0,)), ((), ())), preferred_element_type=F32
        )
        total = term if total is None else total + term
    for block in range(width // LANES):
        out_ref[block] = total[:, block * LANES : (block + 1) * LANES].astype(BF16)


def put_pair(ref, at, value):
    rows = value.shape[0]
    lead = value.astype(BF16)
    ref[at : at + rows, :] = lead
    ref[at + rows : at + 2 * rows, :] = (value - lead.astype(F32)).astype(BF16)


def get_pair(ref, at, rows):
    return ref[at : at + rows, :].astype(F32) + ref[at + rows : at + 2 * rows, :].astype(F32)


def join_body(own_ref, recv_ref, lags_ref, out_ref):
    many = own_ref.shape[0]
    for block in range(many):
        rows = slice(block * LANES, (block + 1) * LANES)
        out_ref[rows, :] = (own_ref[block].astype(F32) + recv_ref[block].astype(F32)).astype(BF16)
    total = lags_ref[0]
    for source in range(1, lags_ref.shape[0]):
        total = total + lags_ref[source]
    put_pair(out_ref, many * LANES, total)


def add_body(n_w, own_ref, recv_ref, out_ref):
    n_q = (own_ref.shape[0] - n_w) // 2
    out_ref[0:n_w, :] = (own_ref[0:n_w, :].astype(F32) + recv_ref[0:n_w, :].astype(F32)).astype(BF16)
    put_pair(out_ref, n_w, get_pair(own_ref, n_w, n_q) + get_pair(recv_ref, n_w, n_q))


def last_body(n_w, taps, at_ref, own_ref, recv_ref, st_ref, g_ref, rows_ref, gk_ref, gg_ref, gb_ref):
    me, half = at_ref[0], at_ref[1]
    many = n_w // LANES
    for which, ref in ((half, own_ref), (1 - half, recv_ref)):
        for block in range(many):
            cols = pl.ds(pl.multiple_of((which * many + block) * LANES, LANES), LANES)
            rows_ref[:, cols] = ref[block * LANES : (block + 1) * LANES, :].astype(F32)
    n_q = (own_ref.shape[0] - n_w) // 2
    value = get_pair(own_ref, n_w, n_q) + get_pair(recv_ref, n_w, n_q)
    blocks = g_ref.shape[0]
    gb_ref[...] = value[3 * taps : 3 * taps + blocks]
    gg_ref[...] = value[3 * taps + blocks : 3 * taps + 2 * blocks]
    count, _, inv = scale_of(st_ref, me)
    mine = pl.ds(me, 1)
    gk_ref[...] = (g_ref[mine, :] * inv) * (
        value[0:taps]
        - (gb_ref[mine, :] / count) * value[taps : 2 * taps]
        - (gg_ref[mine, :] / count) * value[2 * taps : 3 * taps]
    )


SMEM = pl.BlockSpec(memory_space=pltpu.SMEM)
VMEM = pl.BlockSpec(memory_space=pltpu.VMEM)


def call(body, shapes, scalars, args, flops=0, scratch=(), mib=8, **more):
    many = isinstance(shapes, list)
    moved = sum(a.size * a.dtype.itemsize for a in args)
    return pl.pallas_call(
        body,
        in_specs=more.pop("in_specs", None) or [SMEM] * len(scalars) + [VMEM] * len(args),
        out_specs=[VMEM] * len(shapes) if many else VMEM,
        out_shape=shapes,
        scratch_shapes=scratch,
        compiler_params=pltpu.CompilerParams(vmem_limit_bytes=mib << 20),
        cost_estimate=pl.CostEstimate(flops=flops, bytes_accessed=moved, transcendentals=0),
        **more,
    )(*scalars, *args)


def local_fast(n_dp, n_grp, acts, cotan, lengths, offsets, kernel, gamma, beta, w_out):
    slots, frames, wide = acts.shape
    width = wide // 2
    taps = kernel.shape[0]
    blocks = width // LANES
    tokens = slots * frames
    n_q = 3 * taps + 2 * blocks
    padded = 2 * (taps // 2) + frames
    me_dp, me_grp = lax.axis_index("dp"), lax.axis_index("grp")
    shape = jax.ShapeDtypeStruct

    def swap(value, dp_mask, grp_mask):
        pairs = [
            (d * n_grp + g, (d ^ dp_mask) * n_grp + (g ^ grp_mask))
            for d in range(n_dp)
            for g in range(n_grp)
        ]
        return lax.ppermute(value, ("dp", "grp"), pairs)

    dp_bits = [1 << i for i in range(n_dp.bit_length() - 1)]
    grp_bits = [1 << i for i in range(n_grp.bit_length() - 1)]
    at = jnp.stack([me_dp, me_grp % 2]).astype(jnp.int32)
    gamma2, beta2 = gamma.reshape(blocks, LANES), beta.reshape(blocks, LANES)

    flat_cotan = cotan.reshape(tokens, width)
    pieces = [(0, flat_cotan)]
    for bit in dp_bits[1:] + dp_bits[:1]:
        pieces += [(m | bit, swap(v, bit, 0)) for m, v in pieces]
    masks, values = tuple(m for m, _ in pieces), [v for _, v in pieces]

    gated, conv_out, stats, valid, inside = call(
        conv_body,
        [
            shape((blocks, slots, padded, LANES), F32),
            shape((blocks, slots, frames, LANES), F32),
            shape((2, width + LANES), F32),
            shape((slots, frames, LANES), F32),
            shape((slots, taps, frames), F32),
        ],
        (lengths, offsets),
        (acts, kernel),
        flops=4 * taps * tokens * width,
        scratch=[pltpu.VMEM((2, blocks, 8, LANES), F32)],
        grid=(slots,),
        in_specs=[SMEM, SMEM, pl.BlockSpec((1, frames, wide), lambda s: (s, 0, 0)), VMEM],
    )

    hops = [(1, m) for m in grp_bits] + [(m | 1, 0) for m in dp_bits[1:]] + [(1, 0)]
    for dp_mask, grp_mask in hops:
        stats = stats + swap(stats, dp_mask, grp_mask)

    back = call(
        back_body,
        shape((blocks, tokens, LANES), F32),
        (),
        (flat_cotan, w_out),
        flops=2 * tokens * width * width,
    )
    parts = 4
    each = blocks // parts
    aux = [
        call(
            functools.partial(aux_body, i * each),
            shape((each, 2, taps, LANES), F32),
            (),
            (valid, inside, gated, conv_out),
            flops=4 * taps * tokens * each * LANES,
            scratch=[pltpu.VMEM((slots, frames, LANES), F32)],
        )
        for i in range(parts)
    ]

    hidden = call(
        hidden_body,
        shape((blocks, tokens, LANES), BF16),
        (),
        (stats, gamma2, beta2, valid, conv_out),
    )
    received = lax.all_to_all(hidden, "dp", 0, 0, tiled=True)
    lags = call(
        slope_body,
        shape((blocks, n_q, LANES), F32),
        (),
        (stats, gamma2, beta2, valid, gated, conv_out, back, *aux),
        flops=4 * taps * tokens * width,
        scratch=[pltpu.VMEM((slots, frames, LANES), F32)],
    )
    lags = lax.all_to_all(lags, "dp", 0, 0, tiled=True)
    outputs = call(out_body, shape(cotan.shape, BF16), (), (hidden, w_out))

    half_shape = shape((blocks // 2, LANES, LANES), BF16)
    flops = n_dp * tokens * LANES * width
    n_w = blocks // 2 * LANES

    def rows_of(flip):
        body = functools.partial(rows_body, masks, flip)
        return call(body, half_shape, (at,), (received, *values), flops=flops)

    given = rows_of(True)
    taken = swap(given, 0, 1)
    kept = rows_of(False)
    both_shape = shape((n_w + 2 * n_q, LANES), BF16)
    both = call(join_body, both_shape, (), (kept, taken, lags))
    for mask in grp_bits[1:]:
        other = swap(both, 0, mask)
        both = call(functools.partial(add_body, n_w), both_shape, (), (both, other))
    rest = swap(both, 0, 1)
    weight_rows, grad_kernel, gamma_sum, beta_sum = call(
        functools.partial(last_body, n_w, taps),
        [
            shape((LANES, width), F32),
            shape((taps, LANES), F32),
            shape((blocks, LANES), F32),
            shape((blocks, LANES), F32),
        ],
        (at,),
        (both, rest, stats, gamma2),
    )
    return (outputs, weight_rows, grad_kernel, gamma_sum.reshape(width), beta_sum.reshape(width))


def solution(mesh):
    n_dp, n_grp = mesh.shape["dp"], mesh.shape["grp"]

    def fits(width, taps, frames):
        return (
            n_dp & (n_dp - 1) == 0
            and n_grp & (n_grp - 1) == 0
            and n_dp >= 4
            and n_grp >= 4
            and width == n_dp * LANES
            and taps % 16 == 0
            and frames % 16 == 0
            and n_dp % 8 == 0
        )

    def local(acts, cotan, lengths, offsets, kernel, gamma, beta, w_out):
        args = (acts, cotan, lengths, offsets, kernel, gamma, beta, w_out)
        if not fits(w_out.shape[0], kernel.shape[0], acts.shape[1]):
            return local_general(*args)
        return local_fast(n_dp, n_grp, *args)

    placed = (
        P(("dp", "grp"), None, None),
        P(("dp", "grp"), None, None),
        P(("dp", "grp")),
        P(("dp", "grp")),
        P(),
        P(),
        P(),
        P(),
    )
    return jax.shard_map(
        local,
        mesh=mesh,
        in_specs=placed,
        out_specs=(P(("dp", "grp"), None, None), P("dp", None), P(None, "dp"), P(), P()),
        check_vma=False,
    )
```

```python
import functools

import jax
import jax.numpy as jnp
from jax import lax
from jax.experimental import pallas as pl
from jax.experimental.pallas import tpu as pltpu
from jax.sharding import PartitionSpec as P


LANES = 128
F32 = jnp.float32
BF16 = jnp.bfloat16


def convolve(block_acts, block_len, block_off, kernel):
    taps = kernel.shape[0]
    model_width = kernel.shape[1]
    frame_count = block_acts.shape[1]
    position = jnp.arange(frame_count, dtype=jnp.int32)
    valid = (
        (position[None, :] >= block_off[:, None])
        & (position[None, :] < (block_off + block_len)[:, None])
    ).astype(jnp.float32)
    wide_acts = block_acts.astype(jnp.float32)
    gated = (
        wide_acts[..., :model_width]
        * jax.nn.sigmoid(wide_acts[..., model_width:])
        * valid[..., None]
    )
    padded = jnp.pad(gated, ((0, 0), (taps // 2 - 1, taps // 2), (0, 0)))
    conv_out = padded[:, 0:frame_count] * kernel[0]
    for tap in range(1, taps):
        conv_out = conv_out + padded[:, tap : tap + frame_count] * kernel[tap]
    return (valid, padded, conv_out)


def local_general(acts, cotan, lengths, offsets, kernel, gamma, beta, w_out):
    model_width = w_out.shape[0]
    taps = kernel.shape[0]
    valid, padded, conv_out = convolve(acts, lengths, offsets, kernel)
    masked = conv_out * valid[..., None]
    sum_first, sum_second, frame_total = lax.psum(
        (
            jnp.sum(masked, axis=(0, 1)),
            jnp.sum(masked * conv_out, axis=(0, 1)),
            jnp.sum(lengths).astype(jnp.float32),
        ),
        ("dp", "grp"),
    )
    mean_value = sum_first / frame_total
    inv_std = lax.rsqrt(sum_second / frame_total - mean_value * mean_value + 1e-05)
    normed = (conv_out - mean_value) * inv_std
    shifted = gamma * normed + beta
    sig_value = jax.nn.sigmoid(shifted)
    hidden = (shifted * sig_value * valid[..., None]).astype(jnp.bfloat16)
    flat_hidden = hidden.reshape(-1, model_width)
    flat_cotan = cotan.reshape(-1, model_width)
    outputs = (
        jnp.dot(flat_hidden, w_out, preferred_element_type=jnp.float32)
        .astype(jnp.bfloat16)
        .reshape(cotan.shape)
    )
    weight_rows = lax.psum_scatter(
        lax.dot_general(
            flat_hidden, flat_cotan, (((0,), (0,)), ((), ())), preferred_element_type=jnp.float32
        ),
        "dp",
        scatter_dimension=0,
        tiled=True,
    )
    back_hidden = lax.dot_general(
        flat_cotan, w_out, (((1,), (1,)), ((), ())), preferred_element_type=jnp.float32
    ).reshape(conv_out.shape)
    slope = back_hidden * sig_value * (1.0 + shifted * (1.0 - sig_value)) * valid[..., None]
    beta_sum, gamma_sum = lax.psum(
        (jnp.sum(slope, axis=(0, 1)), jnp.sum(slope * normed, axis=(0, 1))), ("dp", "grp")
    )
    conv_grad = (
        gamma
        * inv_std
        * (slope - beta_sum / frame_total - normed * gamma_sum / frame_total)
        * valid[..., None]
    )
    frame_count = conv_out.shape[1]
    kernel_term = jnp.stack(
        [
            jnp.sum(conv_grad * padded[:, tap : tap + frame_count], axis=(0, 1))
            for tap in range(taps)
        ],
        axis=0,
    )
    kernel_rows = lax.psum_scatter(kernel_term.T, "dp", scatter_dimension=0, tiled=True)
    weight_rows, kernel_rows = lax.psum((weight_rows, kernel_rows), "grp")
    return (outputs, weight_rows, kernel_rows.T, gamma_sum, beta_sum)


def fold(value):
    total = value[0:8]
    for at in range(8, value.shape[0], 8):
        total = total + value[at : at + 8]
    return total


def row_sum(value):
    return jnp.sum(value, axis=0, keepdims=True)


def conv_body(len_hbm, off_hbm, acts_hbm, k_hbm, gp_ref, cv_ref, st_ref, ok_ref, in_ref,
              acc_ref, len_ref, off_ref, acts_ref, k_ref, sems, slot_sems):
    slots, frames, wide = acts_ref.shape
    blocks, _, rows, _ = gp_ref.shape
    taps = k_ref.shape[0]
    lead = taps // 2
    small = [
        pltpu.make_async_copy(source, target, sems.at[i])
        for i, (source, target) in enumerate(((len_hbm, len_ref), (off_hbm, off_ref), (k_hbm, k_ref)))
    ]

    def fetch(slot):
        return pltpu.make_async_copy(acts_hbm.at[slot], acts_ref.at[slot], slot_sems.at[slot])

    small[0].start()
    small[1].start()
    fetch(0).start()
    small[2].start()
    for slot in range(1, slots):
        fetch(slot).start()
    acc_ref[...] = jnp.zeros_like(acc_ref)
    position = lax.broadcasted_iota(jnp.int32, (frames, LANES), 0)
    reach = lax.broadcasted_iota(jnp.int32, (taps, frames), 1)
    reach = reach - lax.broadcasted_iota(jnp.int32, (taps, frames), 0) + (lead - 1)
    for copy in small:
        copy.wait()

    def one(slot, carry):
        low = off_ref[slot]
        high = low + len_ref[slot]
        valid = ((position >= low) & (position < high)).astype(F32)
        ok_ref[slot] = valid
        in_ref[slot] = (
            (reach >= low) & (reach < high) & (reach >= 0) & (reach < frames)
        ).astype(F32)
        fetch(slot).wait()
        for block in range(blocks):
            cols = slice(block * LANES, (block + 1) * LANES)
            gate = slice(wide // 2 + block * LANES, wide // 2 + (block + 1) * LANES)
            left, right = acts_ref[slot, :, cols].astype(F32), acts_ref[slot, :, gate].astype(F32)
            gp_ref[block, slot, 0:lead, :] = jnp.zeros((lead, LANES), F32)
            gp_ref[block, slot, lead : lead + frames, :] = left * jax.nn.sigmoid(right) * valid
            tail = jnp.zeros((rows - lead - frames, LANES), F32)
            gp_ref[block, slot, lead + frames : rows, :] = tail
        for block in range(blocks):
            cols = slice(block * LANES, (block + 1) * LANES)
            total = gp_ref[block, slot, 1 : 1 + frames, :] * k_ref[0:1, cols]
            for tap in range(1, taps):
                lag = gp_ref[block, slot, 1 + tap : 1 + tap + frames, :]
                total = total + lag * k_ref[tap : tap + 1, cols]
            cv_ref[block, slot] = total
            masked = total * valid
            acc_ref[0, block] += fold(masked)
            acc_ref[1, block] += fold(masked * total)
        return carry

    lax.fori_loop(0, slots, one, 0)
    for block in range(blocks):
        cols = slice(block * LANES, (block + 1) * LANES)
        st_ref[0:1, cols] = row_sum(acc_ref[0, block])
        st_ref[1:2, cols] = row_sum(acc_ref[1, block])
    count = len_ref[0]
    for other in range(1, slots):
        count = count + len_ref[other]
    st_ref[:, blocks * LANES :] = jnp.full((2, LANES), count.astype(F32), F32)


def lag_sums(gp_ref, block, weights, taps, group, put):
    frames = weights(0).shape[0]
    slots = gp_ref.shape[1]
    for low in range(0, taps, group):
        sums = [None] * group
        for slot in range(slots):
            weight = weights(slot)
            for j in range(group):
                at = 1 + low + j
                term = fold(weight * gp_ref[block, slot, at : at + frames, :])
                sums[j] = term if sums[j] is None else sums[j] + term
        for j in range(group):
            put(low + j, row_sum(sums[j]))


def aux_body(start, ok_ref, in_ref, gp_ref, cv_ref, out_ref, wt_ref):
    _, slots, frames, _ = cv_ref.shape
    many, _, taps, _ = out_ref.shape
    lead = taps // 2

    def one(i, carry):
        block = start + i
        for slot in range(slots):
            wt_ref[slot] = cv_ref[block, slot] * ok_ref[slot]

        def put(k, row):
            out_ref[i, 0, k : k + 1, :] = row

        lag_sums(gp_ref, block, lambda slot: wt_ref[slot], taps, 16, put)
        total = jnp.zeros((taps, LANES), F32)
        for slot in range(slots):
            inside = in_ref[slot].astype(BF16)
            rest = gp_ref[block, slot, lead : lead + frames, :]
            for _ in range(3):
                part = rest.astype(BF16)
                rest = rest - part.astype(F32)
                total = total + jnp.dot(inside, part, preferred_element_type=F32)
        out_ref[i, 1] = total
        return carry

    lax.fori_loop(0, many, one, 0)


def scale_of(st_ref, block):
    width = st_ref.shape[1] - LANES
    cols = pl.ds(pl.multiple_of(block * LANES, LANES), LANES)
    count = st_ref[0:1, width:]
    mean = st_ref[0:1, cols] / count
    inv = lax.rsqrt(st_ref[1:2, cols] / count - mean * mean + 1e-05)
    return count, mean, inv


def hidden_body(st_ref, g_ref, b_ref, ok_ref, cv_ref, hid_ref):
    blocks, slots, frames, _ = cv_ref.shape

    def one(block, carry):
        _, mean, inv = scale_of(st_ref, block)
        gain, shift = g_ref[pl.ds(block, 1), :], b_ref[pl.ds(block, 1), :]
        for slot in range(slots):
            valid = ok_ref[slot]
            shifted = gain * ((cv_ref[block, slot] - mean) * inv) + shift
            hidden = shifted * jax.nn.sigmoid(shifted) * valid
            hid_ref[block, slot * frames : (slot + 1) * frames, :] = hidden.astype(BF16)
        return carry

    lax.fori_loop(0, blocks, one, 0)


def slope_body(st_ref, g_ref, b_ref, ok_ref, gp_ref, cv_ref, ct_ref, w_ref, *refs):
    aux_refs, q_ref, sl_ref = refs[:-2], refs[-2], refs[-1]
    blocks, slots, frames, _ = cv_ref.shape
    taps = aux_refs[0].shape[2]
    each = aux_refs[0].shape[0]
    last = 3 * taps

    def one(block, aux_ref, i):
        _, mean, inv = scale_of(st_ref, block)
        gain, shift = g_ref[pl.ds(block, 1), :], b_ref[pl.ds(block, 1), :]
        w_rows = w_ref[pl.ds(pl.multiple_of(block * LANES, LANES), LANES), :]
        backs = lax.dot_general(
            ct_ref[...], w_rows, (((1,), (1,)), ((), ())), preferred_element_type=F32
        )
        first = second = jnp.zeros((8, LANES), F32)
        for slot in range(slots):
            normed = (cv_ref[block, slot] - mean) * inv
            shifted = gain * normed + shift
            sig = jax.nn.sigmoid(shifted)
            back = backs[slot * frames : (slot + 1) * frames, :]
            slope = back * sig * (1.0 + shifted * (1.0 - sig)) * ok_ref[slot]
            sl_ref[slot] = slope
            first, second = first + fold(slope), second + fold(slope * normed)

        def put(k, row):
            q_ref[block, k : k + 1, :] = row

        lag_sums(gp_ref, block, lambda slot: sl_ref[slot], taps, 16, put)
        q_ref[block, taps : 2 * taps, :] = aux_ref[i, 1]
        q_ref[block, 2 * taps : last, :] = inv * (aux_ref[i, 0] - mean * aux_ref[i, 1])
        q_ref[0, pl.ds(last + block, 1), :] = row_sum(first)
        q_ref[0, pl.ds(last + blocks + block, 1), :] = row_sum(second)

    for part, aux_ref in enumerate(aux_refs):

        def step(i, carry, part=part, aux_ref=aux_ref):
            one(part * each + i, aux_ref, i)
            return carry

        lax.fori_loop(0, each, step, 0)
    for block in range(1, blocks):
        q_ref[block, last:, :] = q_ref[0, last:, :]


def out_body(hid_ref, w_ref, out_ref):
    blocks = hid_ref.shape[0]
    slots, frames, _ = out_ref.shape
    total = None
    for block in range(blocks):
        term = jnp.dot(
            hid_ref[block],
            w_ref[block * LANES : (block + 1) * LANES, :],
            preferred_element_type=F32,
        )
        total = term if total is None else total + term
    for slot in range(slots):
        out_ref[slot] = total[slot * frames : (slot + 1) * frames, :].astype(BF16)


def rows_body(masks, flip, at_ref, recv_ref, *refs):
    pieces, (out_ref, held, sems) = refs[:-3], refs[-3:]
    me = at_ref[0]
    half = 1 - at_ref[1] if flip else at_ref[1]
    width = held.shape[2]
    cols = pl.ds(pl.multiple_of(half * width, width), width)
    copies = [
        pltpu.make_async_copy(piece.at[:, cols], held.at[i], sems.at[i])
        for i, piece in enumerate(pieces)
    ]
    for copy in copies:
        copy.start()
    total = None
    for i, mask in enumerate(masks):
        left = recv_ref[jnp.bitwise_xor(me, mask)]
        copies[i].wait()
        term = lax.dot_general(
            left, held[i], (((0,), (0,)), ((), ())), preferred_element_type=F32
        )
        total = term if total is None else total + term
    for block in range(width // LANES):
        out_ref[block] = total[:, block * LANES : (block + 1) * LANES].astype(BF16)


def put_pair(ref, at, value):
    rows = value.shape[0]
    lead = value.astype(BF16)
    ref[at : at + rows, :] = lead
    ref[at + rows : at + 2 * rows, :] = (value - lead.astype(F32)).astype(BF16)


def get_pair(ref, at, rows):
    return ref[at : at + rows, :].astype(F32) + ref[at + rows : at + 2 * rows, :].astype(F32)


def join_body(own_ref, recv_ref, lags_ref, out_ref):
    many = own_ref.shape[0]
    for block in range(many):
        rows = slice(block * LANES, (block + 1) * LANES)
        out_ref[rows, :] = (own_ref[block].astype(F32) + recv_ref[block].astype(F32)).astype(BF16)
    total = lags_ref[0]
    for source in range(1, lags_ref.shape[0]):
        total = total + lags_ref[source]
    put_pair(out_ref, many * LANES, total)


def add_body(n_w, own_ref, recv_ref, out_ref):
    n_q = (own_ref.shape[0] - n_w) // 2
    out_ref[0:n_w, :] = (own_ref[0:n_w, :].astype(F32) + recv_ref[0:n_w, :].astype(F32)).astype(BF16)
    put_pair(out_ref, n_w, get_pair(own_ref, n_w, n_q) + get_pair(recv_ref, n_w, n_q))


def last_body(n_w, taps, at_ref, own_ref, recv_ref, st_ref, g_ref, rows_ref, gk_ref, gg_ref, gb_ref):
    me, half = at_ref[0], at_ref[1]
    many = n_w // LANES
    for which, ref in ((half, own_ref), (1 - half, recv_ref)):
        for block in range(many):
            cols = pl.ds(pl.multiple_of((which * many + block) * LANES, LANES), LANES)
            rows_ref[:, cols] = ref[block * LANES : (block + 1) * LANES, :].astype(F32)
    n_q = (own_ref.shape[0] - n_w) // 2
    value = get_pair(own_ref, n_w, n_q) + get_pair(recv_ref, n_w, n_q)
    blocks = g_ref.shape[0]
    gb_ref[...] = value[3 * taps : 3 * taps + blocks]
    gg_ref[...] = value[3 * taps + blocks : 3 * taps + 2 * blocks]
    count, _, inv = scale_of(st_ref, me)
    mine = pl.ds(me, 1)
    gk_ref[...] = (g_ref[mine, :] * inv) * (
        value[0:taps]
        - (gb_ref[mine, :] / count) * value[taps : 2 * taps]
        - (gg_ref[mine, :] / count) * value[2 * taps : 3 * taps]
    )


SMEM = pl.BlockSpec(memory_space=pltpu.SMEM)
VMEM = pl.BlockSpec(memory_space=pltpu.VMEM)
HBM = pl.BlockSpec(memory_space=pltpu.HBM)
ANY = pl.BlockSpec(memory_space=pl.ANY)


def in_hbm(value):
    return pltpu.with_memory_space_constraint(value, pltpu.HBM)


def call(body, shapes, scalars, args, flops=0, scratch=(), mib=8, **more):
    many = isinstance(shapes, list)
    moved = sum(a.size * a.dtype.itemsize for a in args)
    return pl.pallas_call(
        body,
        in_specs=more.pop("in_specs", None) or [SMEM] * len(scalars) + [VMEM] * len(args),
        out_specs=[VMEM] * len(shapes) if many else VMEM,
        out_shape=shapes,
        scratch_shapes=scratch,
        compiler_params=pltpu.CompilerParams(vmem_limit_bytes=mib << 20),
        cost_estimate=pl.CostEstimate(flops=flops, bytes_accessed=moved, transcendentals=0),
        **more,
    )(*scalars, *args)


def local_fast(n_dp, n_grp, acts, cotan, lengths, offsets, kernel, gamma, beta, w_out):
    slots, frames, wide = acts.shape
    width = wide // 2
    taps = kernel.shape[0]
    blocks = width // LANES
    tokens = slots * frames
    n_q = 3 * taps + 2 * blocks
    padded = 2 * (taps // 2) + frames
    me_dp, me_grp = lax.axis_index("dp"), lax.axis_index("grp")
    shape = jax.ShapeDtypeStruct

    def swap(value, dp_mask, grp_mask):
        pairs = [
            (d * n_grp + g, (d ^ dp_mask) * n_grp + (g ^ grp_mask))
            for d in range(n_dp)
            for g in range(n_grp)
        ]
        return lax.ppermute(value, ("dp", "grp"), pairs)

    dp_bits = [1 << i for i in range(n_dp.bit_length() - 1)]
    grp_bits = [1 << i for i in range(n_grp.bit_length() - 1)]
    at = jnp.stack([me_dp, me_grp % 2]).astype(jnp.int32)
    gamma2, beta2 = gamma.reshape(blocks, LANES), beta.reshape(blocks, LANES)

    flat_cotan = cotan.reshape(tokens, width)
    pieces = [(0, flat_cotan)]
    for bit in dp_bits[1:] + dp_bits[:1]:
        pieces += [(m | bit, swap(v, bit, 0)) for m, v in pieces]
    masks, values = tuple(m for m, _ in pieces), [v for _, v in pieces]

    gated, conv_out, stats, valid, inside = call(
        conv_body,
        [
            shape((blocks, slots, padded, LANES), F32),
            shape((blocks, slots, frames, LANES), F32),
            shape((2, width + LANES), F32),
            shape((slots, frames, LANES), F32),
            shape((slots, taps, frames), F32),
        ],
        (),
        [in_hbm(value) for value in (lengths, offsets, acts, kernel)],
        flops=4 * taps * tokens * width,
        scratch=[
            pltpu.VMEM((2, blocks, 8, LANES), F32),
            pltpu.SMEM((slots,), jnp.int32),
            pltpu.SMEM((slots,), jnp.int32),
            pltpu.VMEM(acts.shape, BF16),
            pltpu.VMEM(kernel.shape, F32),
            pltpu.SemaphoreType.DMA((3,)),
            pltpu.SemaphoreType.DMA((slots,)),
        ],
        in_specs=[HBM] * 4,
    )

    hops = [(1, m) for m in grp_bits] + [(m | 1, 0) for m in dp_bits[1:]] + [(1, 0)]
    for dp_mask, grp_mask in hops:
        stats = stats + swap(stats, dp_mask, grp_mask)

    parts = 4
    each = blocks // parts
    aux = [
        call(
            functools.partial(aux_body, i * each),
            shape((each, 2, taps, LANES), F32),
            (),
            (valid, inside, gated, conv_out),
            flops=4 * taps * tokens * each * LANES,
            scratch=[pltpu.VMEM((slots, frames, LANES), F32)],
        )
        for i in range(parts)
    ]

    hidden = call(
        hidden_body,
        shape((blocks, tokens, LANES), BF16),
        (),
        (stats, gamma2, beta2, valid, conv_out),
    )
    received = lax.all_to_all(hidden, "dp", 0, 0, tiled=True)
    lags = call(
        slope_body,
        shape((blocks, n_q, LANES), F32),
        (),
        (stats, gamma2, beta2, valid, gated, conv_out, flat_cotan, w_out, *aux),
        flops=4 * taps * tokens * width + 2 * tokens * width * width,
        scratch=[pltpu.VMEM((slots, frames, LANES), F32)],
    )
    lags = lax.all_to_all(lags, "dp", 0, 0, tiled=True)
    outputs = call(out_body, shape(cotan.shape, BF16), (), (hidden, w_out))

    half_shape = shape((blocks // 2, LANES, LANES), BF16)
    flops = n_dp * tokens * LANES * width
    n_w = blocks // 2 * LANES

    def rows_of(flip):
        body = functools.partial(rows_body, masks, flip)
        return call(
            body,
            half_shape,
            (at,),
            (received, *values),
            flops=flops,
            scratch=[
                pltpu.VMEM((n_dp, tokens, width // 2), BF16),
                pltpu.SemaphoreType.DMA((n_dp,)),
            ],
            in_specs=[SMEM, VMEM] + [ANY] * n_dp,
        )

    given = rows_of(True)
    taken = swap(given, 0, 1)
    kept = rows_of(False)
    both_shape = shape((n_w + 2 * n_q, LANES), BF16)
    both = call(join_body, both_shape, (), (kept, taken, lags))
    for mask in grp_bits[1:]:
        other = swap(both, 0, mask)
        both = call(functools.partial(add_body, n_w), both_shape, (), (both, other))
    rest = swap(both, 0, 1)
    weight_rows, grad_kernel, gamma_sum, beta_sum = call(
        functools.partial(last_body, n_w, taps),
        [
            shape((LANES, width), F32),
            shape((taps, LANES), F32),
            shape((blocks, LANES), F32),
            shape((blocks, LANES), F32),
        ],
        (at,),
        (both, rest, stats, gamma2),
    )
    return (outputs, weight_rows, grad_kernel, gamma_sum.reshape(width), beta_sum.reshape(width))


def solution(mesh):
    n_dp, n_grp = mesh.shape["dp"], mesh.shape["grp"]

    def fits(width, taps, frames):
        return (
            n_dp & (n_dp - 1) == 0
            and n_grp & (n_grp - 1) == 0
            and n_dp >= 4
            and n_grp >= 4
            and width == n_dp * LANES
            and taps % 16 == 0
            and frames % 16 == 0
            and n_dp % 8 == 0
        )

    def local(acts, cotan, lengths, offsets, kernel, gamma, beta, w_out):
        args = (acts, cotan, lengths, offsets, kernel, gamma, beta, w_out)
        if not fits(w_out.shape[0], kernel.shape[0], acts.shape[1]):
            return local_general(*args)
        return local_fast(n_dp, n_grp, *args)

    placed = (
        P(("dp", "grp"), None, None),
        P(("dp", "grp"), None, None),
        P(("dp", "grp")),
        P(("dp", "grp")),
        P(),
        P(),
        P(),
        P(),
    )
    return jax.shard_map(
        local,
        mesh=mesh,
        in_specs=placed,
        out_specs=(P(("dp", "grp"), None, None), P("dp", None), P(None, "dp"), P(), P()),
        check_vma=False,
    )
```

```python
import functools

import jax
import jax.numpy as jnp
from jax import lax
from jax.experimental import pallas as pl
from jax.experimental.pallas import tpu as pltpu
from jax.sharding import PartitionSpec as P


LANES = 128
F32 = jnp.float32
BF16 = jnp.bfloat16


def convolve(block_acts, block_len, block_off, kernel):
    taps = kernel.shape[0]
    model_width = kernel.shape[1]
    frame_count = block_acts.shape[1]
    position = jnp.arange(frame_count, dtype=jnp.int32)
    valid = (
        (position[None, :] >= block_off[:, None])
        & (position[None, :] < (block_off + block_len)[:, None])
    ).astype(jnp.float32)
    wide_acts = block_acts.astype(jnp.float32)
    gated = (
        wide_acts[..., :model_width]
        * jax.nn.sigmoid(wide_acts[..., model_width:])
        * valid[..., None]
    )
    padded = jnp.pad(gated, ((0, 0), (taps // 2 - 1, taps // 2), (0, 0)))
    conv_out = padded[:, 0:frame_count] * kernel[0]
    for tap in range(1, taps):
        conv_out = conv_out + padded[:, tap : tap + frame_count] * kernel[tap]
    return (valid, padded, conv_out)


def local_general(acts, cotan, lengths, offsets, kernel, gamma, beta, w_out):
    model_width = w_out.shape[0]
    taps = kernel.shape[0]
    valid, padded, conv_out = convolve(acts, lengths, offsets, kernel)
    masked = conv_out * valid[..., None]
    sum_first, sum_second, frame_total = lax.psum(
        (
            jnp.sum(masked, axis=(0, 1)),
            jnp.sum(masked * conv_out, axis=(0, 1)),
            jnp.sum(lengths).astype(jnp.float32),
        ),
        ("dp", "grp"),
    )
    mean_value = sum_first / frame_total
    inv_std = lax.rsqrt(sum_second / frame_total - mean_value * mean_value + 1e-05)
    normed = (conv_out - mean_value) * inv_std
    shifted = gamma * normed + beta
    sig_value = jax.nn.sigmoid(shifted)
    hidden = (shifted * sig_value * valid[..., None]).astype(jnp.bfloat16)
    flat_hidden = hidden.reshape(-1, model_width)
    flat_cotan = cotan.reshape(-1, model_width)
    outputs = (
        jnp.dot(flat_hidden, w_out, preferred_element_type=jnp.float32)
        .astype(jnp.bfloat16)
        .reshape(cotan.shape)
    )
    weight_rows = lax.psum_scatter(
        lax.dot_general(
            flat_hidden, flat_cotan, (((0,), (0,)), ((), ())), preferred_element_type=jnp.float32
        ),
        "dp",
        scatter_dimension=0,
        tiled=True,
    )
    back_hidden = lax.dot_general(
        flat_cotan, w_out, (((1,), (1,)), ((), ())), preferred_element_type=jnp.float32
    ).reshape(conv_out.shape)
    slope = back_hidden * sig_value * (1.0 + shifted * (1.0 - sig_value)) * valid[..., None]
    beta_sum, gamma_sum = lax.psum(
        (jnp.sum(slope, axis=(0, 1)), jnp.sum(slope * normed, axis=(0, 1))), ("dp", "grp")
    )
    conv_grad = (
        gamma
        * inv_std
        * (slope - beta_sum / frame_total - normed * gamma_sum / frame_total)
        * valid[..., None]
    )
    frame_count = conv_out.shape[1]
    kernel_term = jnp.stack(
        [
            jnp.sum(conv_grad * padded[:, tap : tap + frame_count], axis=(0, 1))
            for tap in range(taps)
        ],
        axis=0,
    )
    kernel_rows = lax.psum_scatter(kernel_term.T, "dp", scatter_dimension=0, tiled=True)
    weight_rows, kernel_rows = lax.psum((weight_rows, kernel_rows), "grp")
    return (outputs, weight_rows, kernel_rows.T, gamma_sum, beta_sum)


def fold(value):
    total = value[0:8]
    for at in range(8, value.shape[0], 8):
        total = total + value[at : at + 8]
    return total


def row_sum(value):
    return jnp.sum(value, axis=0, keepdims=True)


def conv_body(len_hbm, off_hbm, acts_hbm, k_hbm, g_hbm, b_hbm, gp_ref, cv_ref, st_ref, ok_ref, in_ref, gb_ref,
              acc_ref, len_ref, off_ref, acts_ref, k_ref, sems, slot_sems):
    slots, frames, wide = acts_ref.shape
    blocks, _, rows, _ = gp_ref.shape
    taps = k_ref.shape[0]
    lead = taps // 2
    small = [
        pltpu.make_async_copy(source, target, sems.at[i])
        for i, (source, target) in enumerate(
            (
                (len_hbm, len_ref),
                (off_hbm, off_ref),
                (k_hbm, k_ref),
                (g_hbm, gb_ref.at[0]),
                (b_hbm, gb_ref.at[1]),
            )
        )
    ]

    def fetch(slot):
        return pltpu.make_async_copy(acts_hbm.at[slot], acts_ref.at[slot], slot_sems.at[slot])

    small[0].start()
    small[1].start()
    fetch(0).start()
    small[2].start()
    for slot in range(1, slots):
        fetch(slot).start()
    small[3].start()
    small[4].start()
    acc_ref[...] = jnp.zeros_like(acc_ref)
    position = lax.broadcasted_iota(jnp.int32, (frames, LANES), 0)
    reach = lax.broadcasted_iota(jnp.int32, (taps, frames), 1)
    reach = reach - lax.broadcasted_iota(jnp.int32, (taps, frames), 0) + (lead - 1)
    for copy in small[:3]:
        copy.wait()

    def one(slot, carry):
        low = off_ref[slot]
        high = low + len_ref[slot]
        valid = ((position >= low) & (position < high)).astype(F32)
        ok_ref[slot] = valid
        in_ref[slot] = (
            (reach >= low) & (reach < high) & (reach >= 0) & (reach < frames)
        ).astype(F32)
        fetch(slot).wait()
        for block in range(blocks):
            cols = slice(block * LANES, (block + 1) * LANES)
            gate = slice(wide // 2 + block * LANES, wide // 2 + (block + 1) * LANES)
            left, right = acts_ref[slot, :, cols].astype(F32), acts_ref[slot, :, gate].astype(F32)
            gp_ref[block, slot, 0:lead, :] = jnp.zeros((lead, LANES), F32)
            gp_ref[block, slot, lead : lead + frames, :] = left * jax.nn.sigmoid(right) * valid
            tail = jnp.zeros((rows - lead - frames, LANES), F32)
            gp_ref[block, slot, lead + frames : rows, :] = tail
        for block in range(blocks):
            cols = slice(block * LANES, (block + 1) * LANES)
            total = gp_ref[block, slot, 1 : 1 + frames, :] * k_ref[0:1, cols]
            for tap in range(1, taps):
                lag = gp_ref[block, slot, 1 + tap : 1 + tap + frames, :]
                total = total + lag * k_ref[tap : tap + 1, cols]
            cv_ref[block, slot] = total
            masked = total * valid
            acc_ref[0, block] += fold(masked)
            acc_ref[1, block] += fold(masked * total)
        return carry

    lax.fori_loop(0, slots, one, 0)
    small[3].wait()
    small[4].wait()
    for block in range(blocks):
        cols = slice(block * LANES, (block + 1) * LANES)
        st_ref[0:1, cols] = row_sum(acc_ref[0, block])
        st_ref[1:2, cols] = row_sum(acc_ref[1, block])
    count = len_ref[0]
    for other in range(1, slots):
        count = count + len_ref[other]
    st_ref[:, blocks * LANES :] = jnp.full((2, LANES), count.astype(F32), F32)


def lag_sums(gp_ref, block, weights, taps, group, put):
    frames = weights(0).shape[0]
    slots = gp_ref.shape[1]
    for low in range(0, taps, group):
        sums = [None] * group
        for slot in range(slots):
            weight = weights(slot)
            for j in range(group):
                at = 1 + low + j
                term = fold(weight * gp_ref[block, slot, at : at + frames, :])
                sums[j] = term if sums[j] is None else sums[j] + term
        for j in range(group):
            put(low + j, row_sum(sums[j]))


def aux_body(start, ok_ref, in_ref, gp_ref, cv_ref, out_ref, wt_ref):
    _, slots, frames, _ = cv_ref.shape
    many, _, taps, _ = out_ref.shape
    lead = taps // 2

    def one(i, carry):
        block = start + i
        for slot in range(slots):
            wt_ref[slot] = cv_ref[block, slot] * ok_ref[slot]

        def put(k, row):
            out_ref[i, 0, k : k + 1, :] = row

        lag_sums(gp_ref, block, lambda slot: wt_ref[slot], taps, 16, put)
        total = jnp.zeros((taps, LANES), F32)
        for slot in range(slots):
            inside = in_ref[slot].astype(BF16)
            rest = gp_ref[block, slot, lead : lead + frames, :]
            for _ in range(3):
                part = rest.astype(BF16)
                rest = rest - part.astype(F32)
                total = total + jnp.dot(inside, part, preferred_element_type=F32)
        out_ref[i, 1] = total
        return carry

    lax.fori_loop(0, many, one, 0)


def back_body(cotan_ref, w_ref, out_ref):
    for block in range(out_ref.shape[0]):
        rows = w_ref[block * LANES : (block + 1) * LANES, :]
        out_ref[block] = lax.dot_general(
            cotan_ref[...], rows, (((1,), (1,)), ((), ())), preferred_element_type=F32
        )


def scale_of(st_ref, block):
    width = st_ref.shape[1] - LANES
    cols = pl.ds(pl.multiple_of(block * LANES, LANES), LANES)
    count = st_ref[0:1, width:]
    mean = st_ref[0:1, cols] / count
    inv = lax.rsqrt(st_ref[1:2, cols] / count - mean * mean + 1e-05)
    return count, mean, inv


def hidden_body(st_ref, gb_ref, ok_ref, cv_ref, hid_ref):
    blocks, slots, frames, _ = cv_ref.shape

    def one(block, carry):
        _, mean, inv = scale_of(st_ref, block)
        gain, shift = gb_ref[0, pl.ds(block, 1), :], gb_ref[1, pl.ds(block, 1), :]
        for slot in range(slots):
            valid = ok_ref[slot]
            shifted = gain * ((cv_ref[block, slot] - mean) * inv) + shift
            hidden = shifted * jax.nn.sigmoid(shifted) * valid
            hid_ref[block, slot * frames : (slot + 1) * frames, :] = hidden.astype(BF16)
        return carry

    lax.fori_loop(0, blocks, one, 0)


def slope_body(st_ref, gb_ref, ok_ref, gp_ref, cv_ref, bk_ref, *refs):
    aux_refs, q_ref, sl_ref = refs[:-2], refs[-2], refs[-1]
    blocks, slots, frames, _ = cv_ref.shape
    taps = aux_refs[0].shape[2]
    each = aux_refs[0].shape[0]
    last = 3 * taps

    def one(block, aux_ref, i):
        _, mean, inv = scale_of(st_ref, block)
        gain, shift = gb_ref[0, pl.ds(block, 1), :], gb_ref[1, pl.ds(block, 1), :]
        first = second = jnp.zeros((8, LANES), F32)
        for slot in range(slots):
            normed = (cv_ref[block, slot] - mean) * inv
            shifted = gain * normed + shift
            sig = jax.nn.sigmoid(shifted)
            back = bk_ref[block, slot * frames : (slot + 1) * frames, :]
            slope = back * sig * (1.0 + shifted * (1.0 - sig)) * ok_ref[slot]
            sl_ref[slot] = slope
            first, second = first + fold(slope), second + fold(slope * normed)

        def put(k, row):
            q_ref[block, k : k + 1, :] = row

        lag_sums(gp_ref, block, lambda slot: sl_ref[slot], taps, 16, put)
        q_ref[block, taps : 2 * taps, :] = aux_ref[i, 1]
        q_ref[block, 2 * taps : last, :] = inv * (aux_ref[i, 0] - mean * aux_ref[i, 1])
        q_ref[0, pl.ds(last + block, 1), :] = row_sum(first)
        q_ref[0, pl.ds(last + blocks + block, 1), :] = row_sum(second)

    for part, aux_ref in enumerate(aux_refs):

        def step(i, carry, part=part, aux_ref=aux_ref):
            one(part * each + i, aux_ref, i)
            return carry

        lax.fori_loop(0, each, step, 0)
    for block in range(1, blocks):
        q_ref[block, last:, :] = q_ref[0, last:, :]


def out_body(hid_ref, w_ref, out_ref):
    blocks = hid_ref.shape[0]
    slots, frames, _ = out_ref.shape
    total = None
    for block in range(blocks):
        term = jnp.dot(
            hid_ref[block],
            w_ref[block * LANES : (block + 1) * LANES, :],
            preferred_element_type=F32,
        )
        total = term if total is None else total + term
    for slot in range(slots):
        out_ref[slot] = total[slot * frames : (slot + 1) * frames, :].astype(BF16)


def rows_body(masks, at_ref, recv_ref, *refs):
    pieces, (give_ref, keep_ref, held, sems) = refs[:-4], refs[-4:]
    me, half = at_ref[0], at_ref[1]
    copies = [
        pltpu.make_async_copy(piece, held.at[i], sems.at[i]) for i, piece in enumerate(pieces)
    ]
    for copy in copies:
        copy.start()
    many = give_ref.shape[0]
    width = many * LANES
    give = pl.ds(pl.multiple_of((1 - half) * width, width), width)
    keep = pl.ds(pl.multiple_of(half * width, width), width)
    totals = [None, None]
    for i, mask in enumerate(masks):
        left = recv_ref[jnp.bitwise_xor(me, mask)]
        copies[i].wait()
        for j, cols in enumerate((give, keep)):
            term = lax.dot_general(
                left, held[i, :, cols], (((0,), (0,)), ((), ())), preferred_element_type=F32
            )
            totals[j] = term if totals[j] is None else totals[j] + term
    for total, ref in zip(totals, (give_ref, keep_ref)):
        for block in range(many):
            ref[block] = total[:, block * LANES : (block + 1) * LANES].astype(BF16)


def add_body(own_ref, recv_ref, out_ref):
    out_ref[...] = (own_ref[...].astype(F32) + recv_ref[...].astype(F32)).astype(BF16)


def sum_body(lags_ref, out_ref):
    total = lags_ref[0]
    for source in range(1, lags_ref.shape[0]):
        total = total + lags_ref[source]
    out_ref[...] = total


def scale_body(at_ref, st_ref, gb_ref, out_ref):
    me = at_ref[0]
    count, _, inv = scale_of(st_ref, me)
    out_ref[0:1, :] = gb_ref[0, pl.ds(me, 1), :] * inv
    out_ref[1:2, :] = count


def last_body(taps, at_ref, own_ref, recv_ref, lags_ref, more_ref, sc_ref, rows_ref, gk_ref, gg_ref, gb_ref):
    me, half = at_ref[0], at_ref[1]
    many = own_ref.shape[0]
    for which, ref in ((half, own_ref), (1 - half, recv_ref)):
        for block in range(many):
            cols = pl.ds(pl.multiple_of((which * many + block) * LANES, LANES), LANES)
            rows_ref[:, cols] = ref[block].astype(F32)
    value = lags_ref[...] + more_ref[...]
    blocks = gb_ref.shape[0]
    gb_ref[...] = value[3 * taps : 3 * taps + blocks]
    gg_ref[...] = value[3 * taps + blocks : 3 * taps + 2 * blocks]
    count = sc_ref[1:2, :]
    mine = pl.ds(me, 1)
    gk_ref[...] = sc_ref[0:1, :] * (
        value[0:taps]
        - (gb_ref[mine, :] / count) * value[taps : 2 * taps]
        - (gg_ref[mine, :] / count) * value[2 * taps : 3 * taps]
    )


SMEM = pl.BlockSpec(memory_space=pltpu.SMEM)
VMEM = pl.BlockSpec(memory_space=pltpu.VMEM)
HBM = pl.BlockSpec(memory_space=pltpu.HBM)
ANY = pl.BlockSpec(memory_space=pl.ANY)


def in_hbm(value):
    return pltpu.with_memory_space_constraint(value, pltpu.HBM)


def call(body, shapes, scalars, args, flops=0, scratch=(), mib=8, **more):
    many = isinstance(shapes, list)
    moved = sum(a.size * a.dtype.itemsize for a in args)
    return pl.pallas_call(
        body,
        in_specs=more.pop("in_specs", None) or [SMEM] * len(scalars) + [VMEM] * len(args),
        out_specs=[VMEM] * len(shapes) if many else VMEM,
        out_shape=shapes,
        scratch_shapes=scratch,
        compiler_params=pltpu.CompilerParams(vmem_limit_bytes=mib << 20),
        cost_estimate=pl.CostEstimate(flops=flops, bytes_accessed=moved, transcendentals=0),
        **more,
    )(*scalars, *args)


def local_fast(n_dp, n_grp, acts, cotan, lengths, offsets, kernel, gamma, beta, w_out):
    slots, frames, wide = acts.shape
    width = wide // 2
    taps = kernel.shape[0]
    blocks = width // LANES
    tokens = slots * frames
    n_q = 3 * taps + 2 * blocks
    padded = 2 * (taps // 2) + frames
    me_dp, me_grp = lax.axis_index("dp"), lax.axis_index("grp")
    shape = jax.ShapeDtypeStruct

    def swap(value, dp_mask, grp_mask):
        pairs = [
            (d * n_grp + g, (d ^ dp_mask) * n_grp + (g ^ grp_mask))
            for d in range(n_dp)
            for g in range(n_grp)
        ]
        return lax.ppermute(value, ("dp", "grp"), pairs)

    dp_bits = [1 << i for i in range(n_dp.bit_length() - 1)]
    grp_bits = [1 << i for i in range(n_grp.bit_length() - 1)]
    at = jnp.stack([me_dp, me_grp % 2]).astype(jnp.int32)
    gamma2, beta2 = gamma.reshape(blocks, LANES), beta.reshape(blocks, LANES)

    flat_cotan = cotan.reshape(tokens, width)
    pieces = [(0, flat_cotan)]
    for bit in dp_bits[1:] + dp_bits[:1]:
        pieces += [(m | bit, swap(v, bit, 0)) for m, v in pieces]
    masks, values = tuple(m for m, _ in pieces), [v for _, v in pieces]

    gated, conv_out, stats, valid, inside, gains = call(
        conv_body,
        [
            shape((blocks, slots, padded, LANES), F32),
            shape((blocks, slots, frames, LANES), F32),
            shape((2, width + LANES), F32),
            shape((slots, frames, LANES), F32),
            shape((slots, taps, frames), F32),
            shape((2, blocks, LANES), F32),
        ],
        (),
        [in_hbm(value) for value in (lengths, offsets, acts, kernel, gamma2, beta2)],
        flops=4 * taps * tokens * width,
        scratch=[
            pltpu.VMEM((2, blocks, 8, LANES), F32),
            pltpu.SMEM((slots,), jnp.int32),
            pltpu.SMEM((slots,), jnp.int32),
            pltpu.VMEM(acts.shape, BF16),
            pltpu.VMEM(kernel.shape, F32),
            pltpu.SemaphoreType.DMA((5,)),
            pltpu.SemaphoreType.DMA((slots,)),
        ],
        in_specs=[HBM] * 6,
    )

    hops = [(m | 1, 0) for m in dp_bits[1:]] + [(1, m) for m in grp_bits] + [(1, 0)]
    for dp_mask, grp_mask in hops:
        stats = stats + swap(stats, dp_mask, grp_mask)

    back = call(
        back_body,
        shape((blocks, tokens, LANES), F32),
        (),
        (flat_cotan, w_out),
        flops=2 * tokens * width * width,
    )
    parts = 4
    each = blocks // parts
    aux = [
        call(
            functools.partial(aux_body, i * each),
            shape((each, 2, taps, LANES), F32),
            (),
            (valid, inside, gated, conv_out),
            flops=4 * taps * tokens * each * LANES,
            scratch=[pltpu.VMEM((slots, frames, LANES), F32)],
        )
        for i in range(parts)
    ]

    hidden = call(
        hidden_body, shape((blocks, tokens, LANES), BF16), (), (stats, gains, valid, conv_out)
    )
    received = lax.all_to_all(hidden, "dp", 0, 0, tiled=True)
    lags = call(
        slope_body,
        shape((blocks, n_q, LANES), F32),
        (),
        (stats, gains, valid, gated, conv_out, back, *aux),
        flops=4 * taps * tokens * width,
        scratch=[pltpu.VMEM((slots, frames, LANES), F32)],
    )
    lags = lax.all_to_all(lags, "dp", 0, 0, tiled=True)
    scale = call(scale_body, shape((2, LANES), F32), (at,), (stats, gains))
    outputs = call(out_body, shape(cotan.shape, BF16), (), (hidden, w_out))

    half_shape = shape((blocks // 2, LANES, LANES), BF16)
    given, kept = call(
        functools.partial(rows_body, masks),
        [half_shape] * 2,
        (at,),
        (received, *values),
        flops=2 * n_dp * tokens * LANES * width,
        scratch=[
            pltpu.VMEM((n_dp, tokens, width), BF16),
            pltpu.SemaphoreType.DMA((n_dp,)),
        ],
        in_specs=[SMEM, VMEM] + [ANY] * n_dp,
    )
    taken = swap(given, 0, 1)
    both = call(add_body, half_shape, (), (kept, taken))
    for mask in grp_bits[1:]:
        other = swap(both, 0, mask)
        both = call(add_body, half_shape, (), (both, other))
    rest = swap(both, 0, 1)

    lags = call(sum_body, shape((n_q, LANES), F32), (), (lags,))
    for mask in grp_bits[1:]:
        lags = lags + swap(lags, 0, mask)
    more = swap(lags, 0, 1)
    weight_rows, grad_kernel, gamma_sum, beta_sum = call(
        functools.partial(last_body, taps),
        [
            shape((LANES, width), F32),
            shape((taps, LANES), F32),
            shape((blocks, LANES), F32),
            shape((blocks, LANES), F32),
        ],
        (at,),
        (both, rest, lags, more, scale),
    )
    return (outputs, weight_rows, grad_kernel, gamma_sum.reshape(width), beta_sum.reshape(width))


def solution(mesh):
    n_dp, n_grp = mesh.shape["dp"], mesh.shape["grp"]

    def fits(width, taps, frames):
        return (
            n_dp & (n_dp - 1) == 0
            and n_grp & (n_grp - 1) == 0
            and n_dp >= 4
            and n_grp >= 4
            and width == n_dp * LANES
            and taps % 16 == 0
            and frames % 16 == 0
            and n_dp % 8 == 0
        )

    def local(acts, cotan, lengths, offsets, kernel, gamma, beta, w_out):
        args = (acts, cotan, lengths, offsets, kernel, gamma, beta, w_out)
        if not fits(w_out.shape[0], kernel.shape[0], acts.shape[1]):
            return local_general(*args)
        return local_fast(n_dp, n_grp, *args)

    placed = (
        P(("dp", "grp"), None, None),
        P(("dp", "grp"), None, None),
        P(("dp", "grp")),
        P(("dp", "grp")),
        P(),
        P(),
        P(),
        P(),
    )
    return jax.shard_map(
        local,
        mesh=mesh,
        in_specs=placed,
        out_specs=(P(("dp", "grp"), None, None), P("dp", None), P(None, "dp"), P(), P()),
        check_vma=False,
    )
```

```python
import functools

import jax
import jax.numpy as jnp
from jax import lax
from jax.experimental import pallas as pl
from jax.experimental.pallas import tpu as pltpu
from jax.sharding import PartitionSpec as P


LANES = 128
F32 = jnp.float32
BF16 = jnp.bfloat16


def convolve(block_acts, block_len, block_off, kernel):
    taps = kernel.shape[0]
    model_width = kernel.shape[1]
    frame_count = block_acts.shape[1]
    position = jnp.arange(frame_count, dtype=jnp.int32)
    valid = (
        (position[None, :] >= block_off[:, None])
        & (position[None, :] < (block_off + block_len)[:, None])
    ).astype(jnp.float32)
    wide_acts = block_acts.astype(jnp.float32)
    gated = (
        wide_acts[..., :model_width]
        * jax.nn.sigmoid(wide_acts[..., model_width:])
        * valid[..., None]
    )
    padded = jnp.pad(gated, ((0, 0), (taps // 2 - 1, taps // 2), (0, 0)))
    conv_out = padded[:, 0:frame_count] * kernel[0]
    for tap in range(1, taps):
        conv_out = conv_out + padded[:, tap : tap + frame_count] * kernel[tap]
    return (valid, padded, conv_out)


def local_general(acts, cotan, lengths, offsets, kernel, gamma, beta, w_out):
    model_width = w_out.shape[0]
    taps = kernel.shape[0]
    valid, padded, conv_out = convolve(acts, lengths, offsets, kernel)
    masked = conv_out * valid[..., None]
    sum_first, sum_second, frame_total = lax.psum(
        (
            jnp.sum(masked, axis=(0, 1)),
            jnp.sum(masked * conv_out, axis=(0, 1)),
            jnp.sum(lengths).astype(jnp.float32),
        ),
        ("dp", "grp"),
    )
    mean_value = sum_first / frame_total
    inv_std = lax.rsqrt(sum_second / frame_total - mean_value * mean_value + 1e-05)
    normed = (conv_out - mean_value) * inv_std
    shifted = gamma * normed + beta
    sig_value = jax.nn.sigmoid(shifted)
    hidden = (shifted * sig_value * valid[..., None]).astype(jnp.bfloat16)
    flat_hidden = hidden.reshape(-1, model_width)
    flat_cotan = cotan.reshape(-1, model_width)
    outputs = (
        jnp.dot(flat_hidden, w_out, preferred_element_type=jnp.float32)
        .astype(jnp.bfloat16)
        .reshape(cotan.shape)
    )
    weight_rows = lax.psum_scatter(
        lax.dot_general(
            flat_hidden, flat_cotan, (((0,), (0,)), ((), ())), preferred_element_type=jnp.float32
        ),
        "dp",
        scatter_dimension=0,
        tiled=True,
    )
    back_hidden = lax.dot_general(
        flat_cotan, w_out, (((1,), (1,)), ((), ())), preferred_element_type=jnp.float32
    ).reshape(conv_out.shape)
    slope = back_hidden * sig_value * (1.0 + shifted * (1.0 - sig_value)) * valid[..., None]
    beta_sum, gamma_sum = lax.psum(
        (jnp.sum(slope, axis=(0, 1)), jnp.sum(slope * normed, axis=(0, 1))), ("dp", "grp")
    )
    conv_grad = (
        gamma
        * inv_std
        * (slope - beta_sum / frame_total - normed * gamma_sum / frame_total)
        * valid[..., None]
    )
    frame_count = conv_out.shape[1]
    kernel_term = jnp.stack(
        [
            jnp.sum(conv_grad * padded[:, tap : tap + frame_count], axis=(0, 1))
            for tap in range(taps)
        ],
        axis=0,
    )
    kernel_rows = lax.psum_scatter(kernel_term.T, "dp", scatter_dimension=0, tiled=True)
    weight_rows, kernel_rows = lax.psum((weight_rows, kernel_rows), "grp")
    return (outputs, weight_rows, kernel_rows.T, gamma_sum, beta_sum)


def fold(value):
    total = value[0:8]
    for at in range(8, value.shape[0], 8):
        total = total + value[at : at + 8]
    return total


def row_sum(value):
    return jnp.sum(value, axis=0, keepdims=True)


def conv_body(len_hbm, off_hbm, acts_hbm, k_hbm, g_hbm, b_hbm, gp_ref, cv_ref, st_ref, ok_ref, in_ref, gb_ref,
              acc_ref, len_ref, off_ref, acts_ref, k_ref, sems, slot_sems):
    slots, frames, wide = acts_ref.shape
    blocks, _, rows, _ = gp_ref.shape
    taps = k_ref.shape[0]
    lead = taps // 2
    small = [
        pltpu.make_async_copy(source, target, sems.at[i])
        for i, (source, target) in enumerate(
            (
                (len_hbm, len_ref),
                (off_hbm, off_ref),
                (k_hbm, k_ref),
                (g_hbm, gb_ref.at[0]),
                (b_hbm, gb_ref.at[1]),
            )
        )
    ]

    def fetch(slot):
        return pltpu.make_async_copy(acts_hbm.at[slot], acts_ref.at[slot], slot_sems.at[slot])

    small[0].start()
    small[1].start()
    fetch(0).start()
    small[2].start()
    for slot in range(1, slots):
        fetch(slot).start()
    small[3].start()
    small[4].start()
    acc_ref[...] = jnp.zeros_like(acc_ref)
    position = lax.broadcasted_iota(jnp.int32, (frames, LANES), 0)
    reach = lax.broadcasted_iota(jnp.int32, (taps, frames), 1)
    reach = reach - lax.broadcasted_iota(jnp.int32, (taps, frames), 0) + (lead - 1)
    for copy in small[:3]:
        copy.wait()

    def one(slot, carry):
        low = off_ref[slot]
        high = low + len_ref[slot]
        valid = ((position >= low) & (position < high)).astype(F32)
        ok_ref[slot] = valid
        in_ref[slot] = (
            (reach >= low) & (reach < high) & (reach >= 0) & (reach < frames)
        ).astype(F32)
        fetch(slot).wait()
        for block in range(blocks):
            cols = slice(block * LANES, (block + 1) * LANES)
            gate = slice(wide // 2 + block * LANES, wide // 2 + (block + 1) * LANES)
            left, right = acts_ref[slot, :, cols].astype(F32), acts_ref[slot, :, gate].astype(F32)
            gp_ref[block, slot, 0:lead, :] = jnp.zeros((lead, LANES), F32)
            gp_ref[block, slot, lead : lead + frames, :] = left * jax.nn.sigmoid(right) * valid
            tail = jnp.zeros((rows - lead - frames, LANES), F32)
            gp_ref[block, slot, lead + frames : rows, :] = tail
        for block in range(blocks):
            cols = slice(block * LANES, (block + 1) * LANES)
            total = gp_ref[block, slot, 1 : 1 + frames, :] * k_ref[0:1, cols]
            for tap in range(1, taps):
                lag = gp_ref[block, slot, 1 + tap : 1 + tap + frames, :]
                total = total + lag * k_ref[tap : tap + 1, cols]
            cv_ref[block, slot] = total
            masked = total * valid
            acc_ref[0, block] += fold(masked)
            acc_ref[1, block] += fold(masked * total)
        return carry

    lax.fori_loop(0, slots, one, 0)
    small[3].wait()
    small[4].wait()
    for block in range(blocks):
        cols = slice(block * LANES, (block + 1) * LANES)
        st_ref[0:1, cols] = row_sum(acc_ref[0, block])
        st_ref[1:2, cols] = row_sum(acc_ref[1, block])
    count = len_ref[0]
    for other in range(1, slots):
        count = count + len_ref[other]
    st_ref[:, blocks * LANES :] = jnp.full((2, LANES), count.astype(F32), F32)


def lag_sums(gp_ref, block, weights, taps, group, put):
    frames = weights(0).shape[0]
    slots = gp_ref.shape[1]
    for low in range(0, taps, group):
        sums = [None] * group
        for slot in range(slots):
            weight = weights(slot)
            for j in range(group):
                at = 1 + low + j
                term = fold(weight * gp_ref[block, slot, at : at + frames, :])
                sums[j] = term if sums[j] is None else sums[j] + term
        for j in range(group):
            put(low + j, row_sum(sums[j]))


def aux_body(start, ok_ref, in_ref, gp_ref, cv_ref, out_ref, wt_ref):
    _, slots, frames, _ = cv_ref.shape
    many, _, taps, _ = out_ref.shape
    lead = taps // 2

    def one(i, carry):
        block = start + i
        for slot in range(slots):
            wt_ref[slot] = cv_ref[block, slot] * ok_ref[slot]

        def put(k, row):
            out_ref[i, 0, k : k + 1, :] = row

        lag_sums(gp_ref, block, lambda slot: wt_ref[slot], taps, 16, put)
        total = jnp.zeros((taps, LANES), F32)
        for slot in range(slots):
            inside = in_ref[slot].astype(BF16)
            rest = gp_ref[block, slot, lead : lead + frames, :]
            for _ in range(3):
                part = rest.astype(BF16)
                rest = rest - part.astype(F32)
                total = total + jnp.dot(inside, part, preferred_element_type=F32)
        out_ref[i, 1] = total
        return carry

    lax.fori_loop(0, many, one, 0)


def back_body(cotan_ref, w_ref, out_ref):
    for block in range(out_ref.shape[0]):
        rows = w_ref[block * LANES : (block + 1) * LANES, :]
        out_ref[block] = lax.dot_general(
            cotan_ref[...], rows, (((1,), (1,)), ((), ())), preferred_element_type=F32
        )


def scale_of(st_ref, block):
    width = st_ref.shape[1] - LANES
    cols = pl.ds(pl.multiple_of(block * LANES, LANES), LANES)
    count = st_ref[0:1, width:]
    mean = st_ref[0:1, cols] / count
    inv = lax.rsqrt(st_ref[1:2, cols] / count - mean * mean + 1e-05)
    return count, mean, inv


def hidden_body(st_ref, gb_ref, ok_ref, cv_ref, hid_ref):
    blocks, slots, frames, _ = cv_ref.shape

    def one(block, carry):
        _, mean, inv = scale_of(st_ref, block)
        gain, shift = gb_ref[0, pl.ds(block, 1), :], gb_ref[1, pl.ds(block, 1), :]
        for slot in range(slots):
            valid = ok_ref[slot]
            shifted = gain * ((cv_ref[block, slot] - mean) * inv) + shift
            hidden = shifted * jax.nn.sigmoid(shifted) * valid
            hid_ref[block, slot * frames : (slot + 1) * frames, :] = hidden.astype(BF16)
        return carry

    lax.fori_loop(0, blocks, one, 0)


def slope_body(at_ref, st_ref, gb_ref, ok_ref, gp_ref, cv_ref, bk_ref, *refs):
    aux_refs, (give_ref, keep_ref, sl_ref) = refs[:-3], refs[-3:]
    blocks, slots, frames, _ = cv_ref.shape
    taps = aux_refs[0].shape[2]
    last = 3 * taps
    bit = at_ref[0] & 1

    def one(i, aux_ref, odd, q_ref):
        block = 2 * i + odd
        _, mean, inv = scale_of(st_ref, block)
        gain, shift = gb_ref[0, pl.ds(block, 1), :], gb_ref[1, pl.ds(block, 1), :]
        first = second = jnp.zeros((8, LANES), F32)
        for slot in range(slots):
            normed = (cv_ref[block, slot] - mean) * inv
            shifted = gain * normed + shift
            sig = jax.nn.sigmoid(shifted)
            back = bk_ref[block, slot * frames : (slot + 1) * frames, :]
            slope = back * sig * (1.0 + shifted * (1.0 - sig)) * ok_ref[slot]
            sl_ref[slot] = slope
            first, second = first + fold(slope), second + fold(slope * normed)

        def put(k, row):
            q_ref[i, k : k + 1, :] = row

        lag_sums(gp_ref, block, lambda slot: sl_ref[slot], taps, 16, put)
        q_ref[i, taps : 2 * taps, :] = aux_ref[odd, 1]
        q_ref[i, 2 * taps : last, :] = inv * (aux_ref[odd, 0] - mean * aux_ref[odd, 1])
        keep_ref[0, pl.ds(last + block, 1), :] = row_sum(first)
        keep_ref[0, pl.ds(last + blocks + block, 1), :] = row_sum(second)

    for i, aux_ref in enumerate(aux_refs):
        one(i, aux_ref, 1 - bit, give_ref)
        one(i, aux_ref, bit, keep_ref)
    for i in range(len(aux_refs)):
        give_ref[i, last:, :] = keep_ref[0, last:, :]
        if i:
            keep_ref[i, last:, :] = keep_ref[0, last:, :]


def halve_body(level, at_ref, own_ref, recv_ref, give_ref, keep_ref):
    bit = (at_ref[0] >> level) & 1
    for i in range(give_ref.shape[0]):
        for odd, ref in ((1 - bit, give_ref), (bit, keep_ref)):
            ref[i] = own_ref[2 * i + odd] + recv_ref[2 * i + odd]


def out_body(hid_ref, w_ref, out_ref):
    blocks = hid_ref.shape[0]
    slots, frames, _ = out_ref.shape
    total = None
    for block in range(blocks):
        term = jnp.dot(
            hid_ref[block],
            w_ref[block * LANES : (block + 1) * LANES, :],
            preferred_element_type=F32,
        )
        total = term if total is None else total + term
    for slot in range(slots):
        out_ref[slot] = total[slot * frames : (slot + 1) * frames, :].astype(BF16)


def rows_body(masks, at_ref, recv_ref, *refs):
    pieces, (give_ref, keep_ref, held, sems) = refs[:-4], refs[-4:]
    me, half = at_ref[0], at_ref[1]
    copies = [
        pltpu.make_async_copy(piece, held.at[i], sems.at[i]) for i, piece in enumerate(pieces)
    ]
    for copy in copies:
        copy.start()
    many = give_ref.shape[0]
    width = many * LANES
    give = pl.ds(pl.multiple_of((1 - half) * width, width), width)
    keep = pl.ds(pl.multiple_of(half * width, width), width)
    totals = [None, None]
    for i, mask in enumerate(masks):
        left = recv_ref[jnp.bitwise_xor(me, mask)]
        copies[i].wait()
        for j, cols in enumerate((give, keep)):
            term = lax.dot_general(
                left, held[i, :, cols], (((0,), (0,)), ((), ())), preferred_element_type=F32
            )
            totals[j] = term if totals[j] is None else totals[j] + term
    for total, ref in zip(totals, (give_ref, keep_ref)):
        for block in range(many):
            ref[block] = total[:, block * LANES : (block + 1) * LANES].astype(BF16)


def add_body(own_ref, recv_ref, out_ref):
    out_ref[...] = (own_ref[...].astype(F32) + recv_ref[...].astype(F32)).astype(BF16)


def scale_body(at_ref, st_ref, gb_ref, out_ref):
    me = at_ref[0]
    count, _, inv = scale_of(st_ref, me)
    out_ref[0:1, :] = gb_ref[0, pl.ds(me, 1), :] * inv
    out_ref[1:2, :] = count


def last_body(taps, at_ref, own_ref, recv_ref, lags_ref, more_ref, sc_ref, rows_ref, gk_ref, gg_ref, gb_ref):
    me, half = at_ref[0], at_ref[1]
    many = own_ref.shape[0]
    for which, ref in ((half, own_ref), (1 - half, recv_ref)):
        for block in range(many):
            cols = pl.ds(pl.multiple_of((which * many + block) * LANES, LANES), LANES)
            rows_ref[:, cols] = ref[block].astype(F32)
    value = lags_ref[...] + more_ref[...]
    blocks = gb_ref.shape[0]
    gb_ref[...] = value[3 * taps : 3 * taps + blocks]
    gg_ref[...] = value[3 * taps + blocks : 3 * taps + 2 * blocks]
    count = sc_ref[1:2, :]
    mine = pl.ds(me, 1)
    gk_ref[...] = sc_ref[0:1, :] * (
        value[0:taps]
        - (gb_ref[mine, :] / count) * value[taps : 2 * taps]
        - (gg_ref[mine, :] / count) * value[2 * taps : 3 * taps]
    )


SMEM = pl.BlockSpec(memory_space=pltpu.SMEM)
VMEM = pl.BlockSpec(memory_space=pltpu.VMEM)
HBM = pl.BlockSpec(memory_space=pltpu.HBM)
ANY = pl.BlockSpec(memory_space=pl.ANY)


def in_hbm(value):
    return pltpu.with_memory_space_constraint(value, pltpu.HBM)


def call(body, shapes, scalars, args, flops=0, scratch=(), mib=8, **more):
    many = isinstance(shapes, list)
    moved = sum(a.size * a.dtype.itemsize for a in args)
    return pl.pallas_call(
        body,
        in_specs=more.pop("in_specs", None) or [SMEM] * len(scalars) + [VMEM] * len(args),
        out_specs=[VMEM] * len(shapes) if many else VMEM,
        out_shape=shapes,
        scratch_shapes=scratch,
        compiler_params=pltpu.CompilerParams(vmem_limit_bytes=mib << 20),
        cost_estimate=pl.CostEstimate(flops=flops, bytes_accessed=moved, transcendentals=0),
        **more,
    )(*scalars, *args)


def local_fast(n_dp, n_grp, acts, cotan, lengths, offsets, kernel, gamma, beta, w_out):
    slots, frames, wide = acts.shape
    width = wide // 2
    taps = kernel.shape[0]
    blocks = width // LANES
    tokens = slots * frames
    n_q = 3 * taps + 2 * blocks
    padded = 2 * (taps // 2) + frames
    me_dp, me_grp = lax.axis_index("dp"), lax.axis_index("grp")
    shape = jax.ShapeDtypeStruct

    def swap(value, dp_mask, grp_mask):
        pairs = [
            (d * n_grp + g, (d ^ dp_mask) * n_grp + (g ^ grp_mask))
            for d in range(n_dp)
            for g in range(n_grp)
        ]
        return lax.ppermute(value, ("dp", "grp"), pairs)

    dp_bits = [1 << i for i in range(n_dp.bit_length() - 1)]
    grp_bits = [1 << i for i in range(n_grp.bit_length() - 1)]
    at = jnp.stack([me_dp, me_grp % 2]).astype(jnp.int32)
    gamma2, beta2 = gamma.reshape(blocks, LANES), beta.reshape(blocks, LANES)

    flat_cotan = cotan.reshape(tokens, width)
    pieces = [(0, flat_cotan)]
    for bit in dp_bits[1:] + dp_bits[:1]:
        pieces += [(m | bit, swap(v, bit, 0)) for m, v in pieces]
    masks, values = tuple(m for m, _ in pieces), [v for _, v in pieces]

    gated, conv_out, stats, valid, inside, gains = call(
        conv_body,
        [
            shape((blocks, slots, padded, LANES), F32),
            shape((blocks, slots, frames, LANES), F32),
            shape((2, width + LANES), F32),
            shape((slots, frames, LANES), F32),
            shape((slots, taps, frames), F32),
            shape((2, blocks, LANES), F32),
        ],
        (),
        [in_hbm(value) for value in (lengths, offsets, acts, kernel, gamma2, beta2)],
        flops=4 * taps * tokens * width,
        scratch=[
            pltpu.VMEM((2, blocks, 8, LANES), F32),
            pltpu.SMEM((slots,), jnp.int32),
            pltpu.SMEM((slots,), jnp.int32),
            pltpu.VMEM(acts.shape, BF16),
            pltpu.VMEM(kernel.shape, F32),
            pltpu.SemaphoreType.DMA((5,)),
            pltpu.SemaphoreType.DMA((slots,)),
        ],
        in_specs=[HBM] * 6,
    )

    hops = [(1, m) for m in grp_bits] + [(m | 1, 0) for m in dp_bits[1:]] + [(1, 0)]
    for dp_mask, grp_mask in hops:
        stats = stats + swap(stats, dp_mask, grp_mask)

    back = call(
        back_body,
        shape((blocks, tokens, LANES), F32),
        (),
        (flat_cotan, w_out),
        flops=2 * tokens * width * width,
    )
    parts = blocks // 2
    each = 2
    aux = [
        call(
            functools.partial(aux_body, i * each),
            shape((each, 2, taps, LANES), F32),
            (),
            (valid, inside, gated, conv_out),
            flops=4 * taps * tokens * each * LANES,
            scratch=[pltpu.VMEM((slots, frames, LANES), F32)],
        )
        for i in range(parts)
    ]

    hidden = call(
        hidden_body, shape((blocks, tokens, LANES), BF16), (), (stats, gains, valid, conv_out)
    )
    received = lax.all_to_all(hidden, "dp", 0, 0, tiled=True)
    give, lags = call(
        slope_body,
        [shape((parts, n_q, LANES), F32)] * 2,
        (at,),
        (stats, gains, valid, gated, conv_out, back, *aux),
        flops=4 * taps * tokens * width,
        scratch=[pltpu.VMEM((slots, frames, LANES), F32)],
    )
    for level in range(1, len(dp_bits)):
        came = swap(give, dp_bits[level - 1], 0)
        give, lags = call(
            functools.partial(halve_body, level),
            [shape((parts >> level, n_q, LANES), F32)] * 2,
            (at,),
            (lags, came),
        )
    lags = (lags + swap(give, dp_bits[-1], 0))[0]
    scale = call(scale_body, shape((2, LANES), F32), (at,), (stats, gains))
    outputs = call(out_body, shape(cotan.shape, BF16), (), (hidden, w_out))

    half_shape = shape((blocks // 2, LANES, LANES), BF16)
    given, kept = call(
        functools.partial(rows_body, masks),
        [half_shape] * 2,
        (at,),
        (received, *values),
        flops=2 * n_dp * tokens * LANES * width,
        scratch=[
            pltpu.VMEM((n_dp, tokens, width), BF16),
            pltpu.SemaphoreType.DMA((n_dp,)),
        ],
        in_specs=[SMEM, VMEM] + [ANY] * n_dp,
    )
    taken = swap(given, 0, 1)
    both = call(add_body, half_shape, (), (kept, taken))
    for mask in grp_bits[1:]:
        other = swap(both, 0, mask)
        both = call(add_body, half_shape, (), (both, other))
    rest = swap(both, 0, 1)

    for mask in grp_bits[1:]:
        lags = lags + swap(lags, 0, mask)
    more = swap(lags, 0, 1)
    weight_rows, grad_kernel, gamma_sum, beta_sum = call(
        functools.partial(last_body, taps),
        [
            shape((LANES, width), F32),
            shape((taps, LANES), F32),
            shape((blocks, LANES), F32),
            shape((blocks, LANES), F32),
        ],
        (at,),
        (both, rest, lags, more, scale),
    )
    return (outputs, weight_rows, grad_kernel, gamma_sum.reshape(width), beta_sum.reshape(width))


def solution(mesh):
    n_dp, n_grp = mesh.shape["dp"], mesh.shape["grp"]

    def fits(width, taps, frames):
        return (
            n_dp & (n_dp - 1) == 0
            and n_grp & (n_grp - 1) == 0
            and n_dp >= 4
            and n_grp >= 4
            and width == n_dp * LANES
            and taps % 16 == 0
            and frames % 16 == 0
            and n_dp % 8 == 0
        )

    def local(acts, cotan, lengths, offsets, kernel, gamma, beta, w_out):
        args = (acts, cotan, lengths, offsets, kernel, gamma, beta, w_out)
        if not fits(w_out.shape[0], kernel.shape[0], acts.shape[1]):
            return local_general(*args)
        return local_fast(n_dp, n_grp, *args)

    placed = (
        P(("dp", "grp"), None, None),
        P(("dp", "grp"), None, None),
        P(("dp", "grp")),
        P(("dp", "grp")),
        P(),
        P(),
        P(),
        P(),
    )
    return jax.shard_map(
        local,
        mesh=mesh,
        in_specs=placed,
        out_specs=(P(("dp", "grp"), None, None), P("dp", None), P(None, "dp"), P(), P()),
        check_vma=False,
    )
```

```python
import functools

import jax
import jax.numpy as jnp
from jax import lax
from jax.experimental import pallas as pl
from jax.experimental.pallas import tpu as pltpu
from jax.sharding import PartitionSpec as P


LANES = 128
F32 = jnp.float32
BF16 = jnp.bfloat16


def convolve(block_acts, block_len, block_off, kernel):
    taps = kernel.shape[0]
    model_width = kernel.shape[1]
    frame_count = block_acts.shape[1]
    position = jnp.arange(frame_count, dtype=jnp.int32)
    valid = (
        (position[None, :] >= block_off[:, None])
        & (position[None, :] < (block_off + block_len)[:, None])
    ).astype(jnp.float32)
    wide_acts = block_acts.astype(jnp.float32)
    gated = (
        wide_acts[..., :model_width]
        * jax.nn.sigmoid(wide_acts[..., model_width:])
        * valid[..., None]
    )
    padded = jnp.pad(gated, ((0, 0), (taps // 2 - 1, taps // 2), (0, 0)))
    conv_out = padded[:, 0:frame_count] * kernel[0]
    for tap in range(1, taps):
        conv_out = conv_out + padded[:, tap : tap + frame_count] * kernel[tap]
    return (valid, padded, conv_out)


def local_general(acts, cotan, lengths, offsets, kernel, gamma, beta, w_out):
    model_width = w_out.shape[0]
    taps = kernel.shape[0]
    valid, padded, conv_out = convolve(acts, lengths, offsets, kernel)
    masked = conv_out * valid[..., None]
    sum_first, sum_second, frame_total = lax.psum(
        (
            jnp.sum(masked, axis=(0, 1)),
            jnp.sum(masked * conv_out, axis=(0, 1)),
            jnp.sum(lengths).astype(jnp.float32),
        ),
        ("dp", "grp"),
    )
    mean_value = sum_first / frame_total
    inv_std = lax.rsqrt(sum_second / frame_total - mean_value * mean_value + 1e-05)
    normed = (conv_out - mean_value) * inv_std
    shifted = gamma * normed + beta
    sig_value = jax.nn.sigmoid(shifted)
    hidden = (shifted * sig_value * valid[..., None]).astype(jnp.bfloat16)
    flat_hidden = hidden.reshape(-1, model_width)
    flat_cotan = cotan.reshape(-1, model_width)
    outputs = (
        jnp.dot(flat_hidden, w_out, preferred_element_type=jnp.float32)
        .astype(jnp.bfloat16)
        .reshape(cotan.shape)
    )
    weight_rows = lax.psum_scatter(
        lax.dot_general(
            flat_hidden, flat_cotan, (((0,), (0,)), ((), ())), preferred_element_type=jnp.float32
        ),
        "dp",
        scatter_dimension=0,
        tiled=True,
    )
    back_hidden = lax.dot_general(
        flat_cotan, w_out, (((1,), (1,)), ((), ())), preferred_element_type=jnp.float32
    ).reshape(conv_out.shape)
    slope = back_hidden * sig_value * (1.0 + shifted * (1.0 - sig_value)) * valid[..., None]
    beta_sum, gamma_sum = lax.psum(
        (jnp.sum(slope, axis=(0, 1)), jnp.sum(slope * normed, axis=(0, 1))), ("dp", "grp")
    )
    conv_grad = (
        gamma
        * inv_std
        * (slope - beta_sum / frame_total - normed * gamma_sum / frame_total)
        * valid[..., None]
    )
    frame_count = conv_out.shape[1]
    kernel_term = jnp.stack(
        [
            jnp.sum(conv_grad * padded[:, tap : tap + frame_count], axis=(0, 1))
            for tap in range(taps)
        ],
        axis=0,
    )
    kernel_rows = lax.psum_scatter(kernel_term.T, "dp", scatter_dimension=0, tiled=True)
    weight_rows, kernel_rows = lax.psum((weight_rows, kernel_rows), "grp")
    return (outputs, weight_rows, kernel_rows.T, gamma_sum, beta_sum)


def fold(value):
    total = value[0:8]
    for at in range(8, value.shape[0], 8):
        total = total + value[at : at + 8]
    return total


def row_sum(value):
    return jnp.sum(value, axis=0, keepdims=True)


def conv_body(len_hbm, off_hbm, acts_hbm, k_hbm, g_hbm, b_hbm, gp_ref, cv_ref, st_ref, ok_ref, in_ref, gb_ref,
              acc_ref, len_ref, off_ref, acts_ref, k_ref, sems, slot_sems):
    slots, frames, wide = acts_ref.shape
    blocks, _, rows, _ = gp_ref.shape
    taps = k_ref.shape[0]
    lead = taps // 2
    small = [
        pltpu.make_async_copy(source, target, sems.at[i])
        for i, (source, target) in enumerate(
            (
                (len_hbm, len_ref),
                (off_hbm, off_ref),
                (k_hbm, k_ref),
                (g_hbm, gb_ref.at[0]),
                (b_hbm, gb_ref.at[1]),
            )
        )
    ]

    def fetch(slot):
        return pltpu.make_async_copy(acts_hbm.at[slot], acts_ref.at[slot], slot_sems.at[slot])

    small[0].start()
    small[1].start()
    fetch(0).start()
    small[2].start()
    for slot in range(1, slots):
        fetch(slot).start()
    for copy in small[3:]:
        copy.start()
    acc_ref[...] = jnp.zeros_like(acc_ref)
    position = lax.broadcasted_iota(jnp.int32, (frames, LANES), 0)
    reach = lax.broadcasted_iota(jnp.int32, (taps, frames), 1)
    reach = reach - lax.broadcasted_iota(jnp.int32, (taps, frames), 0) + (lead - 1)
    for copy in small[:3]:
        copy.wait()

    def one(slot, carry):
        low = off_ref[slot]
        high = low + len_ref[slot]
        valid = ((position >= low) & (position < high)).astype(F32)
        ok_ref[slot] = valid
        in_ref[slot] = (
            (reach >= low) & (reach < high) & (reach >= 0) & (reach < frames)
        ).astype(F32)
        fetch(slot).wait()
        for block in range(blocks):
            cols = slice(block * LANES, (block + 1) * LANES)
            gate = slice(wide // 2 + block * LANES, wide // 2 + (block + 1) * LANES)
            left, right = acts_ref[slot, :, cols].astype(F32), acts_ref[slot, :, gate].astype(F32)
            gp_ref[block, slot, 0:lead, :] = jnp.zeros((lead, LANES), F32)
            gp_ref[block, slot, lead : lead + frames, :] = left * jax.nn.sigmoid(right) * valid
            tail = jnp.zeros((rows - lead - frames, LANES), F32)
            gp_ref[block, slot, lead + frames : rows, :] = tail
        for block in range(blocks):
            cols = slice(block * LANES, (block + 1) * LANES)
            total = gp_ref[block, slot, 1 : 1 + frames, :] * k_ref[0:1, cols]
            for tap in range(1, taps):
                lag = gp_ref[block, slot, 1 + tap : 1 + tap + frames, :]
                total = total + lag * k_ref[tap : tap + 1, cols]
            cv_ref[block, slot] = total
            masked = total * valid
            acc_ref[0, block] += fold(masked)
            acc_ref[1, block] += fold(masked * total)
        return carry

    lax.fori_loop(0, slots, one, 0)
    for copy in small[3:]:
        copy.wait()
    for block in range(blocks):
        cols = slice(block * LANES, (block + 1) * LANES)
        st_ref[0:1, cols] = row_sum(acc_ref[0, block])
        st_ref[1:2, cols] = row_sum(acc_ref[1, block])
    count = len_ref[0]
    for other in range(1, slots):
        count = count + len_ref[other]
    st_ref[:, blocks * LANES :] = jnp.full((2, LANES), count.astype(F32), F32)


def lag_sums(gp_ref, block, weights, taps, group, put):
    frames = weights(0).shape[0]
    slots = gp_ref.shape[1]
    for low in range(0, taps, group):
        sums = [None] * group
        for slot in range(slots):
            weight = weights(slot)
            for j in range(group):
                at = 1 + low + j
                term = fold(weight * gp_ref[block, slot, at : at + frames, :])
                sums[j] = term if sums[j] is None else sums[j] + term
        for j in range(group):
            put(low + j, row_sum(sums[j]))


def aux_body(start, ok_ref, in_ref, gp_ref, cv_ref, out_ref, wt_ref):
    _, slots, frames, _ = cv_ref.shape
    many, _, taps, _ = out_ref.shape
    lead = taps // 2

    def one(i, carry):
        block = start + i
        for slot in range(slots):
            wt_ref[slot] = cv_ref[block, slot] * ok_ref[slot]

        def put(k, row):
            out_ref[i, 0, k : k + 1, :] = row

        lag_sums(gp_ref, block, lambda slot: wt_ref[slot], taps, 16, put)
        total = jnp.zeros((taps, LANES), F32)
        for slot in range(slots):
            inside = in_ref[slot].astype(BF16)
            rest = gp_ref[block, slot, lead : lead + frames, :]
            for _ in range(3):
                part = rest.astype(BF16)
                rest = rest - part.astype(F32)
                total = total + jnp.dot(inside, part, preferred_element_type=F32)
        out_ref[i, 1] = total
        return carry

    lax.fori_loop(0, many, one, 0)


def back_body(cotan_hbm, w_hbm, out_ref, cotan_ref, w_ref, sems):
    blocks = out_ref.shape[0]
    fetch = pltpu.make_async_copy(cotan_hbm, cotan_ref, sems.at[blocks])
    fetch.start()
    copies = []
    for block in range(blocks):
        rows = pl.ds(block * LANES, LANES)
        copies.append(pltpu.make_async_copy(w_hbm.at[rows], w_ref.at[rows], sems.at[block]))
        copies[-1].start()
    fetch.wait()
    for block in range(blocks):
        copies[block].wait()
        rows = w_ref[block * LANES : (block + 1) * LANES, :]
        out_ref[block] = lax.dot_general(
            cotan_ref[...], rows, (((1,), (1,)), ((), ())), preferred_element_type=F32
        )


def scale_of(st_ref, block):
    width = st_ref.shape[1] - LANES
    cols = pl.ds(pl.multiple_of(block * LANES, LANES), LANES)
    count = st_ref[0:1, width:]
    mean = st_ref[0:1, cols] / count
    inv = lax.rsqrt(st_ref[1:2, cols] / count - mean * mean + 1e-05)
    return count, mean, inv


def hidden_body(st_ref, gb_ref, ok_ref, cv_ref, hid_ref):
    blocks, slots, frames, _ = cv_ref.shape

    def one(block, carry):
        _, mean, inv = scale_of(st_ref, block)
        gain, shift = gb_ref[0, pl.ds(block, 1), :], gb_ref[1, pl.ds(block, 1), :]
        for slot in range(slots):
            valid = ok_ref[slot]
            shifted = gain * ((cv_ref[block, slot] - mean) * inv) + shift
            hidden = shifted * jax.nn.sigmoid(shifted) * valid
            hid_ref[block, slot * frames : (slot + 1) * frames, :] = hidden.astype(BF16)
        return carry

    lax.fori_loop(0, blocks, one, 0)


def slope_body(st_ref, gb_ref, ok_ref, gp_ref, cv_ref, bk_ref, *refs):
    aux_refs, (give_ref, keep_ref, sl_ref) = refs[:-3], refs[-3:]
    blocks, slots, frames, _ = cv_ref.shape
    taps = aux_refs[0].shape[2]
    last = 3 * taps
    bit = lax.axis_index("dp") & 1

    def one(i, aux_ref, odd, q_ref):
        block = 2 * i + odd
        _, mean, inv = scale_of(st_ref, block)
        gain, shift = gb_ref[0, pl.ds(block, 1), :], gb_ref[1, pl.ds(block, 1), :]
        first = second = jnp.zeros((8, LANES), F32)
        for slot in range(slots):
            normed = (cv_ref[block, slot] - mean) * inv
            shifted = gain * normed + shift
            sig = jax.nn.sigmoid(shifted)
            back = bk_ref[block, slot * frames : (slot + 1) * frames, :]
            slope = back * sig * (1.0 + shifted * (1.0 - sig)) * ok_ref[slot]
            sl_ref[slot] = slope
            first, second = first + fold(slope), second + fold(slope * normed)

        def put(k, row):
            q_ref[i, k : k + 1, :] = row

        lag_sums(gp_ref, block, lambda slot: sl_ref[slot], taps, 16, put)
        q_ref[i, taps : 2 * taps, :] = aux_ref[odd, 1]
        q_ref[i, 2 * taps : last, :] = inv * (aux_ref[odd, 0] - mean * aux_ref[odd, 1])
        keep_ref[0, pl.ds(last + block, 1), :] = row_sum(first)
        keep_ref[0, pl.ds(last + blocks + block, 1), :] = row_sum(second)

    for i, aux_ref in enumerate(aux_refs):
        one(i, aux_ref, 1 - bit, give_ref)
        one(i, aux_ref, bit, keep_ref)
    for i in range(len(aux_refs)):
        give_ref[i, last:, :] = keep_ref[0, last:, :]
        if i:
            keep_ref[i, last:, :] = keep_ref[0, last:, :]


def halve_body(level, own_ref, recv_ref, give_ref, keep_ref):
    bit = (lax.axis_index("dp") >> level) & 1
    for i in range(give_ref.shape[0]):
        for odd, ref in ((1 - bit, give_ref), (bit, keep_ref)):
            ref[i] = own_ref[2 * i + odd] + recv_ref[2 * i + odd]


def out_body(hid_ref, w_ref, out_ref):
    blocks = hid_ref.shape[0]
    slots, frames, _ = out_ref.shape
    total = None
    for block in range(blocks):
        term = jnp.dot(
            hid_ref[block],
            w_ref[block * LANES : (block + 1) * LANES, :],
            preferred_element_type=F32,
        )
        total = term if total is None else total + term
    for slot in range(slots):
        out_ref[slot] = total[slot * frames : (slot + 1) * frames, :].astype(BF16)


def stage_body(*refs):
    pieces, out_ref, sems = refs[:-2], refs[-2], refs[-1]
    copies = [
        pltpu.make_async_copy(piece, out_ref.at[i], sems.at[i]) for i, piece in enumerate(pieces)
    ]
    for copy in copies:
        copy.start()
    for copy in copies:
        copy.wait()


def rows_body(masks, recv_ref, staged_ref, *refs):
    pieces, (give_ref, keep_ref, held, sems) = refs[:-4], refs[-4:]
    me, half = lax.axis_index("dp"), lax.axis_index("grp") & 1
    copies = [
        pltpu.make_async_copy(piece, held.at[i], sems.at[i]) for i, piece in enumerate(pieces)
    ]
    for copy in copies:
        copy.start()
    early = staged_ref.shape[0]
    many = give_ref.shape[0]
    width = many * LANES
    give = pl.ds(pl.multiple_of((1 - half) * width, width), width)
    keep = pl.ds(pl.multiple_of(half * width, width), width)
    totals = [None, None]
    for i, mask in enumerate(masks):
        left = recv_ref[jnp.bitwise_xor(me, mask)]
        if i >= early:
            copies[i - early].wait()
        for j, cols in enumerate((give, keep)):
            right = staged_ref[i, :, cols] if i < early else held[i - early, :, cols]
            term = lax.dot_general(
                left, right, (((0,), (0,)), ((), ())), preferred_element_type=F32
            )
            totals[j] = term if totals[j] is None else totals[j] + term
    for total, ref in zip(totals, (give_ref, keep_ref)):
        for block in range(many):
            ref[block] = total[:, block * LANES : (block + 1) * LANES].astype(BF16)


def plus_body(own_ref, recv_ref, out_ref):
    out_ref[...] = own_ref[...] + recv_ref[...]


def add_body(own_ref, recv_ref, out_ref):
    out_ref[...] = (own_ref[...].astype(F32) + recv_ref[...].astype(F32)).astype(BF16)


def scale_body(st_ref, gb_ref, out_ref):
    me = lax.axis_index("dp")
    count, _, inv = scale_of(st_ref, me)
    out_ref[0:1, :] = gb_ref[0, pl.ds(me, 1), :] * inv
    out_ref[1:2, :] = count


def last_body(taps, own_ref, recv_ref, lags_ref, more_ref, sc_ref, rows_ref, gk_ref, gg_ref, gb_ref):
    me, half = lax.axis_index("dp"), lax.axis_index("grp") & 1
    many = own_ref.shape[0]
    for which, ref in ((half, own_ref), (1 - half, recv_ref)):
        for block in range(many):
            cols = pl.ds(pl.multiple_of((which * many + block) * LANES, LANES), LANES)
            rows_ref[:, cols] = ref[block].astype(F32)
    value = lags_ref[0] + more_ref[0]
    blocks = gb_ref.shape[0]
    gb_ref[...] = value[3 * taps : 3 * taps + blocks]
    gg_ref[...] = value[3 * taps + blocks : 3 * taps + 2 * blocks]
    count = sc_ref[1:2, :]
    mine = pl.ds(me, 1)
    gk_ref[...] = sc_ref[0:1, :] * (
        value[0:taps]
        - (gb_ref[mine, :] / count) * value[taps : 2 * taps]
        - (gg_ref[mine, :] / count) * value[2 * taps : 3 * taps]
    )


SMEM = pl.BlockSpec(memory_space=pltpu.SMEM)
VMEM = pl.BlockSpec(memory_space=pltpu.VMEM)
HBM = pl.BlockSpec(memory_space=pltpu.HBM)
ANY = pl.BlockSpec(memory_space=pl.ANY)


def in_hbm(value):
    return pltpu.with_memory_space_constraint(value, pltpu.HBM)


def call(body, shapes, scalars, args, flops=0, scratch=(), mib=8, **more):
    many = isinstance(shapes, list)
    moved = sum(a.size * a.dtype.itemsize for a in args)
    return pl.pallas_call(
        body,
        in_specs=more.pop("in_specs", None) or [SMEM] * len(scalars) + [VMEM] * len(args),
        out_specs=[VMEM] * len(shapes) if many else VMEM,
        out_shape=shapes,
        scratch_shapes=scratch,
        compiler_params=pltpu.CompilerParams(vmem_limit_bytes=mib << 20),
        cost_estimate=pl.CostEstimate(flops=flops, bytes_accessed=moved, transcendentals=0),
        **more,
    )(*scalars, *args)


def local_fast(n_dp, n_grp, acts, cotan, lengths, offsets, kernel, gamma, beta, w_out):
    slots, frames, wide = acts.shape
    width = wide // 2
    taps = kernel.shape[0]
    blocks = width // LANES
    tokens = slots * frames
    n_q = 3 * taps + 2 * blocks
    padded = 2 * (taps // 2) + frames
    shape = jax.ShapeDtypeStruct

    def swap(value, dp_mask, grp_mask):
        pairs = [
            (d * n_grp + g, (d ^ dp_mask) * n_grp + (g ^ grp_mask))
            for d in range(n_dp)
            for g in range(n_grp)
        ]
        return lax.ppermute(value, ("dp", "grp"), pairs)

    def plus(own, other):
        return call(plus_body, shape(own.shape, own.dtype), (), (own, other))

    dp_bits = [1 << i for i in range(n_dp.bit_length() - 1)]
    grp_bits = [1 << i for i in range(n_grp.bit_length() - 1)]
    gamma2, beta2 = gamma.reshape(blocks, LANES), beta.reshape(blocks, LANES)

    flat_cotan = cotan.reshape(tokens, width)
    pieces = [(0, flat_cotan)]
    for bit in dp_bits[1:] + dp_bits[:1]:
        pieces += [(m | bit, swap(v, bit, 0)) for m, v in pieces]
    late_bits = dp_bits[-1] | dp_bits[-2]
    pieces.sort(key=lambda piece: piece[0] & late_bits == late_bits)
    masks, values = tuple(m for m, _ in pieces), [v for _, v in pieces]
    early = sum(m & late_bits != late_bits for m in masks)

    gated, conv_out, stats, valid, inside, gains = call(
        conv_body,
        [
            shape((blocks, slots, padded, LANES), F32),
            shape((blocks, slots, frames, LANES), F32),
            shape((2, width + LANES), F32),
            shape((slots, frames, LANES), F32),
            shape((slots, taps, frames), F32),
            shape((2, blocks, LANES), F32),
        ],
        (),
        [in_hbm(v) for v in (lengths, offsets, acts, kernel, gamma2, beta2)],
        flops=4 * taps * tokens * width,
        scratch=[
            pltpu.VMEM((2, blocks, 8, LANES), F32),
            pltpu.SMEM((slots,), jnp.int32),
            pltpu.SMEM((slots,), jnp.int32),
            pltpu.VMEM(acts.shape, BF16),
            pltpu.VMEM(kernel.shape, F32),
            pltpu.SemaphoreType.DMA((5,)),
            pltpu.SemaphoreType.DMA((slots,)),
        ],
        in_specs=[HBM] * 6,
    )

    hops = [(1, m) for m in grp_bits] + [(m | 1, 0) for m in dp_bits[1:]] + [(1, 0)]
    for dp_mask, grp_mask in hops:
        stats = plus(stats, swap(stats, dp_mask, grp_mask))

    back = call(
        back_body,
        shape((blocks, tokens, LANES), F32),
        (),
        (in_hbm(flat_cotan), in_hbm(w_out)),
        flops=2 * tokens * width * width,
        scratch=[
            pltpu.VMEM(flat_cotan.shape, BF16),
            pltpu.VMEM(w_out.shape, BF16),
            pltpu.SemaphoreType.DMA((blocks + 1,)),
        ],
        in_specs=[HBM] * 2,
    )
    parts = blocks // 2
    each = 2
    aux = [
        call(
            functools.partial(aux_body, i * each),
            shape((each, 2, taps, LANES), F32),
            (),
            (valid, inside, gated, conv_out),
            flops=4 * taps * tokens * each * LANES,
            scratch=[pltpu.VMEM((slots, frames, LANES), F32)],
        )
        for i in range(parts)
    ]

    hidden = call(
        hidden_body, shape((blocks, tokens, LANES), BF16), (), (stats, gains, valid, conv_out)
    )
    received = lax.all_to_all(hidden, "dp", 0, 0, tiled=True)
    give, lags = call(
        slope_body,
        [shape((parts, n_q, LANES), F32)] * 2,
        (),
        (stats, gains, valid, gated, conv_out, back, *aux),
        flops=4 * taps * tokens * width,
        scratch=[pltpu.VMEM((slots, frames, LANES), F32)],
    )
    for level in range(1, len(dp_bits)):
        came = swap(give, dp_bits[level - 1], 0)
        give, lags = call(
            functools.partial(halve_body, level),
            [shape((parts >> level, n_q, LANES), F32)] * 2,
            (),
            (lags, came),
        )
    lags = plus(lags, swap(give, dp_bits[-1], 0))
    scale = call(scale_body, shape((2, LANES), F32), (), (stats, gains))
    outputs = call(out_body, shape(cotan.shape, BF16), (), (hidden, w_out))

    half_shape = shape((blocks // 2, LANES, LANES), BF16)
    staged = call(
        stage_body,
        shape((early, tokens, width), BF16),
        (),
        values[:early],
        scratch=[pltpu.SemaphoreType.DMA((early,))],
        in_specs=[ANY] * early,
    )
    given, kept = call(
        functools.partial(rows_body, masks),
        [half_shape] * 2,
        (),
        (received, staged, *values[early:]),
        flops=2 * n_dp * tokens * LANES * width,
        scratch=[
            pltpu.VMEM((n_dp - early, tokens, width), BF16),
            pltpu.SemaphoreType.DMA((n_dp - early,)),
        ],
        in_specs=[VMEM, VMEM] + [ANY] * (n_dp - early),
    )
    taken = swap(given, 0, 1)
    both = call(add_body, half_shape, (), (kept, taken))
    for mask in grp_bits[1:]:
        other = swap(both, 0, mask)
        both = call(add_body, half_shape, (), (both, other))
    rest = swap(both, 0, 1)

    for mask in grp_bits[:-1]:
        lags = plus(lags, swap(lags, 0, mask))
    more = swap(lags, 0, grp_bits[-1])
    weight_rows, grad_kernel, gamma_sum, beta_sum = call(
        functools.partial(last_body, taps),
        [
            shape((LANES, width), F32),
            shape((taps, LANES), F32),
            shape((blocks, LANES), F32),
            shape((blocks, LANES), F32),
        ],
        (),
        (both, rest, lags, more, scale),
    )
    return (outputs, weight_rows, grad_kernel, gamma_sum.reshape(width), beta_sum.reshape(width))


def solution(mesh):
    n_dp, n_grp = mesh.shape["dp"], mesh.shape["grp"]

    def fits(width, taps, frames):
        return (
            n_dp & (n_dp - 1) == 0
            and n_grp & (n_grp - 1) == 0
            and n_dp >= 4
            and n_grp >= 4
            and width == n_dp * LANES
            and taps % 16 == 0
            and frames % 16 == 0
            and n_dp % 8 == 0
        )

    def local(acts, cotan, lengths, offsets, kernel, gamma, beta, w_out):
        args = (acts, cotan, lengths, offsets, kernel, gamma, beta, w_out)
        if not fits(w_out.shape[0], kernel.shape[0], acts.shape[1]):
            return local_general(*args)
        return local_fast(n_dp, n_grp, *args)

    placed = (
        P(("dp", "grp"), None, None),
        P(("dp", "grp"), None, None),
        P(("dp", "grp")),
        P(("dp", "grp")),
        P(),
        P(),
        P(),
        P(),
    )
    return jax.shard_map(
        local,
        mesh=mesh,
        in_specs=placed,
        out_specs=(P(("dp", "grp"), None, None), P("dp", None), P(None, "dp"), P(), P()),
        check_vma=False,
    )
```

```python
import functools

import jax
import jax.numpy as jnp
from jax import lax
from jax.experimental import pallas as pl
from jax.experimental.pallas import tpu as pltpu
from jax.sharding import PartitionSpec as P


LANES = 128
F32 = jnp.float32
BF16 = jnp.bfloat16


def convolve(block_acts, block_len, block_off, kernel):
    taps = kernel.shape[0]
    model_width = kernel.shape[1]
    frame_count = block_acts.shape[1]
    position = jnp.arange(frame_count, dtype=jnp.int32)
    valid = (
        (position[None, :] >= block_off[:, None])
        & (position[None, :] < (block_off + block_len)[:, None])
    ).astype(jnp.float32)
    wide_acts = block_acts.astype(jnp.float32)
    gated = (
        wide_acts[..., :model_width]
        * jax.nn.sigmoid(wide_acts[..., model_width:])
        * valid[..., None]
    )
    padded = jnp.pad(gated, ((0, 0), (taps // 2 - 1, taps // 2), (0, 0)))
    conv_out = padded[:, 0:frame_count] * kernel[0]
    for tap in range(1, taps):
        conv_out = conv_out + padded[:, tap : tap + frame_count] * kernel[tap]
    return (valid, padded, conv_out)


def local_general(acts, cotan, lengths, offsets, kernel, gamma, beta, w_out):
    model_width = w_out.shape[0]
    taps = kernel.shape[0]
    valid, padded, conv_out = convolve(acts, lengths, offsets, kernel)
    masked = conv_out * valid[..., None]
    sum_first, sum_second, frame_total = lax.psum(
        (
            jnp.sum(masked, axis=(0, 1)),
            jnp.sum(masked * conv_out, axis=(0, 1)),
            jnp.sum(lengths).astype(jnp.float32),
        ),
        ("dp", "grp"),
    )
    mean_value = sum_first / frame_total
    inv_std = lax.rsqrt(sum_second / frame_total - mean_value * mean_value + 1e-05)
    normed = (conv_out - mean_value) * inv_std
    shifted = gamma * normed + beta
    sig_value = jax.nn.sigmoid(shifted)
    hidden = (shifted * sig_value * valid[..., None]).astype(jnp.bfloat16)
    flat_hidden = hidden.reshape(-1, model_width)
    flat_cotan = cotan.reshape(-1, model_width)
    outputs = (
        jnp.dot(flat_hidden, w_out, preferred_element_type=jnp.float32)
        .astype(jnp.bfloat16)
        .reshape(cotan.shape)
    )
    weight_rows = lax.psum_scatter(
        lax.dot_general(
            flat_hidden, flat_cotan, (((0,), (0,)), ((), ())), preferred_element_type=jnp.float32
        ),
        "dp",
        scatter_dimension=0,
        tiled=True,
    )
    back_hidden = lax.dot_general(
        flat_cotan, w_out, (((1,), (1,)), ((), ())), preferred_element_type=jnp.float32
    ).reshape(conv_out.shape)
    slope = back_hidden * sig_value * (1.0 + shifted * (1.0 - sig_value)) * valid[..., None]
    beta_sum, gamma_sum = lax.psum(
        (jnp.sum(slope, axis=(0, 1)), jnp.sum(slope * normed, axis=(0, 1))), ("dp", "grp")
    )
    conv_grad = (
        gamma
        * inv_std
        * (slope - beta_sum / frame_total - normed * gamma_sum / frame_total)
        * valid[..., None]
    )
    frame_count = conv_out.shape[1]
    kernel_term = jnp.stack(
        [
            jnp.sum(conv_grad * padded[:, tap : tap + frame_count], axis=(0, 1))
            for tap in range(taps)
        ],
        axis=0,
    )
    kernel_rows = lax.psum_scatter(kernel_term.T, "dp", scatter_dimension=0, tiled=True)
    weight_rows, kernel_rows = lax.psum((weight_rows, kernel_rows), "grp")
    return (outputs, weight_rows, kernel_rows.T, gamma_sum, beta_sum)


def fold(value):
    total = value[0:8]
    for at in range(8, value.shape[0], 8):
        total = total + value[at : at + 8]
    return total


def row_sum(value):
    return jnp.sum(value, axis=0, keepdims=True)


def conv_body(len_hbm, off_hbm, acts_hbm, k_hbm, g_hbm, b_hbm, gp_ref, cv_ref, st_ref, ok_ref, in_ref, gb_ref,
              acc_ref, len_ref, off_ref, acts_ref, k_ref, sems, slot_sems):
    slots, frames, wide = acts_ref.shape
    blocks, _, rows, _ = gp_ref.shape
    taps = k_ref.shape[0]
    lead = taps // 2
    small = [
        pltpu.make_async_copy(source, target, sems.at[i])
        for i, (source, target) in enumerate(
            (
                (len_hbm, len_ref),
                (off_hbm, off_ref),
                (k_hbm, k_ref),
                (g_hbm, gb_ref.at[0]),
                (b_hbm, gb_ref.at[1]),
            )
        )
    ]

    def fetch(slot):
        return pltpu.make_async_copy(acts_hbm.at[slot], acts_ref.at[slot], slot_sems.at[slot])

    small[0].start()
    small[1].start()
    fetch(0).start()
    small[2].start()
    for slot in range(1, slots):
        fetch(slot).start()
    for copy in small[3:]:
        copy.start()
    acc_ref[...] = jnp.zeros_like(acc_ref)
    position = lax.broadcasted_iota(jnp.int32, (frames, LANES), 0)
    reach = lax.broadcasted_iota(jnp.int32, (taps, frames), 1)
    reach = reach - lax.broadcasted_iota(jnp.int32, (taps, frames), 0) + (lead - 1)
    for copy in small[:3]:
        copy.wait()

    def one(slot, carry):
        low = off_ref[slot]
        high = low + len_ref[slot]
        valid = ((position >= low) & (position < high)).astype(F32)
        ok_ref[slot] = valid
        in_ref[slot] = (
            (reach >= low) & (reach < high) & (reach >= 0) & (reach < frames)
        ).astype(F32)
        fetch(slot).wait()
        for block in range(blocks):
            cols = slice(block * LANES, (block + 1) * LANES)
            gate = slice(wide // 2 + block * LANES, wide // 2 + (block + 1) * LANES)
            left, right = acts_ref[slot, :, cols].astype(F32), acts_ref[slot, :, gate].astype(F32)
            gp_ref[block, slot, 0:lead, :] = jnp.zeros((lead, LANES), F32)
            gp_ref[block, slot, lead : lead + frames, :] = left * jax.nn.sigmoid(right) * valid
            tail = jnp.zeros((rows - lead - frames, LANES), F32)
            gp_ref[block, slot, lead + frames : rows, :] = tail
        for block in range(blocks):
            cols = slice(block * LANES, (block + 1) * LANES)
            total = gp_ref[block, slot, 1 : 1 + frames, :] * k_ref[0:1, cols]
            for tap in range(1, taps):
                lag = gp_ref[block, slot, 1 + tap : 1 + tap + frames, :]
                total = total + lag * k_ref[tap : tap + 1, cols]
            cv_ref[block, slot] = total
            masked = total * valid
            acc_ref[0, block] += fold(masked)
            acc_ref[1, block] += fold(masked * total)
        return carry

    lax.fori_loop(0, slots, one, 0)
    for copy in small[3:]:
        copy.wait()
    for block in range(blocks):
        cols = slice(block * LANES, (block + 1) * LANES)
        st_ref[0:1, cols] = row_sum(acc_ref[0, block])
        st_ref[1:2, cols] = row_sum(acc_ref[1, block])
    count = len_ref[0]
    for other in range(1, slots):
        count = count + len_ref[other]
    st_ref[:, blocks * LANES :] = jnp.full((2, LANES), count.astype(F32), F32)


def lag_sums(gp_ref, block, weights, taps, group, put):
    frames = weights(0).shape[0]
    slots = gp_ref.shape[1]
    for low in range(0, taps, group):
        sums = [None] * group
        for slot in range(slots):
            weight = weights(slot)
            for j in range(group):
                at = 1 + low + j
                term = fold(weight * gp_ref[block, slot, at : at + frames, :])
                sums[j] = term if sums[j] is None else sums[j] + term
        for j in range(group):
            put(low + j, row_sum(sums[j]))


def aux_body(start, ok_ref, in_ref, gp_ref, cv_ref, out_ref, wt_ref):
    _, slots, frames, _ = cv_ref.shape
    many, _, taps, _ = out_ref.shape
    lead = taps // 2

    def one(i, carry):
        block = start + i
        for slot in range(slots):
            wt_ref[slot] = cv_ref[block, slot] * ok_ref[slot]

        def put(k, row):
            out_ref[i, 0, k : k + 1, :] = row

        lag_sums(gp_ref, block, lambda slot: wt_ref[slot], taps, 16, put)
        total = jnp.zeros((taps, LANES), F32)
        for slot in range(slots):
            inside = in_ref[slot].astype(BF16)
            rest = gp_ref[block, slot, lead : lead + frames, :]
            for _ in range(3):
                part = rest.astype(BF16)
                rest = rest - part.astype(F32)
                total = total + jnp.dot(inside, part, preferred_element_type=F32)
        out_ref[i, 1] = total
        return carry

    lax.fori_loop(0, many, one, 0)


def back_body(start, cotan_hbm, w_hbm, out_ref, cotan_ref, w_ref, sems):
    blocks = out_ref.shape[0]
    fetch = pltpu.make_async_copy(cotan_hbm, cotan_ref, sems.at[blocks])
    fetch.start()
    copies = []
    for block in range(blocks):
        rows, source = pl.ds(block * LANES, LANES), pl.ds((start + block) * LANES, LANES)
        copies.append(pltpu.make_async_copy(w_hbm.at[source], w_ref.at[rows], sems.at[block]))
        copies[-1].start()
    fetch.wait()
    for block in range(blocks):
        copies[block].wait()
        rows = w_ref[block * LANES : (block + 1) * LANES, :]
        out_ref[block] = lax.dot_general(
            cotan_ref[...], rows, (((1,), (1,)), ((), ())), preferred_element_type=F32
        )


def scale_of(st_ref, block):
    width = st_ref.shape[1] - LANES
    cols = pl.ds(pl.multiple_of(block * LANES, LANES), LANES)
    count = st_ref[0:1, width:]
    mean = st_ref[0:1, cols] / count
    inv = lax.rsqrt(st_ref[1:2, cols] / count - mean * mean + 1e-05)
    return count, mean, inv


def hidden_body(st_ref, gb_ref, ok_ref, cv_ref, hid_ref):
    blocks, slots, frames, _ = cv_ref.shape

    def one(block, carry):
        _, mean, inv = scale_of(st_ref, block)
        gain, shift = gb_ref[0, pl.ds(block, 1), :], gb_ref[1, pl.ds(block, 1), :]
        for slot in range(slots):
            valid = ok_ref[slot]
            shifted = gain * ((cv_ref[block, slot] - mean) * inv) + shift
            hidden = shifted * jax.nn.sigmoid(shifted) * valid
            hid_ref[block, slot * frames : (slot + 1) * frames, :] = hidden.astype(BF16)
        return carry

    lax.fori_loop(0, blocks, one, 0)


def slope_body(st_ref, gb_ref, ok_ref, gp_ref, cv_ref, low_ref, high_ref, *refs):
    aux_refs, (give_ref, keep_ref, sl_ref) = refs[:-3], refs[-3:]
    blocks, slots, frames, _ = cv_ref.shape
    taps = aux_refs[0].shape[2]
    last = 3 * taps
    bit = lax.axis_index("dp") & 1

    def one(i, aux_ref, odd, q_ref):
        block = 2 * i + odd
        bk_ref, at = (low_ref, block) if 4 * i < blocks else (high_ref, block - blocks // 2)
        _, mean, inv = scale_of(st_ref, block)
        gain, shift = gb_ref[0, pl.ds(block, 1), :], gb_ref[1, pl.ds(block, 1), :]
        first = second = jnp.zeros((8, LANES), F32)
        for slot in range(slots):
            normed = (cv_ref[block, slot] - mean) * inv
            shifted = gain * normed + shift
            sig = jax.nn.sigmoid(shifted)
            back = bk_ref[at, slot * frames : (slot + 1) * frames, :]
            slope = back * sig * (1.0 + shifted * (1.0 - sig)) * ok_ref[slot]
            sl_ref[slot] = slope
            first, second = first + fold(slope), second + fold(slope * normed)

        def put(k, row):
            q_ref[i, k : k + 1, :] = row

        lag_sums(gp_ref, block, lambda slot: sl_ref[slot], taps, 16, put)
        q_ref[i, taps : 2 * taps, :] = aux_ref[odd, 1]
        q_ref[i, 2 * taps : last, :] = inv * (aux_ref[odd, 0] - mean * aux_ref[odd, 1])
        keep_ref[0, pl.ds(last + block, 1), :] = row_sum(first)
        keep_ref[0, pl.ds(last + blocks + block, 1), :] = row_sum(second)

    for i, aux_ref in enumerate(aux_refs):
        one(i, aux_ref, 1 - bit, give_ref)
        one(i, aux_ref, bit, keep_ref)
    for i in range(len(aux_refs)):
        give_ref[i, last:, :] = keep_ref[0, last:, :]
        if i:
            keep_ref[i, last:, :] = keep_ref[0, last:, :]


def halve_body(level, own_ref, recv_ref, give_ref, keep_ref):
    bit = (lax.axis_index("dp") >> level) & 1
    for i in range(give_ref.shape[0]):
        for odd, ref in ((1 - bit, give_ref), (bit, keep_ref)):
            ref[i] = own_ref[2 * i + odd] + recv_ref[2 * i + odd]


def out_body(hid_ref, w_ref, out_ref):
    blocks = hid_ref.shape[0]
    slots, frames, _ = out_ref.shape
    total = None
    for block in range(blocks):
        term = jnp.dot(
            hid_ref[block],
            w_ref[block * LANES : (block + 1) * LANES, :],
            preferred_element_type=F32,
        )
        total = term if total is None else total + term
    for slot in range(slots):
        out_ref[slot] = total[slot * frames : (slot + 1) * frames, :].astype(BF16)


def stage_body(*refs):
    pieces, out_ref, sems = refs[:-2], refs[-2], refs[-1]
    copies = [
        pltpu.make_async_copy(piece, out_ref.at[i], sems.at[i]) for i, piece in enumerate(pieces)
    ]
    for copy in copies:
        copy.start()
    for copy in copies:
        copy.wait()


def rows_body(masks, recv_hbm, staged_ref, *refs):
    pieces, (give_ref, keep_ref, recv_ref, held, sems) = refs[:-5], refs[-5:]
    me, half = lax.axis_index("dp"), lax.axis_index("grp") & 1
    copies = [
        pltpu.make_async_copy(piece, held.at[i], sems.at[i]) for i, piece in enumerate(pieces)
    ]
    fetch = pltpu.make_async_copy(recv_hbm, recv_ref, sems.at[len(pieces)])
    fetch.start()
    for copy in copies:
        copy.start()
    fetch.wait()
    early = staged_ref.shape[0]
    many = give_ref.shape[0]
    width = many * LANES
    give = pl.ds(pl.multiple_of((1 - half) * width, width), width)
    keep = pl.ds(pl.multiple_of(half * width, width), width)
    totals = [None, None]
    for i, mask in enumerate(masks):
        left = recv_ref[jnp.bitwise_xor(me, mask)]
        if i >= early:
            copies[i - early].wait()
        for j, cols in enumerate((give, keep)):
            right = staged_ref[i, :, cols] if i < early else held[i - early, :, cols]
            term = lax.dot_general(
                left, right, (((0,), (0,)), ((), ())), preferred_element_type=F32
            )
            totals[j] = term if totals[j] is None else totals[j] + term
    for total, ref in zip(totals, (give_ref, keep_ref)):
        for block in range(many):
            ref[block] = total[:, block * LANES : (block + 1) * LANES].astype(BF16)


def plus_body(own_ref, recv_ref, out_ref):
    out_ref[...] = own_ref[...] + recv_ref[...]


def add_body(own_ref, recv_ref, out_ref):
    out_ref[...] = (own_ref[...].astype(F32) + recv_ref[...].astype(F32)).astype(BF16)


def scale_body(st_ref, gb_ref, out_ref):
    me = lax.axis_index("dp")
    count, _, inv = scale_of(st_ref, me)
    out_ref[0:1, :] = gb_ref[0, pl.ds(me, 1), :] * inv
    out_ref[1:2, :] = count


def last_body(taps, own_ref, recv_ref, lags_ref, more_ref, sc_ref, rows_ref, gk_ref, gg_ref, gb_ref):
    me, half = lax.axis_index("dp"), lax.axis_index("grp") & 1
    many = own_ref.shape[0]
    for which, ref in ((half, own_ref), (1 - half, recv_ref)):
        for block in range(many):
            cols = pl.ds(pl.multiple_of((which * many + block) * LANES, LANES), LANES)
            rows_ref[:, cols] = ref[block].astype(F32)
    value = lags_ref[0] + more_ref[0]
    blocks = gb_ref.shape[0]
    gb_ref[...] = value[3 * taps : 3 * taps + blocks]
    gg_ref[...] = value[3 * taps + blocks : 3 * taps + 2 * blocks]
    count = sc_ref[1:2, :]
    mine = pl.ds(me, 1)
    gk_ref[...] = sc_ref[0:1, :] * (
        value[0:taps]
        - (gb_ref[mine, :] / count) * value[taps : 2 * taps]
        - (gg_ref[mine, :] / count) * value[2 * taps : 3 * taps]
    )


SMEM = pl.BlockSpec(memory_space=pltpu.SMEM)
VMEM = pl.BlockSpec(memory_space=pltpu.VMEM)
HBM = pl.BlockSpec(memory_space=pltpu.HBM)
ANY = pl.BlockSpec(memory_space=pl.ANY)


def in_hbm(value):
    return pltpu.with_memory_space_constraint(value, pltpu.HBM)


def call(body, shapes, scalars, args, flops=0, scratch=(), mib=8, **more):
    many = isinstance(shapes, list)
    moved = sum(a.size * a.dtype.itemsize for a in args)
    return pl.pallas_call(
        body,
        in_specs=more.pop("in_specs", None) or [SMEM] * len(scalars) + [VMEM] * len(args),
        out_specs=[VMEM] * len(shapes) if many else VMEM,
        out_shape=shapes,
        scratch_shapes=scratch,
        compiler_params=pltpu.CompilerParams(vmem_limit_bytes=mib << 20),
        cost_estimate=pl.CostEstimate(flops=flops, bytes_accessed=moved, transcendentals=0),
        **more,
    )(*scalars, *args)


def local_fast(n_dp, n_grp, acts, cotan, lengths, offsets, kernel, gamma, beta, w_out):
    slots, frames, wide = acts.shape
    width = wide // 2
    taps = kernel.shape[0]
    blocks = width // LANES
    tokens = slots * frames
    n_q = 3 * taps + 2 * blocks
    padded = 2 * (taps // 2) + frames
    shape = jax.ShapeDtypeStruct

    def swap(value, dp_mask, grp_mask):
        pairs = [
            (d * n_grp + g, (d ^ dp_mask) * n_grp + (g ^ grp_mask))
            for d in range(n_dp)
            for g in range(n_grp)
        ]
        return lax.ppermute(value, ("dp", "grp"), pairs)

    def plus(own, other):
        return call(plus_body, shape(own.shape, own.dtype), (), (own, other))

    dp_bits = [1 << i for i in range(n_dp.bit_length() - 1)]
    grp_bits = [1 << i for i in range(n_grp.bit_length() - 1)]
    gamma2, beta2 = gamma.reshape(blocks, LANES), beta.reshape(blocks, LANES)

    flat_cotan = cotan.reshape(tokens, width)
    pieces = [(0, flat_cotan)]
    for bit in dp_bits[1:] + dp_bits[:1]:
        pieces += [(m | bit, swap(v, bit, 0)) for m, v in pieces]
    late_bits = dp_bits[-1] | dp_bits[-2]
    pieces.sort(key=lambda piece: piece[0] & late_bits == late_bits)
    masks, values = tuple(m for m, _ in pieces), [v for _, v in pieces]
    early = sum(m & late_bits != late_bits for m in masks)

    gated, conv_out, stats, valid, inside, gains = call(
        conv_body,
        [
            shape((blocks, slots, padded, LANES), F32),
            shape((blocks, slots, frames, LANES), F32),
            shape((2, width + LANES), F32),
            shape((slots, frames, LANES), F32),
            shape((slots, taps, frames), F32),
            shape((2, blocks, LANES), F32),
        ],
        (),
        [in_hbm(v) for v in (lengths, offsets, acts, kernel, gamma2, beta2)],
        flops=4 * taps * tokens * width,
        scratch=[
            pltpu.VMEM((2, blocks, 8, LANES), F32),
            pltpu.SMEM((slots,), jnp.int32),
            pltpu.SMEM((slots,), jnp.int32),
            pltpu.VMEM(acts.shape, BF16),
            pltpu.VMEM(kernel.shape, F32),
            pltpu.SemaphoreType.DMA((5,)),
            pltpu.SemaphoreType.DMA((slots,)),
        ],
        in_specs=[HBM] * 6,
    )

    hops = [(1, m) for m in grp_bits] + [(m | 1, 0) for m in dp_bits[:0:-1]] + [(1, 0)]
    for dp_mask, grp_mask in hops:
        stats = plus(stats, swap(stats, dp_mask, grp_mask))

    back = [
        call(
            functools.partial(back_body, i * (blocks // 2)),
            shape((blocks // 2, tokens, LANES), F32),
            (),
            (in_hbm(flat_cotan), in_hbm(w_out)),
            flops=tokens * width * width,
            scratch=[
                pltpu.VMEM(flat_cotan.shape, BF16),
                pltpu.VMEM((width // 2, width), BF16),
                pltpu.SemaphoreType.DMA((blocks // 2 + 1,)),
            ],
            in_specs=[HBM] * 2,
        )
        for i in range(2)
    ]
    parts = blocks // 2
    each = 2
    aux = [
        call(
            functools.partial(aux_body, i * each),
            shape((each, 2, taps, LANES), F32),
            (),
            (valid, inside, gated, conv_out),
            flops=4 * taps * tokens * each * LANES,
            scratch=[pltpu.VMEM((slots, frames, LANES), F32)],
        )
        for i in range(parts)
    ]

    hidden = call(
        hidden_body, shape((blocks, tokens, LANES), BF16), (), (stats, gains, valid, conv_out)
    )
    received = lax.all_to_all(hidden, "dp", 0, 0, tiled=True)
    give, lags = call(
        slope_body,
        [shape((parts, n_q, LANES), F32)] * 2,
        (),
        (stats, gains, valid, gated, conv_out, *back, *aux),
        flops=4 * taps * tokens * width,
        scratch=[pltpu.VMEM((slots, frames, LANES), F32)],
    )
    for level in range(1, len(dp_bits)):
        came = swap(give, dp_bits[level - 1], 0)
        give, lags = call(
            functools.partial(halve_body, level),
            [shape((parts >> level, n_q, LANES), F32)] * 2,
            (),
            (lags, came),
        )
    lags = plus(lags, swap(give, dp_bits[-1], 0))
    scale = call(scale_body, shape((2, LANES), F32), (), (stats, gains))
    outputs = call(out_body, shape(cotan.shape, BF16), (), (hidden, w_out))

    half_shape = shape((blocks // 2, LANES, LANES), BF16)
    staged = call(
        stage_body,
        shape((early, tokens, width), BF16),
        (),
        values[:early],
        scratch=[pltpu.SemaphoreType.DMA((early,))],
        in_specs=[ANY] * early,
    )
    given, kept = call(
        functools.partial(rows_body, masks),
        [half_shape] * 2,
        (),
        (received, staged, *values[early:]),
        flops=2 * n_dp * tokens * LANES * width,
        scratch=[
            pltpu.VMEM(received.shape, BF16),
            pltpu.VMEM((n_dp - early, tokens, width), BF16),
            pltpu.SemaphoreType.DMA((n_dp - early + 1,)),
        ],
        in_specs=[ANY, VMEM] + [ANY] * (n_dp - early),
    )
    taken = swap(given, 0, 1)
    both = call(add_body, half_shape, (), (kept, taken))
    for mask in grp_bits[1:]:
        other = swap(both, 0, mask)
        both = call(add_body, half_shape, (), (both, other))
    rest = swap(both, 0, 1)

    for mask in grp_bits[:-1]:
        lags = plus(lags, swap(lags, 0, mask))
    more = swap(lags, 0, grp_bits[-1])
    weight_rows, grad_kernel, gamma_sum, beta_sum = call(
        functools.partial(last_body, taps),
        [
            shape((LANES, width), F32),
            shape((taps, LANES), F32),
            shape((blocks, LANES), F32),
            shape((blocks, LANES), F32),
        ],
        (),
        (both, rest, lags, more, scale),
    )
    return (outputs, weight_rows, grad_kernel, gamma_sum.reshape(width), beta_sum.reshape(width))


def solution(mesh):
    n_dp, n_grp = mesh.shape["dp"], mesh.shape["grp"]

    def fits(width, taps, frames):
        return (
            n_dp & (n_dp - 1) == 0
            and n_grp & (n_grp - 1) == 0
            and n_dp >= 4
            and n_grp >= 4
            and width == n_dp * LANES
            and taps % 16 == 0
            and frames % 16 == 0
            and n_dp % 8 == 0
        )

    def local(acts, cotan, lengths, offsets, kernel, gamma, beta, w_out):
        args = (acts, cotan, lengths, offsets, kernel, gamma, beta, w_out)
        if not fits(w_out.shape[0], kernel.shape[0], acts.shape[1]):
            return local_general(*args)
        return local_fast(n_dp, n_grp, *args)

    placed = (
        P(("dp", "grp"), None, None),
        P(("dp", "grp"), None, None),
        P(("dp", "grp")),
        P(("dp", "grp")),
        P(),
        P(),
        P(),
        P(),
    )
    return jax.shard_map(
        local,
        mesh=mesh,
        in_specs=placed,
        out_specs=(P(("dp", "grp"), None, None), P("dp", None), P(None, "dp"), P(), P()),
        check_vma=False,
    )
```

```python
import functools

import jax
import jax.numpy as jnp
from jax import lax
from jax.experimental import pallas as pl
from jax.experimental.pallas import tpu as pltpu
from jax.sharding import PartitionSpec as P


LANES = 128
F32 = jnp.float32
BF16 = jnp.bfloat16


def convolve(block_acts, block_len, block_off, kernel):
    taps = kernel.shape[0]
    model_width = kernel.shape[1]
    frame_count = block_acts.shape[1]
    position = jnp.arange(frame_count, dtype=jnp.int32)
    valid = (
        (position[None, :] >= block_off[:, None])
        & (position[None, :] < (block_off + block_len)[:, None])
    ).astype(jnp.float32)
    wide_acts = block_acts.astype(jnp.float32)
    gated = (
        wide_acts[..., :model_width]
        * jax.nn.sigmoid(wide_acts[..., model_width:])
        * valid[..., None]
    )
    padded = jnp.pad(gated, ((0, 0), (taps // 2 - 1, taps // 2), (0, 0)))
    conv_out = padded[:, 0:frame_count] * kernel[0]
    for tap in range(1, taps):
        conv_out = conv_out + padded[:, tap : tap + frame_count] * kernel[tap]
    return (valid, padded, conv_out)


def local_general(acts, cotan, lengths, offsets, kernel, gamma, beta, w_out):
    model_width = w_out.shape[0]
    taps = kernel.shape[0]
    valid, padded, conv_out = convolve(acts, lengths, offsets, kernel)
    masked = conv_out * valid[..., None]
    sum_first, sum_second, frame_total = lax.psum(
        (
            jnp.sum(masked, axis=(0, 1)),
            jnp.sum(masked * conv_out, axis=(0, 1)),
            jnp.sum(lengths).astype(jnp.float32),
        ),
        ("dp", "grp"),
    )
    mean_value = sum_first / frame_total
    inv_std = lax.rsqrt(sum_second / frame_total - mean_value * mean_value + 1e-05)
    normed = (conv_out - mean_value) * inv_std
    shifted = gamma * normed + beta
    sig_value = jax.nn.sigmoid(shifted)
    hidden = (shifted * sig_value * valid[..., None]).astype(jnp.bfloat16)
    flat_hidden = hidden.reshape(-1, model_width)
    flat_cotan = cotan.reshape(-1, model_width)
    outputs = (
        jnp.dot(flat_hidden, w_out, preferred_element_type=jnp.float32)
        .astype(jnp.bfloat16)
        .reshape(cotan.shape)
    )
    weight_rows = lax.psum_scatter(
        lax.dot_general(
            flat_hidden, flat_cotan, (((0,), (0,)), ((), ())), preferred_element_type=jnp.float32
        ),
        "dp",
        scatter_dimension=0,
        tiled=True,
    )
    back_hidden = lax.dot_general(
        flat_cotan, w_out, (((1,), (1,)), ((), ())), preferred_element_type=jnp.float32
    ).reshape(conv_out.shape)
    slope = back_hidden * sig_value * (1.0 + shifted * (1.0 - sig_value)) * valid[..., None]
    beta_sum, gamma_sum = lax.psum(
        (jnp.sum(slope, axis=(0, 1)), jnp.sum(slope * normed, axis=(0, 1))), ("dp", "grp")
    )
    conv_grad = (
        gamma
        * inv_std
        * (slope - beta_sum / frame_total - normed * gamma_sum / frame_total)
        * valid[..., None]
    )
    frame_count = conv_out.shape[1]
    kernel_term = jnp.stack(
        [
            jnp.sum(conv_grad * padded[:, tap : tap + frame_count], axis=(0, 1))
            for tap in range(taps)
        ],
        axis=0,
    )
    kernel_rows = lax.psum_scatter(kernel_term.T, "dp", scatter_dimension=0, tiled=True)
    weight_rows, kernel_rows = lax.psum((weight_rows, kernel_rows), "grp")
    return (outputs, weight_rows, kernel_rows.T, gamma_sum, beta_sum)


def fold(value):
    total = value[0:8]
    for at in range(8, value.shape[0], 8):
        total = total + value[at : at + 8]
    return total


def row_sum(value):
    return jnp.sum(value, axis=0, keepdims=True)


def conv_body(len_hbm, off_hbm, acts_hbm, k_hbm, g_hbm, b_hbm, w_hbm, c_hbm,
              gp_ref, cv_ref, st_ref, ok_ref, in_ref, gb_ref, bk_hbm,
              acc_ref, len_ref, off_ref, acts_ref, k_ref, w_ref, c_ref, bk_ref,
              sems, slot_sems, w_sems, bk_sems):
    slots, frames, wide = acts_ref.shape
    blocks = gp_ref.shape[0]
    taps = k_ref.shape[0]
    lead = taps // 2
    pitch = frames + lead
    pairs = (
        (len_hbm, len_ref),
        (off_hbm, off_ref),
        (k_hbm, k_ref),
        (c_hbm, c_ref),
        (g_hbm, gb_ref.at[0]),
        (b_hbm, gb_ref.at[1]),
    )
    small = [
        pltpu.make_async_copy(source, target, sems.at[i]) for i, (source, target) in enumerate(pairs)
    ]

    def fetch(slot):
        return pltpu.make_async_copy(acts_hbm.at[slot], acts_ref.at[slot], slot_sems.at[slot])

    def fetch_rows(block):
        rows = pl.ds(pl.multiple_of(block * LANES, LANES), LANES)
        return pltpu.make_async_copy(w_hbm.at[rows], w_ref.at[rows], w_sems.at[block])

    def put_back(block):
        return pltpu.make_async_copy(bk_ref.at[block], bk_hbm.at[block], bk_sems.at[block])

    small[0].start()
    small[1].start()
    fetch(0).start()
    small[2].start()
    small[3].start()
    for at in range(max(blocks, slots)):
        if at < blocks:
            fetch_rows(at).start()
        if 0 < at + 1 < slots:
            fetch(at + 1).start()
    small[4].start()
    small[5].start()
    acc_ref[...] = jnp.zeros_like(acc_ref)
    for block in range(blocks):
        for slot in range(slots + 1):
            gp_ref[block, slot * pitch : slot * pitch + lead, :] = jnp.zeros((lead, LANES), F32)
    position = lax.broadcasted_iota(jnp.int32, (frames, LANES), 0)
    reach = lax.broadcasted_iota(jnp.int32, (taps, frames), 1)
    reach = reach - lax.broadcasted_iota(jnp.int32, (taps, frames), 0) + (lead - 1)
    for copy in small[:4]:
        copy.wait()

    def back(block):
        rows = pl.ds(pl.multiple_of(block * LANES, LANES), LANES)
        bk_ref[block] = lax.dot_general(
            c_ref[...], w_ref[rows, :], (((1,), (1,)), ((), ())), preferred_element_type=F32
        )
        put_back(block).start()

    inside = min(slots, blocks)

    def one(slot, carry, also=False):
        low = off_ref[slot]
        high = low + len_ref[slot]
        fetch(slot).wait()
        if also:
            fetch_rows(slot).wait()
            back(slot)
        valid = ((position >= low) & (position < high)).astype(F32)
        ok_ref[slot] = valid
        in_ref[slot] = (
            (reach >= low) & (reach < high) & (reach >= 0) & (reach < frames)
        ).astype(F32).astype(BF16)
        first = pl.multiple_of(slot * pitch, 8)
        for block in range(blocks):
            cols = slice(block * LANES, (block + 1) * LANES)
            gate = slice(wide // 2 + block * LANES, wide // 2 + (block + 1) * LANES)
            left, right = acts_ref[slot, :, cols].astype(F32), acts_ref[slot, :, gate].astype(F32)
            rows = pl.ds(pl.multiple_of(first + lead, 8), frames)
            gp_ref[block, rows, :] = left * jax.nn.sigmoid(right) * valid
        for block in range(blocks):
            cols = slice(block * LANES, (block + 1) * LANES)
            total = gp_ref[block, pl.ds(first + 1, frames), :] * k_ref[0:1, cols]
            for tap in range(1, taps):
                lag = gp_ref[block, pl.ds(first + 1 + tap, frames), :]
                total = total + lag * k_ref[tap : tap + 1, cols]
            cv_ref[block, slot] = total
            masked = total * valid
            acc_ref[0, block] += fold(masked)
            acc_ref[1, block] += fold(masked * total)
        return carry

    lax.fori_loop(0, inside, functools.partial(one, also=True), 0)
    lax.fori_loop(inside, slots, one, 0)
    for block in range(inside, blocks):
        fetch_rows(block).wait()
        back(block)
    small[4].wait()
    small[5].wait()
    for block in range(blocks):
        put_back(block).wait()
    for block in range(blocks):
        cols = slice(block * LANES, (block + 1) * LANES)
        st_ref[0:1, cols] = row_sum(acc_ref[0, block])
        st_ref[1:2, cols] = row_sum(acc_ref[1, block])
    count = len_ref[0]
    for other in range(1, slots):
        count = count + len_ref[other]
    st_ref[:, blocks * LANES :] = jnp.full((2, LANES), count.astype(F32), F32)


def lag_sums(gp_ref, block, weights, slots, taps, group, put):
    frames = weights(0).shape[0]
    pitch = frames + taps // 2
    for low in range(0, taps, group):
        sums = [None] * group
        for slot in range(slots):
            weight = weights(slot)
            for j in range(group):
                at = slot * pitch + 1 + low + j
                term = fold(weight * gp_ref[block, at : at + frames, :])
                sums[j] = term if sums[j] is None else sums[j] + term
        for j in range(group):
            put(low + j, row_sum(sums[j]))


def aux_body(start, ok_ref, in_ref, gp_ref, cv_ref, out_ref, wt_ref):
    _, slots, frames, _ = cv_ref.shape
    many, _, taps, _ = out_ref.shape
    lead = taps // 2

    def one(i, carry):
        block = start + i
        for slot in range(slots):
            wt_ref[slot] = cv_ref[block, slot] * ok_ref[slot]

        def put(k, row):
            out_ref[i, 0, k : k + 1, :] = row

        lag_sums(gp_ref, block, lambda slot: wt_ref[slot], slots, taps, 16, put)
        total = jnp.zeros((taps, LANES), F32)
        for slot in range(slots):
            inside = in_ref[slot]
            first = slot * (frames + lead) + lead
            rest = gp_ref[block, first : first + frames, :]
            for _ in range(3):
                part = rest.astype(BF16)
                rest = rest - part.astype(F32)
                total = total + jnp.dot(inside, part, preferred_element_type=F32)
        out_ref[i, 1] = total
        return carry

    lax.fori_loop(0, many, one, 0)


def scale_of(st_ref, block):
    width = st_ref.shape[1] - LANES
    cols = pl.ds(pl.multiple_of(block * LANES, LANES), LANES)
    count = st_ref[0:1, width:]
    mean = st_ref[0:1, cols] / count
    inv = lax.rsqrt(st_ref[1:2, cols] / count - mean * mean + 1e-05)
    return count, mean, inv


def hidden_body(st_ref, gb_ref, ok_ref, cv_ref, hid_ref):
    blocks, slots, frames, _ = cv_ref.shape

    def one(block, carry):
        _, mean, inv = scale_of(st_ref, block)
        gain, shift = gb_ref[0, pl.ds(block, 1), :], gb_ref[1, pl.ds(block, 1), :]
        for slot in range(slots):
            valid = ok_ref[slot]
            shifted = gain * ((cv_ref[block, slot] - mean) * inv) + shift
            hidden = shifted * jax.nn.sigmoid(shifted) * valid
            hid_ref[block, slot * frames : (slot + 1) * frames, :] = hidden.astype(BF16)
        return carry

    lax.fori_loop(0, blocks, one, 0)


def slope_body(bk_hbm, st_ref, gb_ref, ok_ref, gp_ref, cv_ref, *refs):
    aux_refs, (give_ref, keep_ref, sl_ref, bk_ref, sem) = refs[:-5], refs[-5:]
    fetch = pltpu.make_async_copy(bk_hbm, bk_ref, sem)
    fetch.start()
    blocks, slots, frames, _ = cv_ref.shape
    taps = aux_refs[0].shape[2]
    last = 3 * taps
    bit = lax.axis_index("dp") & 1

    def one(i, aux_ref, odd, q_ref):
        block = 2 * i + odd
        _, mean, inv = scale_of(st_ref, block)
        gain, shift = gb_ref[0, pl.ds(block, 1), :], gb_ref[1, pl.ds(block, 1), :]
        first = second = jnp.zeros((8, LANES), F32)
        for slot in range(slots):
            normed = (cv_ref[block, slot] - mean) * inv
            shifted = gain * normed + shift
            sig = jax.nn.sigmoid(shifted)
            back = bk_ref[block, slot * frames : (slot + 1) * frames, :]
            slope = back * sig * (1.0 + shifted * (1.0 - sig)) * ok_ref[slot]
            sl_ref[slot] = slope
            first, second = first + fold(slope), second + fold(slope * normed)

        def put(k, row):
            q_ref[i, k : k + 1, :] = row

        lag_sums(gp_ref, block, lambda slot: sl_ref[slot], slots, taps, 16, put)
        q_ref[i, taps : 2 * taps, :] = aux_ref[odd, 1]
        q_ref[i, 2 * taps : last, :] = inv * (aux_ref[odd, 0] - mean * aux_ref[odd, 1])
        keep_ref[0, pl.ds(last + block, 1), :] = row_sum(first)
        keep_ref[0, pl.ds(last + blocks + block, 1), :] = row_sum(second)

    fetch.wait()
    for i, aux_ref in enumerate(aux_refs):
        one(i, aux_ref, 1 - bit, give_ref)
        one(i, aux_ref, bit, keep_ref)
    for i in range(len(aux_refs)):
        give_ref[i, last:, :] = keep_ref[0, last:, :]
        if i:
            keep_ref[i, last:, :] = keep_ref[0, last:, :]


def halve_body(level, own_ref, recv_ref, give_ref, keep_ref):
    bit = (lax.axis_index("dp") >> level) & 1
    for i in range(give_ref.shape[0]):
        for odd, ref in ((1 - bit, give_ref), (bit, keep_ref)):
            ref[i] = own_ref[2 * i + odd] + recv_ref[2 * i + odd]


def out_body(hid_hbm, w_hbm, out_ref, hid_ref, w_ref, sems):
    blocks = hid_ref.shape[0]
    slots, frames, _ = out_ref.shape
    copies = []
    for block in range(blocks):
        rows = pl.ds(block * LANES, LANES)
        copies.append(
            (
                pltpu.make_async_copy(hid_hbm.at[block], hid_ref.at[block], sems.at[0, block]),
                pltpu.make_async_copy(w_hbm.at[rows], w_ref.at[rows], sems.at[1, block]),
            )
        )
        copies[-1][0].start()
        copies[-1][1].start()
    total = None
    for block in range(blocks):
        copies[block][0].wait()
        copies[block][1].wait()
        rows = w_ref[block * LANES : (block + 1) * LANES, :]
        term = jnp.dot(hid_ref[block], rows, preferred_element_type=F32)
        total = term if total is None else total + term
    for slot in range(slots):
        out_ref[slot] = total[slot * frames : (slot + 1) * frames, :].astype(BF16)


def stage_body(*refs):
    pieces, out_ref, sems = refs[:-2], refs[-2], refs[-1]
    copies = [
        pltpu.make_async_copy(piece, out_ref.at[i], sems.at[i]) for i, piece in enumerate(pieces)
    ]
    for copy in copies:
        copy.start()
    for copy in copies:
        copy.wait()


def rows_body(masks, recv_hbm, staged_ref, *refs):
    pieces, (give_ref, keep_ref, recv_ref, held, sems) = refs[:-5], refs[-5:]
    me, half = lax.axis_index("dp"), lax.axis_index("grp") & 1
    copies = [
        pltpu.make_async_copy(piece, held.at[i], sems.at[i]) for i, piece in enumerate(pieces)
    ]
    fetch = pltpu.make_async_copy(recv_hbm, recv_ref, sems.at[len(pieces)])
    fetch.start()
    for copy in copies:
        copy.start()
    fetch.wait()
    early = staged_ref.shape[0]
    many = give_ref.shape[0]
    width = many * LANES
    give = pl.ds(pl.multiple_of((1 - half) * width, width), width)
    keep = pl.ds(pl.multiple_of(half * width, width), width)
    totals = [None, None]
    for i, mask in enumerate(masks):
        left = recv_ref[jnp.bitwise_xor(me, mask)]
        if i >= early:
            copies[i - early].wait()
        for j, cols in enumerate((give, keep)):
            right = staged_ref[i, :, cols] if i < early else held[i - early, :, cols]
            term = lax.dot_general(
                left, right, (((0,), (0,)), ((), ())), preferred_element_type=F32
            )
            totals[j] = term if totals[j] is None else totals[j] + term
    for total, ref in zip(totals, (give_ref, keep_ref)):
        for block in range(many):
            ref[block] = total[:, block * LANES : (block + 1) * LANES].astype(BF16)


def plus_body(own_ref, recv_ref, out_ref):
    out_ref[...] = own_ref[...] + recv_ref[...]


def add_body(own_ref, recv_ref, out_ref):
    out_ref[...] = (own_ref[...].astype(F32) + recv_ref[...].astype(F32)).astype(BF16)


def scale_body(st_ref, gb_ref, out_ref):
    me = lax.axis_index("dp")
    count, _, inv = scale_of(st_ref, me)
    out_ref[0:1, :] = gb_ref[0, pl.ds(me, 1), :] * inv
    out_ref[1:2, :] = count


def last_body(taps, own_ref, recv_ref, lags_ref, more_ref, sc_ref, rows_ref, gk_ref, gg_ref, gb_ref):
    me, half = lax.axis_index("dp"), lax.axis_index("grp") & 1
    many = own_ref.shape[0]
    for which, ref in ((half, own_ref), (1 - half, recv_ref)):
        for block in range(many):
            cols = pl.ds(pl.multiple_of((which * many + block) * LANES, LANES), LANES)
            rows_ref[:, cols] = ref[block].astype(F32)
    value = lags_ref[0] + more_ref[0]
    blocks = gb_ref.shape[0]
    gb_ref[...] = value[3 * taps : 3 * taps + blocks]
    gg_ref[...] = value[3 * taps + blocks : 3 * taps + 2 * blocks]
    count = sc_ref[1:2, :]
    mine = pl.ds(me, 1)
    gk_ref[...] = sc_ref[0:1, :] * (
        value[0:taps]
        - (gb_ref[mine, :] / count) * value[taps : 2 * taps]
        - (gg_ref[mine, :] / count) * value[2 * taps : 3 * taps]
    )


SMEM = pl.BlockSpec(memory_space=pltpu.SMEM)
VMEM = pl.BlockSpec(memory_space=pltpu.VMEM)
HBM = pl.BlockSpec(memory_space=pltpu.HBM)
ANY = pl.BlockSpec(memory_space=pl.ANY)


def in_hbm(value):
    return pltpu.with_memory_space_constraint(value, pltpu.HBM)


def call(body, shapes, scalars, args, flops=0, scratch=(), mib=8, here=False, **more):
    many = isinstance(shapes, list)
    if here:
        colour = lambda leaf: pltpu.VMEM(leaf.shape, leaf.dtype)
        shapes = [colour(leaf) for leaf in shapes] if many else colour(shapes)
    moved = sum(a.size * a.dtype.itemsize for a in args)
    return pl.pallas_call(
        body,
        in_specs=more.pop("in_specs", None) or [SMEM] * len(scalars) + [VMEM] * len(args),
        out_specs=more.pop("out_specs", None) or ([VMEM] * len(shapes) if many else VMEM),
        out_shape=shapes,
        scratch_shapes=scratch,
        compiler_params=pltpu.CompilerParams(vmem_limit_bytes=mib << 20),
        cost_estimate=pl.CostEstimate(flops=flops, bytes_accessed=moved, transcendentals=0),
        **more,
    )(*scalars, *args)


def local_fast(n_dp, n_grp, acts, cotan, lengths, offsets, kernel, gamma, beta, w_out):
    slots, frames, wide = acts.shape
    width = wide // 2
    taps = kernel.shape[0]
    blocks = width // LANES
    tokens = slots * frames
    n_q = 3 * taps + 2 * blocks
    padded = slots * (frames + taps // 2) + taps // 2
    shape = jax.ShapeDtypeStruct

    def swap(value, dp_mask, grp_mask):
        pairs = [
            (d * n_grp + g, (d ^ dp_mask) * n_grp + (g ^ grp_mask))
            for d in range(n_dp)
            for g in range(n_grp)
        ]
        return lax.ppermute(value, ("dp", "grp"), pairs)

    def plus(own, other):
        return call(plus_body, shape(own.shape, own.dtype), (), (own, other))

    dp_bits = [1 << i for i in range(n_dp.bit_length() - 1)]
    grp_bits = [1 << i for i in range(n_grp.bit_length() - 1)]
    gamma2, beta2 = gamma.reshape(blocks, LANES), beta.reshape(blocks, LANES)

    flat_cotan = cotan.reshape(tokens, width)
    pieces = [(0, flat_cotan)]
    for bit in dp_bits[1:] + dp_bits[:1]:
        pieces += [(m | bit, swap(v, bit, 0)) for m, v in pieces]
    late_bits = dp_bits[-1] | dp_bits[-2]
    pieces.sort(key=lambda piece: piece[0] & late_bits == late_bits)
    masks, values = tuple(m for m, _ in pieces), [v for _, v in pieces]
    early = n_dp * 5 // 8

    gated, conv_out, stats, valid, inside, gains, back = call(
        conv_body,
        [
            shape((blocks, padded, LANES), F32),
            shape((blocks, slots, frames, LANES), F32),
            shape((2, width + LANES), F32),
            shape((slots, frames, LANES), F32),
            shape((slots, taps, frames), BF16),
            shape((2, blocks, LANES), F32),
            pltpu.HBM((blocks, tokens, LANES), F32),
        ],
        (),
        [in_hbm(v) for v in (lengths, offsets, acts, kernel, gamma2, beta2, w_out, flat_cotan)],
        flops=4 * taps * tokens * width,
        scratch=[
            pltpu.VMEM((2, blocks, 8, LANES), F32),
            pltpu.SMEM((slots,), jnp.int32),
            pltpu.SMEM((slots,), jnp.int32),
            pltpu.VMEM(acts.shape, BF16),
            pltpu.VMEM(kernel.shape, F32),
            pltpu.VMEM(w_out.shape, BF16),
            pltpu.VMEM(flat_cotan.shape, BF16),
            pltpu.VMEM((blocks, tokens, LANES), F32),
            pltpu.SemaphoreType.DMA((6,)),
            pltpu.SemaphoreType.DMA((slots,)),
            pltpu.SemaphoreType.DMA((blocks,)),
            pltpu.SemaphoreType.DMA((blocks,)),
        ],
        out_specs=[VMEM] * 6 + [HBM],
        in_specs=[HBM] * 8,
    )

    hops = [(1, m) for m in grp_bits] + [(m | 1, 0) for m in dp_bits[:0:-1]] + [(1, 0)]
    for dp_mask, grp_mask in hops:
        stats = plus(stats, swap(stats, dp_mask, grp_mask))

    parts = blocks // 2
    each = 2
    aux = [
        call(
            functools.partial(aux_body, i * each),
            shape((each, 2, taps, LANES), F32),
            (),
            (valid, inside, gated, conv_out),
            flops=4 * taps * tokens * each * LANES,
            here=True,
            scratch=[pltpu.VMEM((slots, frames, LANES), F32)],
        )
        for i in range(parts)
    ]

    hidden = call(
        hidden_body, shape((blocks, tokens, LANES), BF16), (), (stats, gains, valid, conv_out)
    )
    received = lax.all_to_all(hidden, "dp", 0, 0, tiled=True)
    give, lags = call(
        slope_body,
        [shape((parts, n_q, LANES), F32)] * 2,
        (),
        (in_hbm(back), stats, gains, valid, gated, conv_out, *aux),
        flops=4 * taps * tokens * width,
        scratch=[
            pltpu.VMEM((slots, frames, LANES), F32),
            pltpu.VMEM(back.shape, F32),
            pltpu.SemaphoreType.DMA,
        ],
        in_specs=[HBM] + [VMEM] * (5 + parts),
        here=True,
    )
    for level in range(1, len(dp_bits)):
        came = swap(give, dp_bits[level - 1], 0)
        give, lags = call(
            functools.partial(halve_body, level),
            [shape((parts >> level, n_q, LANES), F32)] * 2,
            (),
            (lags, came),
            here=True,
        )
    lags = plus(lags, swap(give, dp_bits[-1], 0))
    scale = call(scale_body, shape((2, LANES), F32), (), (stats, gains))
    outputs = call(
        out_body,
        shape(cotan.shape, BF16),
        (),
        (in_hbm(hidden), in_hbm(w_out)),
        flops=2 * tokens * width * width,
        scratch=[
            pltpu.VMEM(hidden.shape, BF16),
            pltpu.VMEM(w_out.shape, BF16),
            pltpu.SemaphoreType.DMA((2, blocks)),
        ],
        in_specs=[HBM] * 2,
    )

    half_shape = shape((blocks // 2, LANES, LANES), BF16)
    staged = call(
        stage_body,
        shape((early, tokens, width), BF16),
        (),
        values[:early],
        scratch=[pltpu.SemaphoreType.DMA((early,))],
        in_specs=[ANY] * early,
    )
    given, kept = call(
        functools.partial(rows_body, masks),
        [half_shape] * 2,
        (),
        (received, staged, *values[early:]),
        flops=2 * n_dp * tokens * LANES * width,
        scratch=[
            pltpu.VMEM(received.shape, BF16),
            pltpu.VMEM((n_dp - early, tokens, width), BF16),
            pltpu.SemaphoreType.DMA((n_dp - early + 1,)),
        ],
        in_specs=[ANY, VMEM] + [ANY] * (n_dp - early),
    )
    taken = swap(given, 0, 1)
    both = call(add_body, half_shape, (), (kept, taken))
    for mask in grp_bits[1:]:
        other = swap(both, 0, mask)
        both = call(add_body, half_shape, (), (both, other))
    rest = swap(both, 0, 1)

    for mask in grp_bits[:-1]:
        lags = plus(lags, swap(lags, 0, mask))
    more = swap(lags, 0, grp_bits[-1])
    weight_rows, grad_kernel, gamma_sum, beta_sum = call(
        functools.partial(last_body, taps),
        [
            shape((LANES, width), F32),
            shape((taps, LANES), F32),
            shape((blocks, LANES), F32),
            shape((blocks, LANES), F32),
        ],
        (),
        (both, rest, lags, more, scale),
    )
    return (outputs, weight_rows, grad_kernel, gamma_sum.reshape(width), beta_sum.reshape(width))


def solution(mesh):
    n_dp, n_grp = mesh.shape["dp"], mesh.shape["grp"]

    def fits(width, taps, frames):
        return (
            n_dp & (n_dp - 1) == 0
            and n_grp & (n_grp - 1) == 0
            and n_dp >= 4
            and n_grp >= 4
            and width == n_dp * LANES
            and taps % 16 == 0
            and frames % 16 == 0
            and n_dp % 8 == 0
        )

    def local(acts, cotan, lengths, offsets, kernel, gamma, beta, w_out):
        args = (acts, cotan, lengths, offsets, kernel, gamma, beta, w_out)
        if not fits(w_out.shape[0], kernel.shape[0], acts.shape[1]):
            return local_general(*args)
        return local_fast(n_dp, n_grp, *args)

    placed = (
        P(("dp", "grp"), None, None),
        P(("dp", "grp"), None, None),
        P(("dp", "grp")),
        P(("dp", "grp")),
        P(),
        P(),
        P(),
        P(),
    )
    return jax.shard_map(
        local,
        mesh=mesh,
        in_specs=placed,
        out_specs=(P(("dp", "grp"), None, None), P("dp", None), P(None, "dp"), P(), P()),
        check_vma=False,
    )
```

```python
import functools

import jax
import jax.numpy as jnp
from jax import lax
from jax.experimental import pallas as pl
from jax.experimental.pallas import tpu as pltpu
from jax.sharding import PartitionSpec as P


LANES = 128
F32 = jnp.float32
BF16 = jnp.bfloat16


def convolve(block_acts, block_len, block_off, kernel):
    taps = kernel.shape[0]
    model_width = kernel.shape[1]
    frame_count = block_acts.shape[1]
    position = jnp.arange(frame_count, dtype=jnp.int32)
    valid = (
        (position[None, :] >= block_off[:, None])
        & (position[None, :] < (block_off + block_len)[:, None])
    ).astype(jnp.float32)
    wide_acts = block_acts.astype(jnp.float32)
    gated = (
        wide_acts[..., :model_width]
        * jax.nn.sigmoid(wide_acts[..., model_width:])
        * valid[..., None]
    )
    padded = jnp.pad(gated, ((0, 0), (taps // 2 - 1, taps // 2), (0, 0)))
    conv_out = padded[:, 0:frame_count] * kernel[0]
    for tap in range(1, taps):
        conv_out = conv_out + padded[:, tap : tap + frame_count] * kernel[tap]
    return (valid, padded, conv_out)


def local_general(acts, cotan, lengths, offsets, kernel, gamma, beta, w_out):
    model_width = w_out.shape[0]
    taps = kernel.shape[0]
    valid, padded, conv_out = convolve(acts, lengths, offsets, kernel)
    masked = conv_out * valid[..., None]
    sum_first, sum_second, frame_total = lax.psum(
        (
            jnp.sum(masked, axis=(0, 1)),
            jnp.sum(masked * conv_out, axis=(0, 1)),
            jnp.sum(lengths).astype(jnp.float32),
        ),
        ("dp", "grp"),
    )
    mean_value = sum_first / frame_total
    inv_std = lax.rsqrt(sum_second / frame_total - mean_value * mean_value + 1e-05)
    normed = (conv_out - mean_value) * inv_std
    shifted = gamma * normed + beta
    sig_value = jax.nn.sigmoid(shifted)
    hidden = (shifted * sig_value * valid[..., None]).astype(jnp.bfloat16)
    flat_hidden = hidden.reshape(-1, model_width)
    flat_cotan = cotan.reshape(-1, model_width)
    outputs = (
        jnp.dot(flat_hidden, w_out, preferred_element_type=jnp.float32)
        .astype(jnp.bfloat16)
        .reshape(cotan.shape)
    )
    weight_rows = lax.psum_scatter(
        lax.dot_general(
            flat_hidden, flat_cotan, (((0,), (0,)), ((), ())), preferred_element_type=jnp.float32
        ),
        "dp",
        scatter_dimension=0,
        tiled=True,
    )
    back_hidden = lax.dot_general(
        flat_cotan, w_out, (((1,), (1,)), ((), ())), preferred_element_type=jnp.float32
    ).reshape(conv_out.shape)
    slope = back_hidden * sig_value * (1.0 + shifted * (1.0 - sig_value)) * valid[..., None]
    beta_sum, gamma_sum = lax.psum(
        (jnp.sum(slope, axis=(0, 1)), jnp.sum(slope * normed, axis=(0, 1))), ("dp", "grp")
    )
    conv_grad = (
        gamma
        * inv_std
        * (slope - beta_sum / frame_total - normed * gamma_sum / frame_total)
        * valid[..., None]
    )
    frame_count = conv_out.shape[1]
    kernel_term = jnp.stack(
        [
            jnp.sum(conv_grad * padded[:, tap : tap + frame_count], axis=(0, 1))
            for tap in range(taps)
        ],
        axis=0,
    )
    kernel_rows = lax.psum_scatter(kernel_term.T, "dp", scatter_dimension=0, tiled=True)
    weight_rows, kernel_rows = lax.psum((weight_rows, kernel_rows), "grp")
    return (outputs, weight_rows, kernel_rows.T, gamma_sum, beta_sum)


def fold(value):
    total = value[0:8]
    for at in range(8, value.shape[0], 8):
        total = total + value[at : at + 8]
    return total


def row_sum(value):
    return jnp.sum(value, axis=0, keepdims=True)


def conv_body(len_hbm, off_hbm, acts_hbm, k_hbm, g_hbm, b_hbm, gp_ref, cv_ref, st_ref, ok_ref, in_ref, gb_ref,
              acc_ref, len_ref, off_ref, acts_ref, k_ref, sems, slot_sems):
    slots, frames, wide = acts_ref.shape
    blocks, _, rows, _ = gp_ref.shape
    taps = k_ref.shape[0]
    lead = taps // 2
    small = [
        pltpu.make_async_copy(source, target, sems.at[i])
        for i, (source, target) in enumerate(
            (
                (len_hbm, len_ref),
                (off_hbm, off_ref),
                (k_hbm, k_ref),
                (g_hbm, gb_ref.at[0]),
                (b_hbm, gb_ref.at[1]),
            )
        )
    ]

    def fetch(slot):
        return pltpu.make_async_copy(acts_hbm.at[slot], acts_ref.at[slot], slot_sems.at[slot])

    small[0].start()
    small[1].start()
    fetch(0).start()
    small[2].start()
    for slot in range(1, slots):
        fetch(slot).start()
    for copy in small[3:]:
        copy.start()
    acc_ref[...] = jnp.zeros_like(acc_ref)
    position = lax.broadcasted_iota(jnp.int32, (frames, LANES), 0)
    reach = lax.broadcasted_iota(jnp.int32, (taps, frames), 1)
    reach = reach - lax.broadcasted_iota(jnp.int32, (taps, frames), 0) + (lead - 1)
    for copy in small[:3]:
        copy.wait()

    def one(slot, carry):
        low = off_ref[slot]
        high = low + len_ref[slot]
        valid = ((position >= low) & (position < high)).astype(F32)
        ok_ref[slot] = valid
        in_ref[slot] = (
            (reach >= low) & (reach < high) & (reach >= 0) & (reach < frames)
        ).astype(F32)
        fetch(slot).wait()
        for block in range(blocks):
            cols = slice(block * LANES, (block + 1) * LANES)
            gate = slice(wide // 2 + block * LANES, wide // 2 + (block + 1) * LANES)
            left, right = acts_ref[slot, :, cols].astype(F32), acts_ref[slot, :, gate].astype(F32)
            gp_ref[block, slot, 0:lead, :] = jnp.zeros((lead, LANES), F32)
            gp_ref[block, slot, lead : lead + frames, :] = left * jax.nn.sigmoid(right) * valid
            tail = jnp.zeros((rows - lead - frames, LANES), F32)
            gp_ref[block, slot, lead + frames : rows, :] = tail
        for block in range(blocks):
            cols = slice(block * LANES, (block + 1) * LANES)
            total = gp_ref[block, slot, 1 : 1 + frames, :] * k_ref[0:1, cols]
            for tap in range(1, taps):
                lag = gp_ref[block, slot, 1 + tap : 1 + tap + frames, :]
                total = total + lag * k_ref[tap : tap + 1, cols]
            cv_ref[block, slot] = total
            masked = total * valid
            acc_ref[0, block] += fold(masked)
            acc_ref[1, block] += fold(masked * total)
        return carry

    lax.fori_loop(0, slots, one, 0)
    for copy in small[3:]:
        copy.wait()
    for block in range(blocks):
        cols = slice(block * LANES, (block + 1) * LANES)
        st_ref[0:1, cols] = row_sum(acc_ref[0, block])
        st_ref[1:2, cols] = row_sum(acc_ref[1, block])
    count = len_ref[0]
    for other in range(1, slots):
        count = count + len_ref[other]
    st_ref[:, blocks * LANES :] = jnp.full((2, LANES), count.astype(F32), F32)


def lag_sums(gp_ref, block, weights, taps, group, put):
    frames = weights(0).shape[0]
    slots = gp_ref.shape[1]
    for low in range(0, taps, group):
        sums = [None] * group
        for slot in range(slots):
            weight = weights(slot)
            for j in range(group):
                at = 1 + low + j
                term = fold(weight * gp_ref[block, slot, at : at + frames, :])
                sums[j] = term if sums[j] is None else sums[j] + term
        for j in range(group):
            put(low + j, row_sum(sums[j]))


def aux_body(start, ok_ref, in_ref, gp_ref, cv_ref, out_ref, wt_ref):
    _, slots, frames, _ = cv_ref.shape
    many, _, taps, _ = out_ref.shape
    lead = taps // 2

    def one(i, carry):
        block = start + i
        for slot in range(slots):
            wt_ref[slot] = cv_ref[block, slot] * ok_ref[slot]

        def put(k, row):
            out_ref[i, 0, k : k + 1, :] = row

        lag_sums(gp_ref, block, lambda slot: wt_ref[slot], taps, 16, put)
        total = jnp.zeros((taps, LANES), F32)
        for slot in range(slots):
            inside = in_ref[slot].astype(BF16)
            rest = gp_ref[block, slot, lead : lead + frames, :]
            for _ in range(3):
                part = rest.astype(BF16)
                rest = rest - part.astype(F32)
                total = total + jnp.dot(inside, part, preferred_element_type=F32)
        out_ref[i, 1] = total
        return carry

    lax.fori_loop(0, many, one, 0)


def back_body(cotan_hbm, w_hbm, out_ref, cotan_ref, w_ref, sems):
    blocks = out_ref.shape[0]
    fetch = pltpu.make_async_copy(cotan_hbm, cotan_ref, sems.at[blocks])
    fetch.start()
    copies = []
    for block in range(blocks):
        rows = pl.ds(block * LANES, LANES)
        copies.append(pltpu.make_async_copy(w_hbm.at[rows], w_ref.at[rows], sems.at[block]))
        copies[-1].start()
    fetch.wait()
    for block in range(blocks):
        copies[block].wait()
        rows = w_ref[block * LANES : (block + 1) * LANES, :]
        out_ref[block] = lax.dot_general(
            cotan_ref[...], rows, (((1,), (1,)), ((), ())), preferred_element_type=F32
        )


def scale_of(st_ref, block):
    width = st_ref.shape[1] - LANES
    cols = pl.ds(pl.multiple_of(block * LANES, LANES), LANES)
    count = st_ref[0:1, width:]
    mean = st_ref[0:1, cols] / count
    inv = lax.rsqrt(st_ref[1:2, cols] / count - mean * mean + 1e-05)
    return count, mean, inv


def hidden_body(st_ref, gb_ref, ok_ref, cv_ref, hid_ref):
    blocks, slots, frames, _ = cv_ref.shape

    def one(block, carry):
        _, mean, inv = scale_of(st_ref, block)
        gain, shift = gb_ref[0, pl.ds(block, 1), :], gb_ref[1, pl.ds(block, 1), :]
        for slot in range(slots):
            valid = ok_ref[slot]
            shifted = gain * ((cv_ref[block, slot] - mean) * inv) + shift
            hidden = shifted * jax.nn.sigmoid(shifted) * valid
            hid_ref[block, slot * frames : (slot + 1) * frames, :] = hidden.astype(BF16)
        return carry

    lax.fori_loop(0, blocks, one, 0)


def slope_body(st_ref, gb_ref, ok_ref, gp_ref, cv_ref, bk_ref, *refs):
    aux_refs, (give_ref, keep_ref, sl_ref) = refs[:-3], refs[-3:]
    blocks, slots, frames, _ = cv_ref.shape
    taps = aux_refs[0].shape[2]
    last = 3 * taps
    bit = lax.axis_index("dp") & 1

    def one(i, aux_ref, odd, q_ref):
        block = 2 * i + odd
        _, mean, inv = scale_of(st_ref, block)
        gain, shift = gb_ref[0, pl.ds(block, 1), :], gb_ref[1, pl.ds(block, 1), :]
        first = second = jnp.zeros((8, LANES), F32)
        for slot in range(slots):
            normed = (cv_ref[block, slot] - mean) * inv
            shifted = gain * normed + shift
            sig = jax.nn.sigmoid(shifted)
            back = bk_ref[block, slot * frames : (slot + 1) * frames, :]
            slope = back * sig * (1.0 + shifted * (1.0 - sig)) * ok_ref[slot]
            sl_ref[slot] = slope
            first, second = first + fold(slope), second + fold(slope * normed)

        def put(k, row):
            q_ref[i, k : k + 1, :] = row

        lag_sums(gp_ref, block, lambda slot: sl_ref[slot], taps, 16, put)
        q_ref[i, taps : 2 * taps, :] = aux_ref[odd, 1]
        q_ref[i, 2 * taps : last, :] = inv * (aux_ref[odd, 0] - mean * aux_ref[odd, 1])
        keep_ref[0, pl.ds(last + block, 1), :] = row_sum(first)
        keep_ref[0, pl.ds(last + blocks + block, 1), :] = row_sum(second)

    for i, aux_ref in enumerate(aux_refs):
        one(i, aux_ref, 1 - bit, give_ref)
        one(i, aux_ref, bit, keep_ref)
    for i in range(len(aux_refs)):
        give_ref[i, last:, :] = keep_ref[0, last:, :]
        if i:
            keep_ref[i, last:, :] = keep_ref[0, last:, :]


def halve_body(level, own_ref, recv_ref, give_ref, keep_ref):
    bit = (lax.axis_index("dp") >> level) & 1
    for i in range(give_ref.shape[0]):
        for odd, ref in ((1 - bit, give_ref), (bit, keep_ref)):
            ref[i] = own_ref[2 * i + odd] + recv_ref[2 * i + odd]


def out_body(hid_ref, w_ref, out_ref):
    blocks = hid_ref.shape[0]
    slots, frames, _ = out_ref.shape
    total = None
    for block in range(blocks):
        term = jnp.dot(
            hid_ref[block],
            w_ref[block * LANES : (block + 1) * LANES, :],
            preferred_element_type=F32,
        )
        total = term if total is None else total + term
    for slot in range(slots):
        out_ref[slot] = total[slot * frames : (slot + 1) * frames, :].astype(BF16)


def stage_body(*refs):
    pieces, out_ref, sems = refs[:-2], refs[-2], refs[-1]
    copies = [
        pltpu.make_async_copy(piece, out_ref.at[i], sems.at[i]) for i, piece in enumerate(pieces)
    ]
    for copy in copies:
        copy.start()
    for copy in copies:
        copy.wait()


def rows_body(masks, recv_hbm, staged_ref, *refs):
    pieces, (give_ref, keep_ref, recv_ref, held, sems) = refs[:-5], refs[-5:]
    me, half = lax.axis_index("dp"), lax.axis_index("grp") & 1
    copies = [
        pltpu.make_async_copy(piece, held.at[i], sems.at[i]) for i, piece in enumerate(pieces)
    ]
    fetch = pltpu.make_async_copy(recv_hbm, recv_ref, sems.at[len(pieces)])
    fetch.start()
    for copy in copies:
        copy.start()
    fetch.wait()
    early = staged_ref.shape[0]
    many = give_ref.shape[0]
    width = many * LANES
    give = pl.ds(pl.multiple_of((1 - half) * width, width), width)
    keep = pl.ds(pl.multiple_of(half * width, width), width)
    totals = [None, None]
    for i, mask in enumerate(masks):
        left = recv_ref[jnp.bitwise_xor(me, mask)]
        if i >= early:
            copies[i - early].wait()
        for j, cols in enumerate((give, keep)):
            right = staged_ref[i, :, cols] if i < early else held[i - early, :, cols]
            term = lax.dot_general(
                left, right, (((0,), (0,)), ((), ())), preferred_element_type=F32
            )
            totals[j] = term if totals[j] is None else totals[j] + term
    for total, ref in zip(totals, (give_ref, keep_ref)):
        for block in range(many):
            ref[block] = total[:, block * LANES : (block + 1) * LANES].astype(BF16)


def plus_body(own_ref, recv_ref, out_ref):
    out_ref[...] = own_ref[...] + recv_ref[...]


def add_body(own_ref, recv_ref, out_ref):
    out_ref[...] = (own_ref[...].astype(F32) + recv_ref[...].astype(F32)).astype(BF16)


def scale_body(st_ref, gb_ref, out_ref):
    me = lax.axis_index("dp")
    count, _, inv = scale_of(st_ref, me)
    out_ref[0:1, :] = gb_ref[0, pl.ds(me, 1), :] * inv
    out_ref[1:2, :] = count


def last_body(taps, own_ref, recv_ref, lags_ref, more_ref, sc_ref, rows_ref, gk_ref, gg_ref, gb_ref):
    me, half = lax.axis_index("dp"), lax.axis_index("grp") & 1
    many = own_ref.shape[0]
    for which, ref in ((half, own_ref), (1 - half, recv_ref)):
        for block in range(many):
            cols = pl.ds(pl.multiple_of((which * many + block) * LANES, LANES), LANES)
            rows_ref[:, cols] = ref[block].astype(F32)
    value = lags_ref[0] + more_ref[0]
    blocks = gb_ref.shape[0]
    gb_ref[...] = value[3 * taps : 3 * taps + blocks]
    gg_ref[...] = value[3 * taps + blocks : 3 * taps + 2 * blocks]
    count = sc_ref[1:2, :]
    mine = pl.ds(me, 1)
    gk_ref[...] = sc_ref[0:1, :] * (
        value[0:taps]
        - (gb_ref[mine, :] / count) * value[taps : 2 * taps]
        - (gg_ref[mine, :] / count) * value[2 * taps : 3 * taps]
    )


SMEM = pl.BlockSpec(memory_space=pltpu.SMEM)
VMEM = pl.BlockSpec(memory_space=pltpu.VMEM)
HBM = pl.BlockSpec(memory_space=pltpu.HBM)
ANY = pl.BlockSpec(memory_space=pl.ANY)


def in_hbm(value):
    return pltpu.with_memory_space_constraint(value, pltpu.HBM)


def call(body, shapes, scalars, args, flops=0, scratch=(), mib=8, **more):
    many = isinstance(shapes, list)
    moved = sum(a.size * a.dtype.itemsize for a in args)
    return pl.pallas_call(
        body,
        in_specs=more.pop("in_specs", None) or [SMEM] * len(scalars) + [VMEM] * len(args),
        out_specs=[VMEM] * len(shapes) if many else VMEM,
        out_shape=shapes,
        scratch_shapes=scratch,
        compiler_params=pltpu.CompilerParams(vmem_limit_bytes=mib << 20),
        cost_estimate=pl.CostEstimate(flops=flops, bytes_accessed=moved, transcendentals=0),
        **more,
    )(*scalars, *args)


def local_fast(n_dp, n_grp, acts, cotan, lengths, offsets, kernel, gamma, beta, w_out):
    slots, frames, wide = acts.shape
    width = wide // 2
    taps = kernel.shape[0]
    blocks = width // LANES
    tokens = slots * frames
    n_q = 3 * taps + 2 * blocks
    padded = 2 * (taps // 2) + frames
    shape = jax.ShapeDtypeStruct

    def swap(value, dp_mask, grp_mask):
        pairs = [
            (d * n_grp + g, (d ^ dp_mask) * n_grp + (g ^ grp_mask))
            for d in range(n_dp)
            for g in range(n_grp)
        ]
        return lax.ppermute(value, ("dp", "grp"), pairs)

    def plus(own, other):
        return call(plus_body, shape(own.shape, own.dtype), (), (own, other))

    dp_bits = [1 << i for i in range(n_dp.bit_length() - 1)]
    grp_bits = [1 << i for i in range(n_grp.bit_length() - 1)]
    gamma2, beta2 = gamma.reshape(blocks, LANES), beta.reshape(blocks, LANES)

    flat_cotan = cotan.reshape(tokens, width)
    pieces = [(0, flat_cotan)]
    for bit in dp_bits[1:] + dp_bits[:1]:
        pieces += [(m | bit, swap(v, bit, 0)) for m, v in pieces]
    late_bits = dp_bits[-1] | dp_bits[-2]
    pieces.sort(key=lambda piece: piece[0] & late_bits == late_bits)
    masks, values = tuple(m for m, _ in pieces), [v for _, v in pieces]
    early = sum(m & late_bits != late_bits for m in masks)

    gated, conv_out, stats, valid, inside, gains = call(
        conv_body,
        [
            shape((blocks, slots, padded, LANES), F32),
            shape((blocks, slots, frames, LANES), F32),
            shape((2, width + LANES), F32),
            shape((slots, frames, LANES), F32),
            shape((slots, taps, frames), F32),
            shape((2, blocks, LANES), F32),
        ],
        (),
        [in_hbm(v) for v in (lengths, offsets, acts, kernel, gamma2, beta2)],
        flops=4 * taps * tokens * width,
        scratch=[
            pltpu.VMEM((2, blocks, 8, LANES), F32),
            pltpu.SMEM((slots,), jnp.int32),
            pltpu.SMEM((slots,), jnp.int32),
            pltpu.VMEM(acts.shape, BF16),
            pltpu.VMEM(kernel.shape, F32),
            pltpu.SemaphoreType.DMA((5,)),
            pltpu.SemaphoreType.DMA((slots,)),
        ],
        in_specs=[HBM] * 6,
    )

    hops = [(1, m) for m in grp_bits] + [(m | 1, 0) for m in dp_bits[1:]] + [(1, 0)]
    for dp_mask, grp_mask in hops:
        stats = plus(stats, swap(stats, dp_mask, grp_mask))

    back = call(
        back_body,
        shape((blocks, tokens, LANES), F32),
        (),
        (in_hbm(flat_cotan), in_hbm(w_out)),
        flops=2 * tokens * width * width,
        scratch=[
            pltpu.VMEM(flat_cotan.shape, BF16),
            pltpu.VMEM(w_out.shape, BF16),
            pltpu.SemaphoreType.DMA((blocks + 1,)),
        ],
        in_specs=[HBM] * 2,
    )
    parts = blocks // 2
    each = 2
    aux = [
        call(
            functools.partial(aux_body, i * each),
            shape((each, 2, taps, LANES), F32),
            (),
            (valid, inside, gated, conv_out),
            flops=4 * taps * tokens * each * LANES,
            scratch=[pltpu.VMEM((slots, frames, LANES), F32)],
        )
        for i in range(parts)
    ]

    hidden = call(
        hidden_body, shape((blocks, tokens, LANES), BF16), (), (stats, gains, valid, conv_out)
    )
    received = lax.all_to_all(hidden, "dp", 0, 0, tiled=True)
    give, lags = call(
        slope_body,
        [shape((parts, n_q, LANES), F32)] * 2,
        (),
        (stats, gains, valid, gated, conv_out, back, *aux),
        flops=4 * taps * tokens * width,
        scratch=[pltpu.VMEM((slots, frames, LANES), F32)],
    )
    for level in range(1, len(dp_bits)):
        came = swap(give, dp_bits[level - 1], 0)
        give, lags = call(
            functools.partial(halve_body, level),
            [shape((parts >> level, n_q, LANES), F32)] * 2,
            (),
            (lags, came),
        )
    lags = plus(lags, swap(give, dp_bits[-1], 0))
    scale = call(scale_body, shape((2, LANES), F32), (), (stats, gains))
    outputs = call(out_body, shape(cotan.shape, BF16), (), (hidden, w_out))

    half_shape = shape((blocks // 2, LANES, LANES), BF16)
    staged = call(
        stage_body,
        shape((early, tokens, width), BF16),
        (),
        values[:early],
        scratch=[pltpu.SemaphoreType.DMA((early,))],
        in_specs=[ANY] * early,
    )
    given, kept = call(
        functools.partial(rows_body, masks),
        [half_shape] * 2,
        (),
        (received, staged, *values[early:]),
        flops=2 * n_dp * tokens * LANES * width,
        scratch=[
            pltpu.VMEM(received.shape, BF16),
            pltpu.VMEM((n_dp - early, tokens, width), BF16),
            pltpu.SemaphoreType.DMA((n_dp - early + 1,)),
        ],
        in_specs=[ANY, VMEM] + [ANY] * (n_dp - early),
    )
    taken = swap(given, 0, 1)
    both = call(add_body, half_shape, (), (kept, taken))
    for mask in grp_bits[1:]:
        other = swap(both, 0, mask)
        both = call(add_body, half_shape, (), (both, other))
    rest = swap(both, 0, 1)

    for mask in grp_bits[:-1]:
        lags = plus(lags, swap(lags, 0, mask))
    more = swap(lags, 0, grp_bits[-1])
    weight_rows, grad_kernel, gamma_sum, beta_sum = call(
        functools.partial(last_body, taps),
        [
            shape((LANES, width), F32),
            shape((taps, LANES), F32),
            shape((blocks, LANES), F32),
            shape((blocks, LANES), F32),
        ],
        (),
        (both, rest, lags, more, scale),
    )
    return (outputs, weight_rows, grad_kernel, gamma_sum.reshape(width), beta_sum.reshape(width))


def solution(mesh):
    n_dp, n_grp = mesh.shape["dp"], mesh.shape["grp"]

    def fits(width, taps, frames):
        return (
            n_dp & (n_dp - 1) == 0
            and n_grp & (n_grp - 1) == 0
            and n_dp >= 4
            and n_grp >= 4
            and width == n_dp * LANES
            and taps % 16 == 0
            and frames % 16 == 0
            and n_dp % 8 == 0
        )

    def local(acts, cotan, lengths, offsets, kernel, gamma, beta, w_out):
        args = (acts, cotan, lengths, offsets, kernel, gamma, beta, w_out)
        if not fits(w_out.shape[0], kernel.shape[0], acts.shape[1]):
            return local_general(*args)
        return local_fast(n_dp, n_grp, *args)

    placed = (
        P(("dp", "grp"), None, None),
        P(("dp", "grp"), None, None),
        P(("dp", "grp")),
        P(("dp", "grp")),
        P(),
        P(),
        P(),
        P(),
    )
    return jax.shard_map(
        local,
        mesh=mesh,
        in_specs=placed,
        out_specs=(P(("dp", "grp"), None, None), P("dp", None), P(None, "dp"), P(), P()),
        check_vma=False,
    )
```

```python
import functools

import jax
import jax.numpy as jnp
from jax import lax
from jax.experimental import pallas as pl
from jax.experimental.pallas import tpu as pltpu
from jax.sharding import PartitionSpec as P


LANES = 128
F32 = jnp.float32
BF16 = jnp.bfloat16


def convolve(block_acts, block_len, block_off, kernel):
    taps = kernel.shape[0]
    model_width = kernel.shape[1]
    frame_count = block_acts.shape[1]
    position = jnp.arange(frame_count, dtype=jnp.int32)
    valid = (
        (position[None, :] >= block_off[:, None])
        & (position[None, :] < (block_off + block_len)[:, None])
    ).astype(jnp.float32)
    wide_acts = block_acts.astype(jnp.float32)
    gated = (
        wide_acts[..., :model_width]
        * jax.nn.sigmoid(wide_acts[..., model_width:])
        * valid[..., None]
    )
    padded = jnp.pad(gated, ((0, 0), (taps // 2 - 1, taps // 2), (0, 0)))
    conv_out = padded[:, 0:frame_count] * kernel[0]
    for tap in range(1, taps):
        conv_out = conv_out + padded[:, tap : tap + frame_count] * kernel[tap]
    return (valid, padded, conv_out)


def local_general(acts, cotan, lengths, offsets, kernel, gamma, beta, w_out):
    model_width = w_out.shape[0]
    taps = kernel.shape[0]
    valid, padded, conv_out = convolve(acts, lengths, offsets, kernel)
    masked = conv_out * valid[..., None]
    sum_first, sum_second, frame_total = lax.psum(
        (
            jnp.sum(masked, axis=(0, 1)),
            jnp.sum(masked * conv_out, axis=(0, 1)),
            jnp.sum(lengths).astype(jnp.float32),
        ),
        ("dp", "grp"),
    )
    mean_value = sum_first / frame_total
    inv_std = lax.rsqrt(sum_second / frame_total - mean_value * mean_value + 1e-05)
    normed = (conv_out - mean_value) * inv_std
    shifted = gamma * normed + beta
    sig_value = jax.nn.sigmoid(shifted)
    hidden = (shifted * sig_value * valid[..., None]).astype(jnp.bfloat16)
    flat_hidden = hidden.reshape(-1, model_width)
    flat_cotan = cotan.reshape(-1, model_width)
    outputs = (
        jnp.dot(flat_hidden, w_out, preferred_element_type=jnp.float32)
        .astype(jnp.bfloat16)
        .reshape(cotan.shape)
    )
    weight_rows = lax.psum_scatter(
        lax.dot_general(
            flat_hidden, flat_cotan, (((0,), (0,)), ((), ())), preferred_element_type=jnp.float32
        ),
        "dp",
        scatter_dimension=0,
        tiled=True,
    )
    back_hidden = lax.dot_general(
        flat_cotan, w_out, (((1,), (1,)), ((), ())), preferred_element_type=jnp.float32
    ).reshape(conv_out.shape)
    slope = back_hidden * sig_value * (1.0 + shifted * (1.0 - sig_value)) * valid[..., None]
    beta_sum, gamma_sum = lax.psum(
        (jnp.sum(slope, axis=(0, 1)), jnp.sum(slope * normed, axis=(0, 1))), ("dp", "grp")
    )
    conv_grad = (
        gamma
        * inv_std
        * (slope - beta_sum / frame_total - normed * gamma_sum / frame_total)
        * valid[..., None]
    )
    frame_count = conv_out.shape[1]
    kernel_term = jnp.stack(
        [
            jnp.sum(conv_grad * padded[:, tap : tap + frame_count], axis=(0, 1))
            for tap in range(taps)
        ],
        axis=0,
    )
    kernel_rows = lax.psum_scatter(kernel_term.T, "dp", scatter_dimension=0, tiled=True)
    weight_rows, kernel_rows = lax.psum((weight_rows, kernel_rows), "grp")
    return (outputs, weight_rows, kernel_rows.T, gamma_sum, beta_sum)


def fold(value):
    total = value[0:8]
    for at in range(8, value.shape[0], 8):
        total = total + value[at : at + 8]
    return total


def row_sum(value):
    return jnp.sum(value, axis=0, keepdims=True)


def conv_body(len_hbm, off_hbm, acts_hbm, k_hbm, g_hbm, b_hbm, gp_ref, cv_ref, st_ref, ok_ref, in_ref, gb_ref,
              acc_ref, len_ref, off_ref, acts_ref, k_ref, sems, slot_sems):
    slots, frames, wide = acts_ref.shape
    blocks, _, rows, _ = gp_ref.shape
    taps = k_ref.shape[0]
    lead = taps // 2
    small = [
        pltpu.make_async_copy(source, target, sems.at[i])
        for i, (source, target) in enumerate(
            (
                (len_hbm, len_ref),
                (off_hbm, off_ref),
                (k_hbm, k_ref),
                (g_hbm, gb_ref.at[0]),
                (b_hbm, gb_ref.at[1]),
            )
        )
    ]

    def fetch(slot):
        return pltpu.make_async_copy(acts_hbm.at[slot], acts_ref.at[slot], slot_sems.at[slot])

    small[0].start()
    small[1].start()
    fetch(0).start()
    small[2].start()
    for slot in range(1, slots):
        fetch(slot).start()
    for copy in small[3:]:
        copy.start()
    acc_ref[...] = jnp.zeros_like(acc_ref)
    position = lax.broadcasted_iota(jnp.int32, (frames, LANES), 0)
    reach = lax.broadcasted_iota(jnp.int32, (taps, frames), 1)
    reach = reach - lax.broadcasted_iota(jnp.int32, (taps, frames), 0) + (lead - 1)
    for copy in small[:3]:
        copy.wait()

    def one(slot, carry):
        low = off_ref[slot]
        high = low + len_ref[slot]
        valid = ((position >= low) & (position < high)).astype(F32)
        ok_ref[slot] = valid
        in_ref[slot] = (
            (reach >= low) & (reach < high) & (reach >= 0) & (reach < frames)
        ).astype(F32)
        fetch(slot).wait()
        for block in range(blocks):
            cols = slice(block * LANES, (block + 1) * LANES)
            gate = slice(wide // 2 + block * LANES, wide // 2 + (block + 1) * LANES)
            left, right = acts_ref[slot, :, cols].astype(F32), acts_ref[slot, :, gate].astype(F32)
            gp_ref[block, slot, 0:lead, :] = jnp.zeros((lead, LANES), F32)
            gp_ref[block, slot, lead : lead + frames, :] = left * jax.nn.sigmoid(right) * valid
            tail = jnp.zeros((rows - lead - frames, LANES), F32)
            gp_ref[block, slot, lead + frames : rows, :] = tail
        for block in range(blocks):
            cols = slice(block * LANES, (block + 1) * LANES)
            total = gp_ref[block, slot, 1 : 1 + frames, :] * k_ref[0:1, cols]
            for tap in range(1, taps):
                lag = gp_ref[block, slot, 1 + tap : 1 + tap + frames, :]
                total = total + lag * k_ref[tap : tap + 1, cols]
            cv_ref[block, slot] = total
            masked = total * valid
            acc_ref[0, block] += fold(masked)
            acc_ref[1, block] += fold(masked * total)
        return carry

    lax.fori_loop(0, slots, one, 0)
    for copy in small[3:]:
        copy.wait()
    for block in range(blocks):
        cols = slice(block * LANES, (block + 1) * LANES)
        st_ref[0:1, cols] = row_sum(acc_ref[0, block])
        st_ref[1:2, cols] = row_sum(acc_ref[1, block])
    count = len_ref[0]
    for other in range(1, slots):
        count = count + len_ref[other]
    st_ref[:, blocks * LANES :] = jnp.full((2, LANES), count.astype(F32), F32)


def lag_sums(gp_ref, block, weights, taps, group, put):
    frames = weights(0).shape[0]
    slots = gp_ref.shape[1]
    for low in range(0, taps, group):
        sums = [None] * group
        for slot in range(slots):
            weight = weights(slot)
            for j in range(group):
                at = 1 + low + j
                term = fold(weight * gp_ref[block, slot, at : at + frames, :])
                sums[j] = term if sums[j] is None else sums[j] + term
        for j in range(group):
            put(low + j, row_sum(sums[j]))


def aux_body(start, ok_ref, in_ref, gp_ref, cv_ref, out_ref, wt_ref):
    _, slots, frames, _ = cv_ref.shape
    many, _, taps, _ = out_ref.shape
    lead = taps // 2

    def one(i, carry):
        block = start + i
        for slot in range(slots):
            wt_ref[slot] = cv_ref[block, slot] * ok_ref[slot]

        def put(k, row):
            out_ref[i, 0, k : k + 1, :] = row

        lag_sums(gp_ref, block, lambda slot: wt_ref[slot], taps, 16, put)
        total = jnp.zeros((taps, LANES), F32)
        for slot in range(slots):
            inside = in_ref[slot].astype(BF16)
            rest = gp_ref[block, slot, lead : lead + frames, :]
            for _ in range(3):
                part = rest.astype(BF16)
                rest = rest - part.astype(F32)
                total = total + jnp.dot(inside, part, preferred_element_type=F32)
        out_ref[i, 1] = total
        return carry

    lax.fori_loop(0, many, one, 0)


def back_body(cotan_hbm, w_hbm, out_ref, cotan_ref, w_ref, sems):
    blocks = out_ref.shape[0]
    fetch = pltpu.make_async_copy(cotan_hbm, cotan_ref, sems.at[blocks])
    fetch.start()
    copies = []
    for block in range(blocks):
        rows = pl.ds(block * LANES, LANES)
        copies.append(pltpu.make_async_copy(w_hbm.at[rows], w_ref.at[rows], sems.at[block]))
        copies[-1].start()
    fetch.wait()
    for block in range(blocks):
        copies[block].wait()
        rows = w_ref[block * LANES : (block + 1) * LANES, :]
        out_ref[block] = lax.dot_general(
            cotan_ref[...], rows, (((1,), (1,)), ((), ())), preferred_element_type=F32
        )


def scale_of(st_ref, block):
    width = st_ref.shape[1] - LANES
    cols = pl.ds(pl.multiple_of(block * LANES, LANES), LANES)
    count = st_ref[0:1, width:]
    mean = st_ref[0:1, cols] / count
    inv = lax.rsqrt(st_ref[1:2, cols] / count - mean * mean + 1e-05)
    return count, mean, inv


def hidden_body(st_ref, gb_ref, ok_ref, cv_ref, hid_hbm, hid_ref, sems):
    blocks, slots, frames, _ = cv_ref.shape

    def put(block):
        return pltpu.make_async_copy(hid_ref.at[block], hid_hbm.at[block], sems.at[block])

    def one(block, carry):
        _, mean, inv = scale_of(st_ref, block)
        gain, shift = gb_ref[0, pl.ds(block, 1), :], gb_ref[1, pl.ds(block, 1), :]
        for slot in range(slots):
            valid = ok_ref[slot]
            shifted = gain * ((cv_ref[block, slot] - mean) * inv) + shift
            hidden = shifted * jax.nn.sigmoid(shifted) * valid
            hid_ref[block, slot * frames : (slot + 1) * frames, :] = hidden.astype(BF16)
        put(block).start()
        return carry

    lax.fori_loop(0, blocks, one, 0)
    for block in range(blocks):
        put(block).wait()


def slope_body(c_hbm, w_hbm, st_ref, gb_ref, ok_ref, gp_ref, cv_ref, low_ref, *refs):
    aux_refs, (give_ref, keep_ref, sl_ref, high_ref, c_ref, w_ref, sems) = refs[:-7], refs[-7:]
    many = high_ref.shape[0]
    copies = [pltpu.make_async_copy(c_hbm, c_ref, sems.at[many])]
    for block in range(many):
        rows, source = pl.ds(block * LANES, LANES), pl.ds((many + block) * LANES, LANES)
        copies.append(pltpu.make_async_copy(w_hbm.at[source], w_ref.at[rows], sems.at[block]))
    for copy in copies:
        copy.start()
    blocks, slots, frames, _ = cv_ref.shape
    taps = aux_refs[0].shape[2]
    last = 3 * taps
    bit = lax.axis_index("dp") & 1

    def one(i, aux_ref, odd, q_ref):
        block = 2 * i + odd
        bk_ref, at = (low_ref, block) if 2 * i < many else (high_ref, block - many)
        _, mean, inv = scale_of(st_ref, block)
        gain, shift = gb_ref[0, pl.ds(block, 1), :], gb_ref[1, pl.ds(block, 1), :]
        first = second = jnp.zeros((8, LANES), F32)
        for slot in range(slots):
            normed = (cv_ref[block, slot] - mean) * inv
            shifted = gain * normed + shift
            sig = jax.nn.sigmoid(shifted)
            back = bk_ref[at, slot * frames : (slot + 1) * frames, :]
            slope = back * sig * (1.0 + shifted * (1.0 - sig)) * ok_ref[slot]
            sl_ref[slot] = slope
            first, second = first + fold(slope), second + fold(slope * normed)

        def put(k, row):
            q_ref[i, k : k + 1, :] = row

        lag_sums(gp_ref, block, lambda slot: sl_ref[slot], taps, 16, put)
        q_ref[i, taps : 2 * taps, :] = aux_ref[odd, 1]
        q_ref[i, 2 * taps : last, :] = inv * (aux_ref[odd, 0] - mean * aux_ref[odd, 1])
        keep_ref[0, pl.ds(last + block, 1), :] = row_sum(first)
        keep_ref[0, pl.ds(last + blocks + block, 1), :] = row_sum(second)

    for i, aux_ref in enumerate(aux_refs):
        if 2 * i == many:
            for copy in copies:
                copy.wait()
            for block in range(many):
                rows = w_ref[block * LANES : (block + 1) * LANES, :]
                high_ref[block] = lax.dot_general(
                    c_ref[...], rows, (((1,), (1,)), ((), ())), preferred_element_type=F32
                )
        one(i, aux_ref, 1 - bit, give_ref)
        one(i, aux_ref, bit, keep_ref)
    for i in range(len(aux_refs)):
        give_ref[i, last:, :] = keep_ref[0, last:, :]
        if i:
            keep_ref[i, last:, :] = keep_ref[0, last:, :]


def halve_body(level, own_ref, recv_ref, give_ref, keep_ref):
    bit = (lax.axis_index("dp") >> level) & 1
    for i in range(give_ref.shape[0]):
        for odd, ref in ((1 - bit, give_ref), (bit, keep_ref)):
            ref[i] = own_ref[2 * i + odd] + recv_ref[2 * i + odd]


def out_body(hid_ref, w_ref, out_ref):
    blocks = hid_ref.shape[0]
    slots, frames, _ = out_ref.shape
    total = None
    for block in range(blocks):
        term = jnp.dot(
            hid_ref[block],
            w_ref[block * LANES : (block + 1) * LANES, :],
            preferred_element_type=F32,
        )
        total = term if total is None else total + term
    for slot in range(slots):
        out_ref[slot] = total[slot * frames : (slot + 1) * frames, :].astype(BF16)


def stage_body(*refs):
    pieces, out_ref, sems = refs[:-2], refs[-2], refs[-1]
    copies = [
        pltpu.make_async_copy(piece, out_ref.at[i], sems.at[i]) for i, piece in enumerate(pieces)
    ]
    for copy in copies:
        copy.start()
    for copy in copies:
        copy.wait()


def rows_body(masks, flip, recv_hbm, staged_ref, *refs):
    pieces, (out_ref, recv_ref, held, sems) = refs[:-4], refs[-4:]
    me, half = lax.axis_index("dp"), lax.axis_index("grp") & 1
    half = 1 - half if flip else half
    many = out_ref.shape[0]
    width = many * LANES
    cols = pl.ds(pl.multiple_of(half * width, width), width)
    copies = [
        pltpu.make_async_copy(piece.at[:, cols], held.at[i], sems.at[i])
        for i, piece in enumerate(pieces)
    ]
    fetch = pltpu.make_async_copy(recv_hbm, recv_ref, sems.at[len(pieces)])
    fetch.start()
    for copy in copies:
        copy.start()
    fetch.wait()
    early = staged_ref.shape[0]
    total = None
    for i, mask in enumerate(masks):
        left = recv_ref[jnp.bitwise_xor(me, mask)]
        if i >= early:
            copies[i - early].wait()
        right = staged_ref[i, :, cols] if i < early else held[i - early]
        term = lax.dot_general(
            left, right, (((0,), (0,)), ((), ())), preferred_element_type=F32
        )
        total = term if total is None else total + term
    for block in range(many):
        out_ref[block] = total[:, block * LANES : (block + 1) * LANES].astype(BF16)


def plus_body(own_ref, recv_ref, out_ref):
    out_ref[...] = own_ref[...] + recv_ref[...]


def add_body(own_ref, recv_ref, out_ref):
    out_ref[...] = (own_ref[...].astype(F32) + recv_ref[...].astype(F32)).astype(BF16)


def scale_body(st_ref, gb_ref, out_ref):
    me = lax.axis_index("dp")
    count, _, inv = scale_of(st_ref, me)
    out_ref[0:1, :] = gb_ref[0, pl.ds(me, 1), :] * inv
    out_ref[1:2, :] = count


def last_body(taps, own_ref, recv_ref, lags_ref, more_ref, sc_ref, rows_ref, gk_ref, gg_ref, gb_ref):
    me, half = lax.axis_index("dp"), lax.axis_index("grp") & 1
    many = own_ref.shape[0]
    for which, ref in ((half, own_ref), (1 - half, recv_ref)):
        for block in range(many):
            cols = pl.ds(pl.multiple_of((which * many + block) * LANES, LANES), LANES)
            rows_ref[:, cols] = ref[block].astype(F32)
    value = lags_ref[0] + more_ref[0]
    blocks = gb_ref.shape[0]
    gb_ref[...] = value[3 * taps : 3 * taps + blocks]
    gg_ref[...] = value[3 * taps + blocks : 3 * taps + 2 * blocks]
    count = sc_ref[1:2, :]
    mine = pl.ds(me, 1)
    gk_ref[...] = sc_ref[0:1, :] * (
        value[0:taps]
        - (gb_ref[mine, :] / count) * value[taps : 2 * taps]
        - (gg_ref[mine, :] / count) * value[2 * taps : 3 * taps]
    )


SMEM = pl.BlockSpec(memory_space=pltpu.SMEM)
VMEM = pl.BlockSpec(memory_space=pltpu.VMEM)
HBM = pl.BlockSpec(memory_space=pltpu.HBM)
ANY = pl.BlockSpec(memory_space=pl.ANY)


def in_hbm(value):
    return pltpu.with_memory_space_constraint(value, pltpu.HBM)


def call(body, shapes, scalars, args, flops=0, scratch=(), mib=8, **more):
    many = isinstance(shapes, list)
    moved = sum(a.size * a.dtype.itemsize for a in args)
    return pl.pallas_call(
        body,
        in_specs=more.pop("in_specs", None) or [SMEM] * len(scalars) + [VMEM] * len(args),
        out_specs=more.pop("out_specs", None) or ([VMEM] * len(shapes) if many else VMEM),
        out_shape=shapes,
        scratch_shapes=scratch,
        compiler_params=pltpu.CompilerParams(vmem_limit_bytes=mib << 20),
        cost_estimate=pl.CostEstimate(flops=flops, bytes_accessed=moved, transcendentals=0),
        **more,
    )(*scalars, *args)


def local_fast(n_dp, n_grp, acts, cotan, lengths, offsets, kernel, gamma, beta, w_out):
    slots, frames, wide = acts.shape
    width = wide // 2
    taps = kernel.shape[0]
    blocks = width // LANES
    tokens = slots * frames
    n_q = 3 * taps + 2 * blocks
    padded = 2 * (taps // 2) + frames
    shape = jax.ShapeDtypeStruct

    def swap(value, dp_mask, grp_mask):
        pairs = [
            (d * n_grp + g, (d ^ dp_mask) * n_grp + (g ^ grp_mask))
            for d in range(n_dp)
            for g in range(n_grp)
        ]
        return lax.ppermute(value, ("dp", "grp"), pairs)

    def plus(own, other):
        return call(plus_body, shape(own.shape, own.dtype), (), (own, other))

    dp_bits = [1 << i for i in range(n_dp.bit_length() - 1)]
    grp_bits = [1 << i for i in range(n_grp.bit_length() - 1)]
    gamma2, beta2 = gamma.reshape(blocks, LANES), beta.reshape(blocks, LANES)

    flat_cotan = cotan.reshape(tokens, width)
    pieces = [(0, flat_cotan)]
    for bit in dp_bits[1:] + dp_bits[:1]:
        pieces += [(m | bit, swap(v, bit, 0)) for m, v in pieces]
    late_bits = dp_bits[-1] | dp_bits[-2]
    pieces.sort(key=lambda piece: piece[0] & late_bits == late_bits)
    masks, values = tuple(m for m, _ in pieces), [v for _, v in pieces]
    early = sum(m & late_bits != late_bits for m in masks)

    gated, conv_out, stats, valid, inside, gains = call(
        conv_body,
        [
            shape((blocks, slots, padded, LANES), F32),
            shape((blocks, slots, frames, LANES), F32),
            shape((2, width + LANES), F32),
            shape((slots, frames, LANES), F32),
            shape((slots, taps, frames), F32),
            shape((2, blocks, LANES), F32),
        ],
        (),
        [in_hbm(v) for v in (lengths, offsets, acts, kernel, gamma2, beta2)],
        flops=4 * taps * tokens * width,
        scratch=[
            pltpu.VMEM((2, blocks, 8, LANES), F32),
            pltpu.SMEM((slots,), jnp.int32),
            pltpu.SMEM((slots,), jnp.int32),
            pltpu.VMEM(acts.shape, BF16),
            pltpu.VMEM(kernel.shape, F32),
            pltpu.SemaphoreType.DMA((5,)),
            pltpu.SemaphoreType.DMA((slots,)),
        ],
        in_specs=[HBM] * 6,
    )

    hops = [(1, m) for m in grp_bits] + [(m | 1, 0) for m in dp_bits[1:]] + [(1, 0)]
    for dp_mask, grp_mask in hops:
        stats = plus(stats, swap(stats, dp_mask, grp_mask))

    back = call(
        back_body,
        shape((blocks // 2, tokens, LANES), F32),
        (),
        (in_hbm(flat_cotan), in_hbm(w_out)),
        flops=tokens * width * width,
        scratch=[
            pltpu.VMEM(flat_cotan.shape, BF16),
            pltpu.VMEM((width // 2, width), BF16),
            pltpu.SemaphoreType.DMA((blocks // 2 + 1,)),
        ],
        in_specs=[HBM] * 2,
    )
    parts = blocks // 2
    each = 2
    aux = [
        call(
            functools.partial(aux_body, i * each),
            shape((each, 2, taps, LANES), F32),
            (),
            (valid, inside, gated, conv_out),
            flops=4 * taps * tokens * each * LANES,
            scratch=[pltpu.VMEM((slots, frames, LANES), F32)],
        )
        for i in range(parts)
    ]

    hidden = call(
        hidden_body,
        pltpu.HBM((blocks, tokens, LANES), BF16),
        (),
        (stats, gains, valid, conv_out),
        scratch=[
            pltpu.VMEM((blocks, tokens, LANES), BF16),
            pltpu.SemaphoreType.DMA((blocks,)),
        ],
        out_specs=HBM,
    )
    received = lax.all_to_all(hidden, "dp", 0, 0, tiled=True)
    give, lags = call(
        slope_body,
        [shape((parts, n_q, LANES), F32)] * 2,
        (),
        (in_hbm(flat_cotan), in_hbm(w_out), stats, gains, valid, gated, conv_out, back, *aux),
        flops=4 * taps * tokens * width + tokens * width * width,
        scratch=[
            pltpu.VMEM((slots, frames, LANES), F32),
            pltpu.VMEM((blocks // 2, tokens, LANES), F32),
            pltpu.VMEM(flat_cotan.shape, BF16),
            pltpu.VMEM((width // 2, width), BF16),
            pltpu.SemaphoreType.DMA((blocks // 2 + 1,)),
        ],
        in_specs=[HBM] * 2 + [VMEM] * (6 + parts),
    )
    for level in range(1, len(dp_bits)):
        came = swap(give, dp_bits[level - 1], 0)
        give, lags = call(
            functools.partial(halve_body, level),
            [shape((parts >> level, n_q, LANES), F32)] * 2,
            (),
            (lags, came),
        )
    lags = plus(lags, swap(give, dp_bits[-1], 0))
    scale = call(scale_body, shape((2, LANES), F32), (), (stats, gains))
    outputs = call(out_body, shape(cotan.shape, BF16), (), (hidden, w_out))

    half_shape = shape((blocks // 2, LANES, LANES), BF16)
    staged = call(
        stage_body,
        shape((early, tokens, width), BF16),
        (),
        values[:early],
        scratch=[pltpu.SemaphoreType.DMA((early,))],
        in_specs=[ANY] * early,
    )

    def rows_of(flip):
        return call(
            functools.partial(rows_body, masks, flip),
            half_shape,
            (),
            (received, staged, *values[early:]),
            flops=n_dp * tokens * LANES * width,
            scratch=[
                pltpu.VMEM(received.shape, BF16),
                pltpu.VMEM((n_dp - early, tokens, width // 2), BF16),
                pltpu.SemaphoreType.DMA((n_dp - early + 1,)),
            ],
            in_specs=[ANY, VMEM] + [ANY] * (n_dp - early),
        )

    given = rows_of(True)
    taken = swap(given, 0, 1)
    kept = rows_of(False)
    both = call(add_body, half_shape, (), (kept, taken))
    for mask in grp_bits[1:]:
        other = swap(both, 0, mask)
        both = call(add_body, half_shape, (), (both, other))
    rest = swap(both, 0, 1)

    for mask in grp_bits[:-1]:
        lags = plus(lags, swap(lags, 0, mask))
    more = swap(lags, 0, grp_bits[-1])
    weight_rows, grad_kernel, gamma_sum, beta_sum = call(
        functools.partial(last_body, taps),
        [
            shape((LANES, width), F32),
            shape((taps, LANES), F32),
            shape((blocks, LANES), F32),
            shape((blocks, LANES), F32),
        ],
        (),
        (both, rest, lags, more, scale),
    )
    return (outputs, weight_rows, grad_kernel, gamma_sum.reshape(width), beta_sum.reshape(width))


def solution(mesh):
    n_dp, n_grp = mesh.shape["dp"], mesh.shape["grp"]

    def fits(width, taps, frames):
        return (
            n_dp & (n_dp - 1) == 0
            and n_grp & (n_grp - 1) == 0
            and n_dp >= 4
            and n_grp >= 4
            and width == n_dp * LANES
            and taps % 16 == 0
            and frames % 16 == 0
            and n_dp % 8 == 0
        )

    def local(acts, cotan, lengths, offsets, kernel, gamma, beta, w_out):
        args = (acts, cotan, lengths, offsets, kernel, gamma, beta, w_out)
        if not fits(w_out.shape[0], kernel.shape[0], acts.shape[1]):
            return local_general(*args)
        return local_fast(n_dp, n_grp, *args)

    placed = (
        P(("dp", "grp"), None, None),
        P(("dp", "grp"), None, None),
        P(("dp", "grp")),
        P(("dp", "grp")),
        P(),
        P(),
        P(),
        P(),
    )
    return jax.shard_map(
        local,
        mesh=mesh,
        in_specs=placed,
        out_specs=(P(("dp", "grp"), None, None), P("dp", None), P(None, "dp"), P(), P()),
        check_vma=False,
    )
```

```python
import functools

import jax
import jax.numpy as jnp
from jax import lax
from jax.experimental import pallas as pl
from jax.experimental.pallas import tpu as pltpu
from jax.sharding import PartitionSpec as P


LANES = 128
F32 = jnp.float32
BF16 = jnp.bfloat16


def convolve(block_acts, block_len, block_off, kernel):
    taps = kernel.shape[0]
    model_width = kernel.shape[1]
    frame_count = block_acts.shape[1]
    position = jnp.arange(frame_count, dtype=jnp.int32)
    valid = (
        (position[None, :] >= block_off[:, None])
        & (position[None, :] < (block_off + block_len)[:, None])
    ).astype(jnp.float32)
    wide_acts = block_acts.astype(jnp.float32)
    gated = (
        wide_acts[..., :model_width]
        * jax.nn.sigmoid(wide_acts[..., model_width:])
        * valid[..., None]
    )
    padded = jnp.pad(gated, ((0, 0), (taps // 2 - 1, taps // 2), (0, 0)))
    conv_out = padded[:, 0:frame_count] * kernel[0]
    for tap in range(1, taps):
        conv_out = conv_out + padded[:, tap : tap + frame_count] * kernel[tap]
    return (valid, padded, conv_out)


def local_general(acts, cotan, lengths, offsets, kernel, gamma, beta, w_out):
    model_width = w_out.shape[0]
    taps = kernel.shape[0]
    valid, padded, conv_out = convolve(acts, lengths, offsets, kernel)
    masked = conv_out * valid[..., None]
    sum_first, sum_second, frame_total = lax.psum(
        (
            jnp.sum(masked, axis=(0, 1)),
            jnp.sum(masked * conv_out, axis=(0, 1)),
            jnp.sum(lengths).astype(jnp.float32),
        ),
        ("dp", "grp"),
    )
    mean_value = sum_first / frame_total
    inv_std = lax.rsqrt(sum_second / frame_total - mean_value * mean_value + 1e-05)
    normed = (conv_out - mean_value) * inv_std
    shifted = gamma * normed + beta
    sig_value = jax.nn.sigmoid(shifted)
    hidden = (shifted * sig_value * valid[..., None]).astype(jnp.bfloat16)
    flat_hidden = hidden.reshape(-1, model_width)
    flat_cotan = cotan.reshape(-1, model_width)
    outputs = (
        jnp.dot(flat_hidden, w_out, preferred_element_type=jnp.float32)
        .astype(jnp.bfloat16)
        .reshape(cotan.shape)
    )
    weight_rows = lax.psum_scatter(
        lax.dot_general(
            flat_hidden, flat_cotan, (((0,), (0,)), ((), ())), preferred_element_type=jnp.float32
        ),
        "dp",
        scatter_dimension=0,
        tiled=True,
    )
    back_hidden = lax.dot_general(
        flat_cotan, w_out, (((1,), (1,)), ((), ())), preferred_element_type=jnp.float32
    ).reshape(conv_out.shape)
    slope = back_hidden * sig_value * (1.0 + shifted * (1.0 - sig_value)) * valid[..., None]
    beta_sum, gamma_sum = lax.psum(
        (jnp.sum(slope, axis=(0, 1)), jnp.sum(slope * normed, axis=(0, 1))), ("dp", "grp")
    )
    conv_grad = (
        gamma
        * inv_std
        * (slope - beta_sum / frame_total - normed * gamma_sum / frame_total)
        * valid[..., None]
    )
    frame_count = conv_out.shape[1]
    kernel_term = jnp.stack(
        [
            jnp.sum(conv_grad * padded[:, tap : tap + frame_count], axis=(0, 1))
            for tap in range(taps)
        ],
        axis=0,
    )
    kernel_rows = lax.psum_scatter(kernel_term.T, "dp", scatter_dimension=0, tiled=True)
    weight_rows, kernel_rows = lax.psum((weight_rows, kernel_rows), "grp")
    return (outputs, weight_rows, kernel_rows.T, gamma_sum, beta_sum)


def fold(value):
    total = value[0:8]
    for at in range(8, value.shape[0], 8):
        total = total + value[at : at + 8]
    return total


def row_sum(value):
    return jnp.sum(value, axis=0, keepdims=True)


def conv_body(len_hbm, off_hbm, acts_hbm, k_hbm, g_hbm, b_hbm, gp_ref, cv_ref, st_ref, ok_ref, in_ref, gb_ref,
              acc_ref, len_ref, off_ref, acts_ref, k_ref, sems, slot_sems):
    slots, frames, wide = acts_ref.shape
    blocks, _, rows, _ = gp_ref.shape
    taps = k_ref.shape[0]
    lead = taps // 2
    small = [
        pltpu.make_async_copy(source, target, sems.at[i])
        for i, (source, target) in enumerate(
            (
                (len_hbm, len_ref),
                (off_hbm, off_ref),
                (k_hbm, k_ref),
                (g_hbm, gb_ref.at[0]),
                (b_hbm, gb_ref.at[1]),
            )
        )
    ]

    def fetch(slot):
        return pltpu.make_async_copy(acts_hbm.at[slot], acts_ref.at[slot], slot_sems.at[slot])

    small[0].start()
    small[1].start()
    fetch(0).start()
    small[2].start()
    for slot in range(1, slots):
        fetch(slot).start()
    for copy in small[3:]:
        copy.start()
    acc_ref[...] = jnp.zeros_like(acc_ref)
    position = lax.broadcasted_iota(jnp.int32, (frames, LANES), 0)
    reach = lax.broadcasted_iota(jnp.int32, (taps, frames), 1)
    reach = reach - lax.broadcasted_iota(jnp.int32, (taps, frames), 0) + (lead - 1)
    for copy in small[:3]:
        copy.wait()

    def one(slot, carry):
        low = off_ref[slot]
        high = low + len_ref[slot]
        valid = ((position >= low) & (position < high)).astype(F32)
        ok_ref[slot] = valid
        in_ref[slot] = (
            (reach >= low) & (reach < high) & (reach >= 0) & (reach < frames)
        ).astype(F32)
        fetch(slot).wait()
        for block in range(blocks):
            cols = slice(block * LANES, (block + 1) * LANES)
            gate = slice(wide // 2 + block * LANES, wide // 2 + (block + 1) * LANES)
            left, right = acts_ref[slot, :, cols].astype(F32), acts_ref[slot, :, gate].astype(F32)
            gp_ref[block, slot, 0:lead, :] = jnp.zeros((lead, LANES), F32)
            gp_ref[block, slot, lead : lead + frames, :] = left * jax.nn.sigmoid(right) * valid
            tail = jnp.zeros((rows - lead - frames, LANES), F32)
            gp_ref[block, slot, lead + frames : rows, :] = tail
        for block in range(blocks):
            cols = slice(block * LANES, (block + 1) * LANES)
            total = gp_ref[block, slot, 1 : 1 + frames, :] * k_ref[0:1, cols]
            for tap in range(1, taps):
                lag = gp_ref[block, slot, 1 + tap : 1 + tap + frames, :]
                total = total + lag * k_ref[tap : tap + 1, cols]
            cv_ref[block, slot] = total
            masked = total * valid
            acc_ref[0, block] += fold(masked)
            acc_ref[1, block] += fold(masked * total)
        return carry

    lax.fori_loop(0, slots, one, 0)
    for copy in small[3:]:
        copy.wait()
    for block in range(blocks):
        cols = slice(block * LANES, (block + 1) * LANES)
        st_ref[0:1, cols] = row_sum(acc_ref[0, block])
        st_ref[1:2, cols] = row_sum(acc_ref[1, block])
    count = len_ref[0]
    for other in range(1, slots):
        count = count + len_ref[other]
    st_ref[:, blocks * LANES :] = jnp.full((2, LANES), count.astype(F32), F32)


def lag_sums(gp_ref, block, weights, taps, group, put):
    frames = weights(0).shape[0]
    slots = gp_ref.shape[1]
    for low in range(0, taps, group):
        sums = [None] * group
        for slot in range(slots):
            weight = weights(slot)
            for j in range(group):
                at = 1 + low + j
                term = fold(weight * gp_ref[block, slot, at : at + frames, :])
                sums[j] = term if sums[j] is None else sums[j] + term
        for j in range(group):
            put(low + j, row_sum(sums[j]))


def aux_body(start, ok_ref, in_ref, gp_ref, cv_ref, out_ref, wt_ref):
    _, slots, frames, _ = cv_ref.shape
    many, _, taps, _ = out_ref.shape
    lead = taps // 2

    def one(i, carry):
        block = start + i
        for slot in range(slots):
            wt_ref[slot] = cv_ref[block, slot] * ok_ref[slot]

        def put(k, row):
            out_ref[i, 0, k : k + 1, :] = row

        lag_sums(gp_ref, block, lambda slot: wt_ref[slot], taps, 16, put)
        total = jnp.zeros((taps, LANES), F32)
        for slot in range(slots):
            inside = in_ref[slot].astype(BF16)
            rest = gp_ref[block, slot, lead : lead + frames, :]
            for _ in range(3):
                part = rest.astype(BF16)
                rest = rest - part.astype(F32)
                total = total + jnp.dot(inside, part, preferred_element_type=F32)
        out_ref[i, 1] = total
        return carry

    lax.fori_loop(0, many, one, 0)


def back_body(cotan_ref, w_ref, out_ref):
    for block in range(out_ref.shape[0]):
        rows = w_ref[block * LANES : (block + 1) * LANES, :]
        out_ref[block] = lax.dot_general(
            cotan_ref[...], rows, (((1,), (1,)), ((), ())), preferred_element_type=F32
        )


def scale_of(st_ref, block):
    width = st_ref.shape[1] - LANES
    cols = pl.ds(pl.multiple_of(block * LANES, LANES), LANES)
    count = st_ref[0:1, width:]
    mean = st_ref[0:1, cols] / count
    inv = lax.rsqrt(st_ref[1:2, cols] / count - mean * mean + 1e-05)
    return count, mean, inv


def hidden_body(st_ref, gb_ref, ok_ref, cv_ref, hid_ref):
    blocks, slots, frames, _ = cv_ref.shape

    def one(block, carry):
        _, mean, inv = scale_of(st_ref, block)
        gain, shift = gb_ref[0, pl.ds(block, 1), :], gb_ref[1, pl.ds(block, 1), :]
        for slot in range(slots):
            valid = ok_ref[slot]
            shifted = gain * ((cv_ref[block, slot] - mean) * inv) + shift
            hidden = shifted * jax.nn.sigmoid(shifted) * valid
            hid_ref[block, slot * frames : (slot + 1) * frames, :] = hidden.astype(BF16)
        return carry

    lax.fori_loop(0, blocks, one, 0)


def slope_body(st_ref, gb_ref, ok_ref, gp_ref, cv_ref, bk_ref, *refs):
    aux_refs, (give_ref, keep_ref, sl_ref) = refs[:-3], refs[-3:]
    blocks, slots, frames, _ = cv_ref.shape
    taps = aux_refs[0].shape[2]
    last = 3 * taps
    bit = lax.axis_index("dp") & 1

    def one(i, aux_ref, odd, q_ref):
        block = 2 * i + odd
        _, mean, inv = scale_of(st_ref, block)
        gain, shift = gb_ref[0, pl.ds(block, 1), :], gb_ref[1, pl.ds(block, 1), :]
        first = second = jnp.zeros((8, LANES), F32)
        for slot in range(slots):
            normed = (cv_ref[block, slot] - mean) * inv
            shifted = gain * normed + shift
            sig = jax.nn.sigmoid(shifted)
            back = bk_ref[block, slot * frames : (slot + 1) * frames, :]
            slope = back * sig * (1.0 + shifted * (1.0 - sig)) * ok_ref[slot]
            sl_ref[slot] = slope
            first, second = first + fold(slope), second + fold(slope * normed)

        def put(k, row):
            q_ref[i, k : k + 1, :] = row

        lag_sums(gp_ref, block, lambda slot: sl_ref[slot], taps, 16, put)
        q_ref[i, taps : 2 * taps, :] = aux_ref[odd, 1]
        q_ref[i, 2 * taps : last, :] = inv * (aux_ref[odd, 0] - mean * aux_ref[odd, 1])
        keep_ref[0, pl.ds(last + block, 1), :] = row_sum(first)
        keep_ref[0, pl.ds(last + blocks + block, 1), :] = row_sum(second)

    for i, aux_ref in enumerate(aux_refs):
        one(i, aux_ref, 1 - bit, give_ref)
        one(i, aux_ref, bit, keep_ref)
    for i in range(len(aux_refs)):
        give_ref[i, last:, :] = keep_ref[0, last:, :]
        if i:
            keep_ref[i, last:, :] = keep_ref[0, last:, :]


def halve_body(level, own_ref, recv_ref, give_ref, keep_ref):
    bit = (lax.axis_index("dp") >> level) & 1
    for i in range(give_ref.shape[0]):
        for odd, ref in ((1 - bit, give_ref), (bit, keep_ref)):
            ref[i] = own_ref[2 * i + odd] + recv_ref[2 * i + odd]


def out_body(hid_ref, w_ref, out_ref):
    blocks = hid_ref.shape[0]
    slots, frames, _ = out_ref.shape
    total = None
    for block in range(blocks):
        term = jnp.dot(
            hid_ref[block],
            w_ref[block * LANES : (block + 1) * LANES, :],
            preferred_element_type=F32,
        )
        total = term if total is None else total + term
    for slot in range(slots):
        out_ref[slot] = total[slot * frames : (slot + 1) * frames, :].astype(BF16)


def stage_body(*refs):
    pieces, out_ref, sems = refs[:-2], refs[-2], refs[-1]
    copies = [
        pltpu.make_async_copy(piece, out_ref.at[i], sems.at[i]) for i, piece in enumerate(pieces)
    ]
    for copy in copies:
        copy.start()
    for copy in copies:
        copy.wait()


def rows_body(masks, recv_hbm, staged_ref, *refs):
    pieces, (give_ref, keep_ref, recv_ref, held, sems) = refs[:-5], refs[-5:]
    me, half = lax.axis_index("dp"), lax.axis_index("grp") & 1
    copies = [
        pltpu.make_async_copy(piece, held.at[i], sems.at[i]) for i, piece in enumerate(pieces)
    ]
    fetch = pltpu.make_async_copy(recv_hbm, recv_ref, sems.at[len(pieces)])
    fetch.start()
    for copy in copies:
        copy.start()
    fetch.wait()
    early = staged_ref.shape[0]
    many = give_ref.shape[0]
    width = many * LANES
    give = pl.ds(pl.multiple_of((1 - half) * width, width), width)
    keep = pl.ds(pl.multiple_of(half * width, width), width)
    totals = [None, None]
    for i, mask in enumerate(masks):
        left = recv_ref[jnp.bitwise_xor(me, mask)]
        if i >= early:
            copies[i - early].wait()
        for j, cols in enumerate((give, keep)):
            right = staged_ref[i, :, cols] if i < early else held[i - early, :, cols]
            term = lax.dot_general(
                left, right, (((0,), (0,)), ((), ())), preferred_element_type=F32
            )
            totals[j] = term if totals[j] is None else totals[j] + term
    for total, ref in zip(totals, (give_ref, keep_ref)):
        for block in range(many):
            ref[block] = total[:, block * LANES : (block + 1) * LANES].astype(BF16)


def plus_body(own_ref, recv_ref, out_ref):
    out_ref[...] = own_ref[...] + recv_ref[...]


def add_body(own_ref, recv_ref, out_ref):
    out_ref[...] = (own_ref[...].astype(F32) + recv_ref[...].astype(F32)).astype(BF16)


def scale_body(st_ref, gb_ref, out_ref):
    me = lax.axis_index("dp")
    count, _, inv = scale_of(st_ref, me)
    out_ref[0:1, :] = gb_ref[0, pl.ds(me, 1), :] * inv
    out_ref[1:2, :] = count


def last_body(taps, own_ref, recv_ref, lags_ref, more_ref, sc_ref, rows_ref, gk_ref, gg_ref, gb_ref):
    me, half = lax.axis_index("dp"), lax.axis_index("grp") & 1
    many = own_ref.shape[0]
    for which, ref in ((half, own_ref), (1 - half, recv_ref)):
        for block in range(many):
            cols = pl.ds(pl.multiple_of((which * many + block) * LANES, LANES), LANES)
            rows_ref[:, cols] = ref[block].astype(F32)
    value = lags_ref[0] + more_ref[0]
    blocks = gb_ref.shape[0]
    gb_ref[...] = value[3 * taps : 3 * taps + blocks]
    gg_ref[...] = value[3 * taps + blocks : 3 * taps + 2 * blocks]
    count = sc_ref[1:2, :]
    mine = pl.ds(me, 1)
    gk_ref[...] = sc_ref[0:1, :] * (
        value[0:taps]
        - (gb_ref[mine, :] / count) * value[taps : 2 * taps]
        - (gg_ref[mine, :] / count) * value[2 * taps : 3 * taps]
    )


SMEM = pl.BlockSpec(memory_space=pltpu.SMEM)
VMEM = pl.BlockSpec(memory_space=pltpu.VMEM)
HBM = pl.BlockSpec(memory_space=pltpu.HBM)
ANY = pl.BlockSpec(memory_space=pl.ANY)


def in_hbm(value):
    return pltpu.with_memory_space_constraint(value, pltpu.HBM)


def call(body, shapes, scalars, args, flops=0, scratch=(), mib=8, **more):
    many = isinstance(shapes, list)
    moved = sum(a.size * a.dtype.itemsize for a in args)
    return pl.pallas_call(
        body,
        in_specs=more.pop("in_specs", None) or [SMEM] * len(scalars) + [VMEM] * len(args),
        out_specs=[VMEM] * len(shapes) if many else VMEM,
        out_shape=shapes,
        scratch_shapes=scratch,
        compiler_params=pltpu.CompilerParams(vmem_limit_bytes=mib << 20),
        cost_estimate=pl.CostEstimate(flops=flops, bytes_accessed=moved, transcendentals=0),
        **more,
    )(*scalars, *args)


def local_fast(n_dp, n_grp, acts, cotan, lengths, offsets, kernel, gamma, beta, w_out):
    slots, frames, wide = acts.shape
    width = wide // 2
    taps = kernel.shape[0]
    blocks = width // LANES
    tokens = slots * frames
    n_q = 3 * taps + 2 * blocks
    padded = 2 * (taps // 2) + frames
    shape = jax.ShapeDtypeStruct

    def swap(value, dp_mask, grp_mask):
        pairs = [
            (d * n_grp + g, (d ^ dp_mask) * n_grp + (g ^ grp_mask))
            for d in range(n_dp)
            for g in range(n_grp)
        ]
        return lax.ppermute(value, ("dp", "grp"), pairs)

    def plus(own, other):
        return call(plus_body, shape(own.shape, own.dtype), (), (own, other))

    dp_bits = [1 << i for i in range(n_dp.bit_length() - 1)]
    grp_bits = [1 << i for i in range(n_grp.bit_length() - 1)]
    gamma2, beta2 = gamma.reshape(blocks, LANES), beta.reshape(blocks, LANES)

    flat_cotan = cotan.reshape(tokens, width)
    pieces = [(0, flat_cotan)]
    for bit in dp_bits[1:] + dp_bits[:1]:
        pieces += [(m | bit, swap(v, bit, 0)) for m, v in pieces]
    late_bits = dp_bits[-1] | dp_bits[-2]
    pieces.sort(key=lambda piece: piece[0] & late_bits == late_bits)
    masks, values = tuple(m for m, _ in pieces), [v for _, v in pieces]
    early = sum(m & late_bits != late_bits for m in masks)

    gated, conv_out, stats, valid, inside, gains = call(
        conv_body,
        [
            shape((blocks, slots, padded, LANES), F32),
            shape((blocks, slots, frames, LANES), F32),
            shape((2, width + LANES), F32),
            shape((slots, frames, LANES), F32),
            shape((slots, taps, frames), F32),
            shape((2, blocks, LANES), F32),
        ],
        (),
        [in_hbm(v) for v in (lengths, offsets, acts, kernel, gamma2, beta2)],
        flops=4 * taps * tokens * width,
        scratch=[
            pltpu.VMEM((2, blocks, 8, LANES), F32),
            pltpu.SMEM((slots,), jnp.int32),
            pltpu.SMEM((slots,), jnp.int32),
            pltpu.VMEM(acts.shape, BF16),
            pltpu.VMEM(kernel.shape, F32),
            pltpu.SemaphoreType.DMA((5,)),
            pltpu.SemaphoreType.DMA((slots,)),
        ],
        in_specs=[HBM] * 6,
    )

    hops = [(1, m) for m in grp_bits] + [(m | 1, 0) for m in dp_bits[1:]] + [(1, 0)]
    for dp_mask, grp_mask in hops:
        stats = plus(stats, swap(stats, dp_mask, grp_mask))

    back = call(
        back_body,
        shape((blocks, tokens, LANES), F32),
        (),
        (flat_cotan, w_out),
        flops=2 * tokens * width * width,
    )
    parts = blocks // 2
    each = 2
    aux = [
        call(
            functools.partial(aux_body, i * each),
            shape((each, 2, taps, LANES), F32),
            (),
            (valid, inside, gated, conv_out),
            flops=4 * taps * tokens * each * LANES,
            scratch=[pltpu.VMEM((slots, frames, LANES), F32)],
        )
        for i in range(parts)
    ]

    hidden = call(
        hidden_body, shape((blocks, tokens, LANES), BF16), (), (stats, gains, valid, conv_out)
    )
    received = lax.all_to_all(hidden, "dp", 0, 0, tiled=True)
    give, lags = call(
        slope_body,
        [shape((parts, n_q, LANES), F32)] * 2,
        (),
        (stats, gains, valid, gated, conv_out, back, *aux),
        flops=4 * taps * tokens * width,
        scratch=[pltpu.VMEM((slots, frames, LANES), F32)],
    )
    for level in range(1, len(dp_bits)):
        came = swap(give, dp_bits[level - 1], 0)
        give, lags = call(
            functools.partial(halve_body, level),
            [shape((parts >> level, n_q, LANES), F32)] * 2,
            (),
            (lags, came),
        )
    lags = plus(lags, swap(give, dp_bits[-1], 0))
    scale = call(scale_body, shape((2, LANES), F32), (), (stats, gains))
    outputs = call(out_body, shape(cotan.shape, BF16), (), (hidden, w_out))

    half_shape = shape((blocks // 2, LANES, LANES), BF16)
    staged = call(
        stage_body,
        shape((early, tokens, width), BF16),
        (),
        values[:early],
        scratch=[pltpu.SemaphoreType.DMA((early,))],
        in_specs=[ANY] * early,
    )
    given, kept = call(
        functools.partial(rows_body, masks),
        [half_shape] * 2,
        (),
        (received, staged, *values[early:]),
        flops=2 * n_dp * tokens * LANES * width,
        scratch=[
            pltpu.VMEM(received.shape, BF16),
            pltpu.VMEM((n_dp - early, tokens, width), BF16),
            pltpu.SemaphoreType.DMA((n_dp - early + 1,)),
        ],
        in_specs=[ANY, VMEM] + [ANY] * (n_dp - early),
    )
    taken = swap(given, 0, 1)
    both = call(add_body, half_shape, (), (kept, taken))
    for mask in grp_bits[1:]:
        other = swap(both, 0, mask)
        both = call(add_body, half_shape, (), (both, other))
    rest = swap(both, 0, 1)

    for mask in grp_bits[:-1]:
        lags = plus(lags, swap(lags, 0, mask))
    more = swap(lags, 0, grp_bits[-1])
    weight_rows, grad_kernel, gamma_sum, beta_sum = call(
        functools.partial(last_body, taps),
        [
            shape((LANES, width), F32),
            shape((taps, LANES), F32),
            shape((blocks, LANES), F32),
            shape((blocks, LANES), F32),
        ],
        (),
        (both, rest, lags, more, scale),
    )
    return (outputs, weight_rows, grad_kernel, gamma_sum.reshape(width), beta_sum.reshape(width))


def solution(mesh):
    n_dp, n_grp = mesh.shape["dp"], mesh.shape["grp"]

    def fits(width, taps, frames):
        return (
            n_dp & (n_dp - 1) == 0
            and n_grp & (n_grp - 1) == 0
            and n_dp >= 4
            and n_grp >= 4
            and width == n_dp * LANES
            and taps % 16 == 0
            and frames % 16 == 0
            and n_dp % 8 == 0
        )

    def local(acts, cotan, lengths, offsets, kernel, gamma, beta, w_out):
        args = (acts, cotan, lengths, offsets, kernel, gamma, beta, w_out)
        if not fits(w_out.shape[0], kernel.shape[0], acts.shape[1]):
            return local_general(*args)
        return local_fast(n_dp, n_grp, *args)

    placed = (
        P(("dp", "grp"), None, None),
        P(("dp", "grp"), None, None),
        P(("dp", "grp")),
        P(("dp", "grp")),
        P(),
        P(),
        P(),
        P(),
    )
    return jax.shard_map(
        local,
        mesh=mesh,
        in_specs=placed,
        out_specs=(P(("dp", "grp"), None, None), P("dp", None), P(None, "dp"), P(), P()),
        check_vma=False,
    )
```

```python
import functools

import jax
import jax.numpy as jnp
from jax import lax
from jax.experimental import pallas as pl
from jax.experimental.pallas import tpu as pltpu
from jax.sharding import PartitionSpec as P


LANES = 128
F32 = jnp.float32
BF16 = jnp.bfloat16


def convolve(block_acts, block_len, block_off, kernel):
    taps = kernel.shape[0]
    model_width = kernel.shape[1]
    frame_count = block_acts.shape[1]
    position = jnp.arange(frame_count, dtype=jnp.int32)
    valid = (
        (position[None, :] >= block_off[:, None])
        & (position[None, :] < (block_off + block_len)[:, None])
    ).astype(jnp.float32)
    wide_acts = block_acts.astype(jnp.float32)
    gated = (
        wide_acts[..., :model_width]
        * jax.nn.sigmoid(wide_acts[..., model_width:])
        * valid[..., None]
    )
    padded = jnp.pad(gated, ((0, 0), (taps // 2 - 1, taps // 2), (0, 0)))
    conv_out = padded[:, 0:frame_count] * kernel[0]
    for tap in range(1, taps):
        conv_out = conv_out + padded[:, tap : tap + frame_count] * kernel[tap]
    return (valid, padded, conv_out)


def local_general(acts, cotan, lengths, offsets, kernel, gamma, beta, w_out):
    model_width = w_out.shape[0]
    taps = kernel.shape[0]
    valid, padded, conv_out = convolve(acts, lengths, offsets, kernel)
    masked = conv_out * valid[..., None]
    sum_first, sum_second, frame_total = lax.psum(
        (
            jnp.sum(masked, axis=(0, 1)),
            jnp.sum(masked * conv_out, axis=(0, 1)),
            jnp.sum(lengths).astype(jnp.float32),
        ),
        ("dp", "grp"),
    )
    mean_value = sum_first / frame_total
    inv_std = lax.rsqrt(sum_second / frame_total - mean_value * mean_value + 1e-05)
    normed = (conv_out - mean_value) * inv_std
    shifted = gamma * normed + beta
    sig_value = jax.nn.sigmoid(shifted)
    hidden = (shifted * sig_value * valid[..., None]).astype(jnp.bfloat16)
    flat_hidden = hidden.reshape(-1, model_width)
    flat_cotan = cotan.reshape(-1, model_width)
    outputs = (
        jnp.dot(flat_hidden, w_out, preferred_element_type=jnp.float32)
        .astype(jnp.bfloat16)
        .reshape(cotan.shape)
    )
    weight_rows = lax.psum_scatter(
        lax.dot_general(
            flat_hidden, flat_cotan, (((0,), (0,)), ((), ())), preferred_element_type=jnp.float32
        ),
        "dp",
        scatter_dimension=0,
        tiled=True,
    )
    back_hidden = lax.dot_general(
        flat_cotan, w_out, (((1,), (1,)), ((), ())), preferred_element_type=jnp.float32
    ).reshape(conv_out.shape)
    slope = back_hidden * sig_value * (1.0 + shifted * (1.0 - sig_value)) * valid[..., None]
    beta_sum, gamma_sum = lax.psum(
        (jnp.sum(slope, axis=(0, 1)), jnp.sum(slope * normed, axis=(0, 1))), ("dp", "grp")
    )
    conv_grad = (
        gamma
        * inv_std
        * (slope - beta_sum / frame_total - normed * gamma_sum / frame_total)
        * valid[..., None]
    )
    frame_count = conv_out.shape[1]
    kernel_term = jnp.stack(
        [
            jnp.sum(conv_grad * padded[:, tap : tap + frame_count], axis=(0, 1))
            for tap in range(taps)
        ],
        axis=0,
    )
    kernel_rows = lax.psum_scatter(kernel_term.T, "dp", scatter_dimension=0, tiled=True)
    weight_rows, kernel_rows = lax.psum((weight_rows, kernel_rows), "grp")
    return (outputs, weight_rows, kernel_rows.T, gamma_sum, beta_sum)


def fold(value):
    total = value[0:8]
    for at in range(8, value.shape[0], 8):
        total = total + value[at : at + 8]
    return total


def row_sum(value):
    return jnp.sum(value, axis=0, keepdims=True)


def conv_body(len_hbm, off_hbm, acts_hbm, k_hbm, g_hbm, b_hbm, gp_ref, cv_ref, st_ref, ok_ref, in_ref, gb_ref,
              acc_ref, len_ref, off_ref, acts_ref, k_ref, sems, slot_sems):
    slots, frames, wide = acts_ref.shape
    blocks, _, rows, _ = gp_ref.shape
    taps = k_ref.shape[0]
    lead = taps // 2
    small = [
        pltpu.make_async_copy(source, target, sems.at[i])
        for i, (source, target) in enumerate(
            (
                (len_hbm, len_ref),
                (off_hbm, off_ref),
                (k_hbm, k_ref),
                (g_hbm, gb_ref.at[0]),
                (b_hbm, gb_ref.at[1]),
            )
        )
    ]

    def fetch(slot):
        return pltpu.make_async_copy(acts_hbm.at[slot], acts_ref.at[slot], slot_sems.at[slot])

    small[0].start()
    small[1].start()
    fetch(0).start()
    small[2].start()
    for slot in range(1, slots):
        fetch(slot).start()
    for copy in small[3:]:
        copy.start()
    acc_ref[...] = jnp.zeros_like(acc_ref)
    position = lax.broadcasted_iota(jnp.int32, (frames, LANES), 0)
    reach = lax.broadcasted_iota(jnp.int32, (taps, frames), 1)
    reach = reach - lax.broadcasted_iota(jnp.int32, (taps, frames), 0) + (lead - 1)
    for copy in small[:3]:
        copy.wait()

    def one(slot, carry):
        low = off_ref[slot]
        high = low + len_ref[slot]
        valid = ((position >= low) & (position < high)).astype(F32)
        ok_ref[slot] = valid
        in_ref[slot] = (
            (reach >= low) & (reach < high) & (reach >= 0) & (reach < frames)
        ).astype(F32)
        fetch(slot).wait()
        for block in range(blocks):
            cols = slice(block * LANES, (block + 1) * LANES)
            gate = slice(wide // 2 + block * LANES, wide // 2 + (block + 1) * LANES)
            left, right = acts_ref[slot, :, cols].astype(F32), acts_ref[slot, :, gate].astype(F32)
            gp_ref[block, slot, 0:lead, :] = jnp.zeros((lead, LANES), F32)
            gp_ref[block, slot, lead : lead + frames, :] = left * jax.nn.sigmoid(right) * valid
            tail = jnp.zeros((rows - lead - frames, LANES), F32)
            gp_ref[block, slot, lead + frames : rows, :] = tail
        for block in range(blocks):
            cols = slice(block * LANES, (block + 1) * LANES)
            total = gp_ref[block, slot, 1 : 1 + frames, :] * k_ref[0:1, cols]
            for tap in range(1, taps):
                lag = gp_ref[block, slot, 1 + tap : 1 + tap + frames, :]
                total = total + lag * k_ref[tap : tap + 1, cols]
            cv_ref[block, slot] = total
            masked = total * valid
            acc_ref[0, block] += fold(masked)
            acc_ref[1, block] += fold(masked * total)
        return carry

    lax.fori_loop(0, slots, one, 0)
    for copy in small[3:]:
        copy.wait()
    for block in range(blocks):
        cols = slice(block * LANES, (block + 1) * LANES)
        st_ref[0:1, cols] = row_sum(acc_ref[0, block])
        st_ref[1:2, cols] = row_sum(acc_ref[1, block])
    count = len_ref[0]
    for other in range(1, slots):
        count = count + len_ref[other]
    st_ref[:, blocks * LANES :] = jnp.full((2, LANES), count.astype(F32), F32)


def lag_sums(gp_ref, block, weights, taps, group, put):
    frames = weights(0).shape[0]
    slots = gp_ref.shape[1]
    for low in range(0, taps, group):
        sums = [None] * group
        for slot in range(slots):
            weight = weights(slot)
            for j in range(group):
                at = 1 + low + j
                term = fold(weight * gp_ref[block, slot, at : at + frames, :])
                sums[j] = term if sums[j] is None else sums[j] + term
        for j in range(group):
            put(low + j, row_sum(sums[j]))


def aux_body(start, ok_ref, in_ref, gp_ref, cv_ref, out_ref, wt_ref):
    _, slots, frames, _ = cv_ref.shape
    many, _, taps, _ = out_ref.shape
    lead = taps // 2

    def one(i, carry):
        block = start + i
        for slot in range(slots):
            wt_ref[slot] = cv_ref[block, slot] * ok_ref[slot]

        def put(k, row):
            out_ref[i, 0, k : k + 1, :] = row

        lag_sums(gp_ref, block, lambda slot: wt_ref[slot], taps, 16, put)
        total = jnp.zeros((taps, LANES), F32)
        for slot in range(slots):
            inside = in_ref[slot].astype(BF16)
            rest = gp_ref[block, slot, lead : lead + frames, :]
            for _ in range(3):
                part = rest.astype(BF16)
                rest = rest - part.astype(F32)
                total = total + jnp.dot(inside, part, preferred_element_type=F32)
        out_ref[i, 1] = total
        return carry

    lax.fori_loop(0, many, one, 0)


def back_body(cotan_ref, w_ref, out_ref):
    for block in range(out_ref.shape[0]):
        rows = w_ref[block * LANES : (block + 1) * LANES, :]
        out_ref[block] = lax.dot_general(
            cotan_ref[...], rows, (((1,), (1,)), ((), ())), preferred_element_type=F32
        )


def scale_of(st_ref, block):
    width = st_ref.shape[1] - LANES
    cols = pl.ds(pl.multiple_of(block * LANES, LANES), LANES)
    count = st_ref[0:1, width:]
    mean = st_ref[0:1, cols] / count
    inv = lax.rsqrt(st_ref[1:2, cols] / count - mean * mean + 1e-05)
    return count, mean, inv


def hidden_body(st_ref, gb_ref, ok_ref, cv_ref, hid_ref):
    blocks, slots, frames, _ = cv_ref.shape

    def one(block, carry):
        _, mean, inv = scale_of(st_ref, block)
        gain, shift = gb_ref[0, pl.ds(block, 1), :], gb_ref[1, pl.ds(block, 1), :]
        for slot in range(slots):
            valid = ok_ref[slot]
            shifted = gain * ((cv_ref[block, slot] - mean) * inv) + shift
            hidden = shifted * jax.nn.sigmoid(shifted) * valid
            hid_ref[block, slot * frames : (slot + 1) * frames, :] = hidden.astype(BF16)
        return carry

    lax.fori_loop(0, blocks, one, 0)


def slope_body(st_ref, gb_ref, ok_ref, gp_ref, cv_ref, bk_ref, *refs):
    aux_refs, (give_ref, keep_ref, sl_ref) = refs[:-3], refs[-3:]
    blocks, slots, frames, _ = cv_ref.shape
    taps = aux_refs[0].shape[2]
    last = 3 * taps
    bit = lax.axis_index("dp") & 1

    def one(i, aux_ref, odd, q_ref):
        block = 2 * i + odd
        _, mean, inv = scale_of(st_ref, block)
        gain, shift = gb_ref[0, pl.ds(block, 1), :], gb_ref[1, pl.ds(block, 1), :]
        first = second = jnp.zeros((8, LANES), F32)
        for slot in range(slots):
            normed = (cv_ref[block, slot] - mean) * inv
            shifted = gain * normed + shift
            sig = jax.nn.sigmoid(shifted)
            back = bk_ref[block, slot * frames : (slot + 1) * frames, :]
            slope = back * sig * (1.0 + shifted * (1.0 - sig)) * ok_ref[slot]
            sl_ref[slot] = slope
            first, second = first + fold(slope), second + fold(slope * normed)

        def put(k, row):
            q_ref[i, k : k + 1, :] = row

        lag_sums(gp_ref, block, lambda slot: sl_ref[slot], taps, 16, put)
        q_ref[i, taps : 2 * taps, :] = aux_ref[odd, 1]
        q_ref[i, 2 * taps : last, :] = inv * (aux_ref[odd, 0] - mean * aux_ref[odd, 1])
        keep_ref[0, pl.ds(last + block, 1), :] = row_sum(first)
        keep_ref[0, pl.ds(last + blocks + block, 1), :] = row_sum(second)

    for i, aux_ref in enumerate(aux_refs):
        one(i, aux_ref, 1 - bit, give_ref)
        one(i, aux_ref, bit, keep_ref)
    for i in range(len(aux_refs)):
        give_ref[i, last:, :] = keep_ref[0, last:, :]
        if i:
            keep_ref[i, last:, :] = keep_ref[0, last:, :]


def halve_body(level, own_ref, recv_ref, give_ref, keep_ref):
    bit = (lax.axis_index("dp") >> level) & 1
    for i in range(give_ref.shape[0]):
        for odd, ref in ((1 - bit, give_ref), (bit, keep_ref)):
            ref[i] = own_ref[2 * i + odd] + recv_ref[2 * i + odd]


def out_body(hid_ref, w_ref, out_ref):
    blocks = hid_ref.shape[0]
    slots, frames, _ = out_ref.shape
    total = None
    for block in range(blocks):
        term = jnp.dot(
            hid_ref[block],
            w_ref[block * LANES : (block + 1) * LANES, :],
            preferred_element_type=F32,
        )
        total = term if total is None else total + term
    for slot in range(slots):
        out_ref[slot] = total[slot * frames : (slot + 1) * frames, :].astype(BF16)


def stage_body(*refs):
    pieces, out_ref, sems = refs[:-2], refs[-2], refs[-1]
    copies = [
        pltpu.make_async_copy(piece, out_ref.at[i], sems.at[i]) for i, piece in enumerate(pieces)
    ]
    for copy in copies:
        copy.start()
    for copy in copies:
        copy.wait()


def rows_body(masks, recv_hbm, staged_ref, *refs):
    pieces, (give_ref, keep_ref, recv_ref, held, sems) = refs[:-5], refs[-5:]
    me, half = lax.axis_index("dp"), lax.axis_index("grp") & 1
    copies = [
        pltpu.make_async_copy(piece, held.at[i], sems.at[i]) for i, piece in enumerate(pieces)
    ]
    fetch = pltpu.make_async_copy(recv_hbm, recv_ref, sems.at[len(pieces)])
    fetch.start()
    for copy in copies:
        copy.start()
    fetch.wait()
    early = staged_ref.shape[0]
    many = give_ref.shape[0]
    width = many * LANES
    give = pl.ds(pl.multiple_of((1 - half) * width, width), width)
    keep = pl.ds(pl.multiple_of(half * width, width), width)
    totals = [None, None]
    for i, mask in enumerate(masks):
        left = recv_ref[jnp.bitwise_xor(me, mask)]
        if i >= early:
            copies[i - early].wait()
        for j, cols in enumerate((give, keep)):
            right = staged_ref[i, :, cols] if i < early else held[i - early, :, cols]
            term = lax.dot_general(
                left, right, (((0,), (0,)), ((), ())), preferred_element_type=F32
            )
            totals[j] = term if totals[j] is None else totals[j] + term
    for total, ref in zip(totals, (give_ref, keep_ref)):
        for block in range(many):
            ref[block] = total[:, block * LANES : (block + 1) * LANES].astype(BF16)


def plus_body(own_ref, recv_ref, out_ref):
    out_ref[...] = own_ref[...] + recv_ref[...]


def add_body(own_ref, recv_ref, out_ref):
    out_ref[...] = (own_ref[...].astype(F32) + recv_ref[...].astype(F32)).astype(BF16)


def scale_body(st_ref, gb_ref, out_ref):
    me = lax.axis_index("dp")
    count, _, inv = scale_of(st_ref, me)
    out_ref[0:1, :] = gb_ref[0, pl.ds(me, 1), :] * inv
    out_ref[1:2, :] = count


def last_body(taps, own_ref, recv_ref, lags_ref, more_ref, sc_ref, rows_ref, gk_ref, gg_ref, gb_ref):
    me, half = lax.axis_index("dp"), lax.axis_index("grp") & 1
    many = own_ref.shape[0]
    for which, ref in ((half, own_ref), (1 - half, recv_ref)):
        for block in range(many):
            cols = pl.ds(pl.multiple_of((which * many + block) * LANES, LANES), LANES)
            rows_ref[:, cols] = ref[block].astype(F32)
    value = lags_ref[0] + more_ref[0]
    blocks = gb_ref.shape[0]
    gb_ref[...] = value[3 * taps : 3 * taps + blocks]
    gg_ref[...] = value[3 * taps + blocks : 3 * taps + 2 * blocks]
    count = sc_ref[1:2, :]
    mine = pl.ds(me, 1)
    gk_ref[...] = sc_ref[0:1, :] * (
        value[0:taps]
        - (gb_ref[mine, :] / count) * value[taps : 2 * taps]
        - (gg_ref[mine, :] / count) * value[2 * taps : 3 * taps]
    )


SMEM = pl.BlockSpec(memory_space=pltpu.SMEM)
VMEM = pl.BlockSpec(memory_space=pltpu.VMEM)
HBM = pl.BlockSpec(memory_space=pltpu.HBM)
ANY = pl.BlockSpec(memory_space=pl.ANY)


def in_hbm(value):
    return pltpu.with_memory_space_constraint(value, pltpu.HBM)


def call(body, shapes, scalars, args, flops=0, scratch=(), mib=8, **more):
    many = isinstance(shapes, list)
    moved = sum(a.size * a.dtype.itemsize for a in args)
    return pl.pallas_call(
        body,
        in_specs=more.pop("in_specs", None) or [SMEM] * len(scalars) + [VMEM] * len(args),
        out_specs=[VMEM] * len(shapes) if many else VMEM,
        out_shape=shapes,
        scratch_shapes=scratch,
        compiler_params=pltpu.CompilerParams(vmem_limit_bytes=mib << 20),
        cost_estimate=pl.CostEstimate(flops=flops, bytes_accessed=moved, transcendentals=0),
        **more,
    )(*scalars, *args)


def local_fast(n_dp, n_grp, acts, cotan, lengths, offsets, kernel, gamma, beta, w_out):
    slots, frames, wide = acts.shape
    width = wide // 2
    taps = kernel.shape[0]
    blocks = width // LANES
    tokens = slots * frames
    n_q = 3 * taps + 2 * blocks
    padded = 2 * (taps // 2) + frames
    shape = jax.ShapeDtypeStruct

    def swap(value, dp_mask, grp_mask):
        pairs = [
            (d * n_grp + g, (d ^ dp_mask) * n_grp + (g ^ grp_mask))
            for d in range(n_dp)
            for g in range(n_grp)
        ]
        return lax.ppermute(value, ("dp", "grp"), pairs)

    def plus(own, other):
        return call(plus_body, shape(own.shape, own.dtype), (), (own, other))

    dp_bits = [1 << i for i in range(n_dp.bit_length() - 1)]
    grp_bits = [1 << i for i in range(n_grp.bit_length() - 1)]
    gamma2, beta2 = gamma.reshape(blocks, LANES), beta.reshape(blocks, LANES)

    flat_cotan = cotan.reshape(tokens, width)
    pieces = [(0, flat_cotan)]
    for bit in dp_bits[:0:-1] + dp_bits[:1]:
        pieces += [(m | bit, swap(v, bit, 0)) for m, v in pieces]
    late_bits = dp_bits[-1] | dp_bits[-2]
    pieces.sort(key=lambda piece: piece[0] & late_bits == late_bits)
    masks, values = tuple(m for m, _ in pieces), [v for _, v in pieces]
    early = n_dp - 1

    gated, conv_out, stats, valid, inside, gains = call(
        conv_body,
        [
            shape((blocks, slots, padded, LANES), F32),
            shape((blocks, slots, frames, LANES), F32),
            shape((2, width + LANES), F32),
            shape((slots, frames, LANES), F32),
            shape((slots, taps, frames), F32),
            shape((2, blocks, LANES), F32),
        ],
        (),
        [in_hbm(v) for v in (lengths, offsets, acts, kernel, gamma2, beta2)],
        flops=4 * taps * tokens * width,
        scratch=[
            pltpu.VMEM((2, blocks, 8, LANES), F32),
            pltpu.SMEM((slots,), jnp.int32),
            pltpu.SMEM((slots,), jnp.int32),
            pltpu.VMEM(acts.shape, BF16),
            pltpu.VMEM(kernel.shape, F32),
            pltpu.SemaphoreType.DMA((5,)),
            pltpu.SemaphoreType.DMA((slots,)),
        ],
        in_specs=[HBM] * 6,
    )

    hops = [(m | 1, 0) for m in dp_bits[1:2]] + [(1, m) for m in grp_bits]
    hops += [(1, 0)] + [(m | 1, 0) for m in dp_bits[2:]]
    for dp_mask, grp_mask in hops:
        stats = plus(stats, swap(stats, dp_mask, grp_mask))

    back = call(
        back_body,
        shape((blocks, tokens, LANES), F32),
        (),
        (flat_cotan, w_out),
        flops=2 * tokens * width * width,
    )
    parts = blocks // 2
    each = 2
    aux = [
        call(
            functools.partial(aux_body, i * each),
            shape((each, 2, taps, LANES), F32),
            (),
            (valid, inside, gated, conv_out),
            flops=4 * taps * tokens * each * LANES,
            scratch=[pltpu.VMEM((slots, frames, LANES), F32)],
        )
        for i in range(parts)
    ]

    hidden = call(
        hidden_body, shape((blocks, tokens, LANES), BF16), (), (stats, gains, valid, conv_out)
    )
    received = lax.all_to_all(hidden, "dp", 0, 0, tiled=True)
    give, lags = call(
        slope_body,
        [shape((parts, n_q, LANES), F32)] * 2,
        (),
        (stats, gains, valid, gated, conv_out, back, *aux),
        flops=4 * taps * tokens * width,
        scratch=[pltpu.VMEM((slots, frames, LANES), F32)],
    )
    for level in range(1, len(dp_bits)):
        came = swap(give, dp_bits[level - 1], 0)
        give, lags = call(
            functools.partial(halve_body, level),
            [shape((parts >> level, n_q, LANES), F32)] * 2,
            (),
            (lags, came),
        )
    lags = plus(lags, swap(give, dp_bits[-1], 0))
    scale = call(scale_body, shape((2, LANES), F32), (), (stats, gains))
    outputs = call(out_body, shape(cotan.shape, BF16), (), (hidden, w_out))

    half_shape = shape((blocks // 2, LANES, LANES), BF16)
    staged = call(
        stage_body,
        shape((early, tokens, width), BF16),
        (),
        values[:early],
        scratch=[pltpu.SemaphoreType.DMA((early,))],
        in_specs=[ANY] * early,
    )
    given, kept = call(
        functools.partial(rows_body, masks),
        [half_shape] * 2,
        (),
        (received, staged, *values[early:]),
        flops=2 * n_dp * tokens * LANES * width,
        scratch=[
            pltpu.VMEM(received.shape, BF16),
            pltpu.VMEM((n_dp - early, tokens, width), BF16),
            pltpu.SemaphoreType.DMA((n_dp - early + 1,)),
        ],
        in_specs=[ANY, VMEM] + [ANY] * (n_dp - early),
    )
    taken = swap(given, 0, 1)
    both = call(add_body, half_shape, (), (kept, taken))
    for mask in grp_bits[1:]:
        other = swap(both, 0, mask)
        both = call(add_body, half_shape, (), (both, other))
    rest = swap(both, 0, 1)

    for mask in grp_bits[:-1]:
        lags = plus(lags, swap(lags, 0, mask))
    more = swap(lags, 0, grp_bits[-1])
    weight_rows, grad_kernel, gamma_sum, beta_sum = call(
        functools.partial(last_body, taps),
        [
            shape((LANES, width), F32),
            shape((taps, LANES), F32),
            shape((blocks, LANES), F32),
            shape((blocks, LANES), F32),
        ],
        (),
        (both, rest, lags, more, scale),
    )
    return (outputs, weight_rows, grad_kernel, gamma_sum.reshape(width), beta_sum.reshape(width))


def solution(mesh):
    n_dp, n_grp = mesh.shape["dp"], mesh.shape["grp"]

    def fits(width, taps, frames):
        return (
            n_dp & (n_dp - 1) == 0
            and n_grp & (n_grp - 1) == 0
            and n_dp >= 4
            and n_grp >= 4
            and width == n_dp * LANES
            and taps % 16 == 0
            and frames % 16 == 0
            and n_dp % 8 == 0
        )

    def local(acts, cotan, lengths, offsets, kernel, gamma, beta, w_out):
        args = (acts, cotan, lengths, offsets, kernel, gamma, beta, w_out)
        if not fits(w_out.shape[0], kernel.shape[0], acts.shape[1]):
            return local_general(*args)
        return local_fast(n_dp, n_grp, *args)

    placed = (
        P(("dp", "grp"), None, None),
        P(("dp", "grp"), None, None),
        P(("dp", "grp")),
        P(("dp", "grp")),
        P(),
        P(),
        P(),
        P(),
    )
    return jax.shard_map(
        local,
        mesh=mesh,
        in_specs=placed,
        out_specs=(P(("dp", "grp"), None, None), P("dp", None), P(None, "dp"), P(), P()),
        check_vma=False,
    )
```
